256 devices in a mesh: comp: 64 (over x, y_lo, z), gy: 2 (over y_hi), gx: 2 (over core).
Axes of the slice: x: 4, y: 4 (y_hi: 2, y_lo: 2; y = y_hi * 2 + y_lo), z: 8, core: 2. Of those that a mesh axis runs over, the one named last changes fastest.
Arguments:
- flow_fields: float32 [4, 6, 2048, 384], P(None, None, ('comp', 'gy', 'gx')), may hold values from -6 to 6
- chlorophyll_lag: float32 [6, 2048, 384], P(None, ('comp', 'gy', 'gx')), may hold values from 0.1 to 3
- tracers: float32 [16, 6, 2048, 128], P(None, None, ('comp', 'gy', 'gx')), may hold values from -6 to 6
- forcing: float32 [4, 6, 2048, 128], P(None, None, ('comp', 'gy', 'gx')), may hold values from -6 to 6
- ocean_mask: int32 [512, 384], replicated, may hold values 0 or 1
- bottom: int32 [512, 384], replicated, may hold values from 1 to 6
- reaction: float32 [16, 16], replicated, may hold values from -1.5 to 0.1
Outputs:
- flow_out: float32 [4, 6, 2048, 384], P(None, None, ('comp', 'gy', 'gx'))
- light_out: float32 [6, 2048, 384], P(None, ('comp', 'gy', 'gx'))
- tracers_out: float32 [16, 6, 2048, 128], P(None, None, ('comp', 'gy', 'gx'))
- forcing_out: float32 [4, 6, 2048, 128], P(None, None, ('comp', 'gy', 'gx'))
The draws below stay inside these ranges and needn't reach their ends.
All inputs are finite; a program needn't handle non-finite values.
Results may differ from the reference program's by a relative error of at most 0.0002.
Values sent between devices are 32-bit elements; how exact they have to be, the bound alone decides.
No kernel may reach another device: no remote copies, remote signals or barrier semaphores. Data moves between devices by JAX's collectives and lax.ppermute only.
A program may use at most 64 MiB of HBM per device.

```python
import math
import jax
import jax.numpy as jnp
from jax import lax

DX = 8
YT = 128
Z = 6
NT = 16
SUB = 4
COUPLE = 2
NX = 512
NY = 384
ROWS = 2048


def draw_reaction(key, part):
    first_key, second_key = jax.random.split(jax.random.fold_in(key, 7))
    spread = jnp.clip(0.05 * jax.random.normal(first_key, (NT, NT), jnp.float32), -0.1, 0.1)
    diagonal = -jax.random.uniform(second_key, (NT,), jnp.float32, 0.5, 1.5)
    eye_mask = jnp.eye(NT, dtype=jnp.float32)
    return spread * (1.0 - eye_mask) + eye_mask * diagonal[None, :]


def draw_flow_fields(key, part):
    sign_key, speed_key, scalar_key = jax.random.split(jax.random.fold_in(key, 11), 3)
    grid_shape = (2, Z, ROWS, NY)
    flow_signs = jnp.where(jax.random.uniform(sign_key, grid_shape, jnp.float32) < 0.5, -1.0, 1.0)
    flow_speed = jnp.clip(4.6 + 0.7 * jax.random.normal(speed_key, grid_shape, jnp.float32), 3.0, 6.0)
    scalars = jnp.clip(jax.random.normal(scalar_key, grid_shape, jnp.float32), -6.0, 6.0)
    return jnp.concatenate([flow_signs * flow_speed, scalars], axis=0).astype(jnp.float32)


def touch_ends(array, rng, smallest, top_value):
    spot = [jax.random.randint(jax.random.fold_in(rng, axis), (), 0, length) for axis, length in enumerate(array.shape)]
    widest = array.shape.index(max(array.shape))
    beside = spot[:widest] + [(spot[widest] + 1) % array.shape[widest]] + spot[widest + 1:]
    return array.at[tuple(spot)].set(smallest).at[tuple(beside)].set(top_value)


def block_levels(own_key, shape, cuts, least, largest):
    def one(dim, blocks):
        heights = jax.random.uniform(jax.random.fold_in(jax.random.fold_in(own_key, 6), dim), (blocks,), jnp.float32, least / len(cuts), largest / len(cuts))
        return jnp.repeat(jnp.exp(heights), shape[dim] // blocks).reshape((-1,) + (1,) * (len(shape) - dim - 1))

    level = one(*cuts[0])
    for cut in cuts[1:]:
        level = level * one(*cut)
    return level


def scatter_about(own_key, dims, scale, bound, pieces=(), kind=jnp.bfloat16):
    factor_of = block_levels(own_key, dims, pieces, -0.22, 0.18) if pieces else 1.0
    array = jax.random.normal(own_key, dims, jnp.float32) * scale * factor_of
    return jnp.minimum(jnp.maximum(array, -bound), bound).astype(kind)


def setup_inputs(seed: int = 0) -> dict:
    seeds = jax.random.split(jax.random.key(seed), 8)
    flow_fields = draw_flow_fields(jax.random.fold_in(seeds[7], 71), 0)
    chlorophyll_lag = jnp.clip(jnp.exp(math.log(3.0) - 3.4011974 * jax.random.uniform(seeds[1], (Z, ROWS, NY), jnp.float32) ** block_levels(seeds[1], (Z, ROWS, NY), ((1, 256),), -0.2, 0.2)), 0.1, 3.0)
    tracers = scatter_about(seeds[2], (NT, Z, ROWS, YT), 1.0, 6.0, ((2, 256),), jnp.float32)
    forcing = scatter_about(seeds[3], (4, Z, ROWS, YT), 1.0, 6.0, ((2, 256),), jnp.float32)
    ocean_mask = touch_ends((jax.random.randint(seeds[4], (NX, NY), 0, 5) < 4).astype(jnp.int32), jax.random.fold_in(seeds[4], 1), 0, 1)
    bottom = touch_ends(jax.random.randint(seeds[5], (NX, NY), 1, Z + 1), jax.random.fold_in(seeds[5], 1), 1, Z).astype(jnp.int32)
    reaction = draw_reaction(jax.random.fold_in(seeds[7], 71), 0)
    return dict(flow_fields=flow_fields, chlorophyll_lag=chlorophyll_lag, tracers=tracers, forcing=forcing, ocean_mask=ocean_mask, bottom=bottom, reaction=reaction)


step_time = 0.1
coriolis = 1.0
viscosity = 0.5
friction = 0.1
diffusion = 0.5
expansion = 0.2
contraction = 0.2
water_attenuation = 0.05
pigment_attenuation = 0.3
heating_rate = 5.0
tracer_time = 0.1
tracer_diffusion = 0.5
warm_rate = 0.1
salt_rate = 0.05


def interior(values):
    return values[..., 1:-1, 1:-1]


def laplace(values):
    return (values[..., 2:, 1:-1] + values[..., :-2, 1:-1] + values[..., 1:-1, 2:] + values[..., 1:-1, :-2]
            - 4.0 * interior(values))


def derive_rows(values):
    return 0.5 * (values[..., 2:, 1:-1] - values[..., :-2, 1:-1])


def derive_cols(values):
    return 0.5 * (values[..., 1:-1, 2:] - values[..., 1:-1, :-2])


def pad_plane(values):
    return jnp.pad(values, [(0, 0)] * (values.ndim - 2) + [(1, 1), (1, 1)])


def absorb(pigment):
    optical = jnp.cumsum(water_attenuation + pigment_attenuation * pigment, axis=0)
    lower_light = jnp.exp(-optical)
    upper_light = jnp.concatenate([jnp.ones_like(lower_light[:1]), lower_light[:-1]], axis=0)
    return heating_rate * (upper_light - lower_light)


def dynamics_update(padded, heating, wet_cells):
    flow_x, flow_y, warmth, saltness = padded[0], padded[1], padded[2], padded[3]
    pressure = jnp.cumsum(expansion * saltness - contraction * warmth, axis=0)
    centre_x = interior(flow_x)
    centre_y = interior(flow_y)
    centre_warm = interior(warmth)
    centre_salt = interior(saltness)
    new_x = wet_cells * (centre_x + step_time * (coriolis * centre_y - derive_rows(pressure)
                                                 + viscosity * laplace(flow_x) - friction * centre_x))
    new_y = wet_cells * (centre_y + step_time * (-coriolis * centre_x - derive_cols(pressure)
                                                 + viscosity * laplace(flow_y) - friction * centre_y))
    new_warm = wet_cells * (centre_warm + step_time * (-(derive_rows(flow_x * warmth) + derive_cols(flow_y * warmth))
                                                       + diffusion * laplace(warmth) + heating))
    new_salt = wet_cells * (centre_salt + step_time * (-(derive_rows(flow_x * saltness) + derive_cols(flow_y * saltness))
                                                       + diffusion * laplace(saltness)))
    return jnp.stack([new_x, new_y, new_warm, new_salt], axis=0)


def tracer_update(padded, warmth, saltness, wet_cells, reaction):
    planes = padded.shape[0] - 2
    tracer_pad = padded[:planes]
    flow_x = padded[planes]
    flow_y = padded[planes + 1]
    advect = derive_rows(flow_x[None] * tracer_pad) + derive_cols(flow_y[None] * tracer_pad)
    centre = interior(tracer_pad)
    growth = jnp.exp(warm_rate * warmth - salt_rate * saltness)
    reacted = jnp.einsum("ab,bzxy->azxy", reaction, centre, precision=lax.Precision.HIGHEST) * growth[None]
    return wet_cells[None] * (centre + tracer_time * (tracer_diffusion * laplace(tracer_pad) - advect + reacted))


def pigment_of(tracer_state):
    return 0.25 * (tracer_state[0] * tracer_state[0] + tracer_state[1] * tracer_state[1])


def tracer_view(values):
    planes = values.shape[0]
    live_rows = jnp.roll(values, DX, axis=2)[:, :, :3 * NX]
    return live_rows.reshape(planes, Z, 3, NX, YT).transpose(0, 1, 3, 2, 4).reshape(planes, Z, NX, NY)


def tracer_store(values):
    planes = values.shape[0]
    arranged = values.reshape(planes, Z, NX, 3, YT).transpose(0, 1, 3, 2, 4).reshape(planes, Z, 3 * NX, YT)
    whole = jnp.concatenate([arranged, jnp.zeros((planes, Z, NX, YT), jnp.float32)], axis=2)
    return jnp.roll(whole, -DX, axis=2)


def reference(flow_fields, chlorophyll_lag, tracers, forcing, ocean_mask, bottom, reaction):
    level_index = jnp.arange(Z, dtype=jnp.int32)[:, None, None]
    wet_cells = jnp.where((ocean_mask[None] == 1) & (level_index < bottom[None]), 1.0, 0.0).astype(jnp.float32)
    flow_state = jnp.roll(flow_fields, DX, axis=2)[:, :, 3 * NX:]
    pigment = jnp.roll(chlorophyll_lag, DX, axis=1)[:, 3 * NX:]
    tracer_state = tracer_view(tracers)
    driving = tracer_view(forcing)
    for coupling in range(COUPLE):
        heating = absorb(pigment)
        total_x = jnp.zeros_like(flow_state[0])
        total_y = jnp.zeros_like(flow_state[0])
        for substep in range(SUB):
            flow_state = dynamics_update(pad_plane(flow_state), heating, wet_cells)
            total_x = total_x + flow_state[0]
            total_y = total_y + flow_state[1]
        new_driving = jnp.stack([total_x / SUB, total_y / SUB, flow_state[2], flow_state[3]], axis=0)
        stacked = pad_plane(jnp.concatenate([tracer_state, driving[:2]], axis=0))
        tracer_state = tracer_update(stacked, driving[2], driving[3], wet_cells, reaction)
        pigment = pigment_of(tracer_state)
        driving = new_driving
    flow_out = jnp.roll(jnp.concatenate([jnp.zeros((4, Z, 3 * NX, NY), jnp.float32), flow_state], axis=2), -DX, axis=2)
    light_out = jnp.roll(jnp.concatenate([jnp.zeros((Z, 3 * NX, NY), jnp.float32), pigment], axis=1), -DX, axis=1)
    return flow_out, light_out, tracer_store(tracer_state), tracer_store(driving)
```

```python
import jax
import jax.numpy as jnp
from jax import lax
from jax.experimental import pallas as pl
from jax.experimental.pallas import tpu as pltpu
from jax.sharding import PartitionSpec as P

AXES = ("comp", "gy", "gx")
SECTIONS = 4
DT = 0.1
F32 = jnp.float32
VMEM_LIMIT = 48 * 1024 * 1024


def place():
    gy = lax.axis_size("gy")
    gx = lax.axis_size("gx")
    total = lax.axis_size("comp") * gy * gx
    group = total // SECTIONS
    position = (lax.axis_index("comp") * gy + lax.axis_index("gy")) * gx + lax.axis_index("gx")
    moved = lax.rem(position + 1, total)
    return moved // group, lax.rem(moved, group), group


def lanes(rows):
    return lax.broadcasted_iota(jnp.int32, (rows, 128), 1)


def roll_lanes(x, by):
    by = by % 128
    return x if by == 0 else pltpu.roll(x, by, 1)


def swap(x):
    return pltpu.roll(x, 4, 0)


def upper_half():
    return lax.broadcasted_iota(jnp.int32, (8, 128), 0) < 4


def spread(flag):
    return jnp.where(flag, 1.0, 0.0).astype(F32)


def mask_kernel(ocean, bottom, out, ocean_rows, bottom_rows, sems):
    _, strip, group = place()
    starts = [jnp.maximum(strip - 1, 0), strip, jnp.minimum(strip + 1, group - 1)]
    copies = []
    for i, start in enumerate(starts):
        rows = pl.ds(pl.multiple_of(start * 8, 8), 8)
        copies.append(pltpu.make_async_copy(ocean.at[rows], ocean_rows.at[i], sems.at[i]))
        copies.append(pltpu.make_async_copy(bottom.at[rows], bottom_rows.at[i], sems.at[3 + i]))
    for copy in copies:
        copy.start()
    for copy in copies:
        copy.wait()
    inside = [(strip > 0).astype(jnp.int32), 1, (strip < group - 1).astype(jnp.int32)]
    for i in range(3):
        out[8 * i : 8 * i + 8] = jnp.where(ocean_rows[i] == 1, bottom_rows[i], 0) * inside[i]


def edge_tile(planes):
    lane = lanes(planes[0].shape[0])
    edges = jnp.zeros_like(planes[0])
    for a, x in enumerate(planes):
        edges = jnp.where(lane == a, roll_lanes(x, a + 1), edges)
        edges = jnp.where(lane == 64 + a, roll_lanes(x, 64 + a), edges)
    return edges


def edges_kernel(tracers, forcing, out):
    nt = tracers.shape[0]

    def level(l, carry):
        out[l] = edge_tile([tracers[a, l] for a in range(nt)] + [forcing[1, l]])
        return carry

    lax.fori_loop(0, tracers.shape[1], level, 0)


def open_edges(section, from_left, from_right, rows):
    lane = lanes(rows)
    return jnp.where(
        lane < 64, from_left * spread(section > 0), from_right * spread(section < 2)
    )


def rows_kernel(flow, pigment, tracers, forcing, from_left, from_right, to_next, to_prev, edges):
    section, _, _ = place()
    levels = pigment.shape[0]
    nt = tracers.shape[0]

    @pl.when(section == 3)
    def _():
        def level(l, carry):
            for f in range(5):
                for j in range(3):
                    cols = slice(128 * j, 128 * j + 128)
                    tile = flow[f, l, :, cols] if f < 4 else pigment[l, :, cols]
                    to_next[3 * f + j, l] = tile
                    to_prev[3 * f + j, l] = tile
            return carry

        lax.fori_loop(0, levels, level, 0)
        edges[...] = jnp.zeros_like(edges)

    @pl.when(section != 3)
    def _():
        half = upper_half()
        for l in range(levels):
            edges[l] = open_edges(section, from_left[l], from_right[l], 8)

        def put(plane, pair, even, odd):
            row, col = plane // 2, 3 * (plane % 2)
            to_next[row, col + pair] = jnp.where(half, swap(even), odd)
            to_prev[row, col + pair] = jnp.where(half, even, swap(odd))

        for pair in range(3):
            even, odd = 2 * pair, 2 * pair + 1
            for a in range(nt):
                put(a, pair, tracers[a, even], tracers[a, odd])
            put(nt, pair, forcing[0, even], forcing[0, odd])
            put(nt + 1, pair, forcing[1, even], forcing[1, odd])
            growth = [jnp.exp(0.1 * forcing[2, l] - 0.05 * forcing[3, l]) for l in (even, odd)]
            put(nt + 2, pair, growth[0], growth[1])
            put(nt + 3, pair, edges[even], edges[odd])
        for row in range(10, 15):
            for l in range(levels):
                to_next[row, l] = jnp.zeros((8, 128), F32)
                to_prev[row, l] = jnp.zeros((8, 128), F32)


def shifted(tiles):
    lane = lanes(tiles[0].shape[0])
    left = [roll_lanes(x, 127) for x in tiles]
    right = [roll_lanes(x, 1) for x in tiles]
    count = len(tiles)
    east = [
        jnp.where(lane == 127, left[j + 1] if j + 1 < count else 0.0, left[j]) for j in range(count)
    ]
    west = [jnp.where(lane == 0, right[j - 1] if j > 0 else 0.0, right[j]) for j in range(count)]
    return east, west


def substep(source, target, heat, wet_rows, tiles, read_at, write_at, heat_at, wet_at):
    levels = heat.shape[0]
    thirds = 3
    for tile in range(tiles):
        row = read_at + 8 * tile
        put = write_at + 8 * tile
        floors = [
            wet_rows[wet_at + 8 * tile : wet_at + 8 * tile + 8, 128 * j : 128 * j + 128]
            for j in range(thirds)
        ]

        def level(l, carry, row=row, put=put, tile=tile, floors=floors):
            slope_x, slope_y = carry

            def load(f, by):
                return [
                    source[f, l, row + by : row + by + 8, 128 * j : 128 * j + 128]
                    for j in range(thirds)
                ]

            centre = [load(f, 0) for f in range(4)]
            up = [load(f, -1) for f in range(4)]
            down = [load(f, 1) for f in range(4)]
            sides = [shifted(centre[f]) for f in range(4)]
            new_x, new_y = [], []
            for j in range(thirds):
                u, v, t, s = (centre[f][j] for f in range(4))
                un, vn, tn, sn = (up[f][j] for f in range(4))
                us, vs, ts, ss = (down[f][j] for f in range(4))
                ue, ve, te, se = (sides[f][0][j] for f in range(4))
                uw, vw, tw, sw = (sides[f][1][j] for f in range(4))
                px = slope_x[j] + ((ss - sn) - (ts - tn))
                py = slope_y[j] + ((se - sw) - (te - tw))
                new_x.append(px)
                new_y.append(py)
                is_wet = floors[j] > l
                a = 0.05 - 0.05 * us
                b = 0.05 + 0.05 * un
                c = 0.05 - 0.05 * ve
                d = 0.05 + 0.05 * vw
                cols = slice(128 * j, 128 * j + 128)
                h = heat[l, heat_at + 8 * tile : heat_at + 8 * tile + 8, cols]
                results = (
                    0.79 * u + 0.1 * v - 0.01 * px + 0.05 * ((un + us) + (ue + uw)),
                    0.79 * v - 0.1 * u - 0.01 * py + 0.05 * ((vn + vs) + (ve + vw)),
                    (0.8 * t + h) + ((ts * a + tn * b) + (te * c + tw * d)),
                    0.8 * s + ((ss * a + sn * b) + (se * c + sw * d)),
                )
                for f in range(4):
                    target[f, l, put : put + 8, cols] = jnp.where(is_wet, results[f], 0.0)
            return new_x, new_y

        zero = [jnp.zeros((8, 128), F32) for _ in range(thirds)]
        lax.fori_loop(0, levels, level, (zero, zero))


def fill_heat(load, heat):
    levels, rows = heat.shape[0], heat.shape[1]
    for tile in range(rows // 8):
        for j in range(3):
            optical = jnp.zeros((8, 128), F32)
            light = jnp.ones((8, 128), F32)
            for l in range(levels):
                optical = optical + (0.05 + 0.3 * load(l, tile, j))
                lower = jnp.exp(-optical)
                heat[l, 8 * tile : 8 * tile + 8, 128 * j : 128 * j + 128] = (5.0 * DT) * (
                    light - lower
                )
                light = lower


def extend(own, above, below, half):
    turned = swap(own)
    return jnp.concatenate([jnp.where(half, above, turned), jnp.where(half, turned, below)], axis=0)


def tracer_weights(u_up, u_down, v_east, v_west, growth, is_wet):
    wet = spread(is_wet)
    scale = wet * 0.05
    return (
        scale - scale * u_down,
        scale + scale * u_up,
        scale - scale * v_east,
        scale + scale * v_west,
        wet * 0.8,
        (wet * DT) * growth,
    )


def tracer_level(centre, up, down, edges, weights, reaction):
    nt = len(centre)
    lane = lanes(edges.shape[0])
    a, b, c, d, keep, grow = weights
    results = []
    for i in range(nt):
        east = jnp.where(lane == 127, roll_lanes(edges, 63 - i), roll_lanes(centre[i], 127))
        west = jnp.where(lane == 0, roll_lanes(edges, -i), roll_lanes(centre[i], 1))
        mixed = reaction[i, 0] * centre[0]
        for k in range(1, nt):
            mixed = mixed + reaction[i, k] * centre[k]
        results.append(
            (keep * centre[i] + grow * mixed)
            + ((down[i] * a + up[i] * b) + (east * c + west * d))
        )
    return results


def pigment_of(first, second):
    return 0.25 * (first * first + second * second)


def first_kernel(
    flow, pigment, tracers, forcing, edges, above, below, wet_rows, reaction,
    out_a, out_b, out_c, flow_next, tracers_next, buffers, heat, cells, winds,
):
    section, strip, group = place()
    levels = pigment.shape[0]
    nt = tracers.shape[0]
    low = spread(strip > 0)
    high = spread(strip < group - 1)

    @pl.when(section == 3)
    def _():
        def fill(l, carry):
            for f in range(4):
                for j in range(3):
                    cols = slice(128 * j, 128 * j + 128)
                    buffers[0, f, l, 8:16, cols] = above[3 * f + j, l] * low
                    buffers[0, f, l, 16:24, cols] = flow[f, l, :, cols]
                    buffers[0, f, l, 24:32, cols] = below[3 * f + j, l] * high
            return carry

        lax.fori_loop(0, levels, fill, 0)

        def load(l, tile, j):
            if tile == 1:
                return pigment[l, :, 128 * j : 128 * j + 128]
            return (above if tile == 0 else below)[12 + j, l]

        fill_heat(load, heat)
        for n in range(3):
            substep(buffers.at[n], buffers.at[n + 1], heat, wet_rows, 3, 8, 8, 0, 0)
        substep(buffers.at[3], flow_next, heat, wet_rows, 2, 12, 8, 4, 4)
        lane = lanes(8)
        outs = (out_a, out_b, out_c)
        sub = lax.broadcasted_iota(jnp.int32, (8, 128), 0)

        def mean(f, l, row, cols):
            total = buffers[1, f, l, row : row + 8, cols] + buffers[2, f, l, row : row + 8, cols]
            total = total + buffers[3, f, l, row : row + 8, cols]
            return 0.25 * (total + flow_next[f, l, row - 4 : row + 4, cols])

        edge_v = [jnp.zeros((8, 128), F32) for _ in range(3)]
        rows_above = [jnp.zeros((8, 128), F32) for _ in range(3)]
        rows_below = [jnp.zeros((8, 128), F32) for _ in range(3)]
        for l in range(levels):
            v_mean = []
            for j in range(3):
                cols = slice(128 * j, 128 * j + 128)
                outs[j][l] = mean(0, l, 16, cols)
                v_mean.append(mean(1, l, 16, cols))
                outs[j][6 + l] = v_mean[j]
                warm = flow_next[2, l, 12:20, cols]
                salt = flow_next[3, l, 12:20, cols]
                outs[j][12 + l] = jnp.exp(0.1 * warm - 0.05 * salt)
                first = mean(0, l, 15, cols)
                last = mean(0, l, 17, cols)
                rows_above[j] = jnp.where(sub == l, roll_rows(first, l), rows_above[j])
                rows_below[j] = jnp.where(sub == l, roll_rows(last, l + 1), rows_below[j])
            for j in range(3):
                if j > 0:
                    edge_v[j] = jnp.where(
                        lane == 2 * l, roll_lanes(v_mean[j - 1], 2 * l + 1), edge_v[j]
                    )
                if j < 2:
                    edge_v[j] = jnp.where(
                        lane == 2 * l + 1, roll_lanes(v_mean[j + 1], 2 * l + 1), edge_v[j]
                    )
        for j in range(3):
            outs[j][18] = edge_v[j]
            outs[j][19] = rows_above[j]
            outs[j][20] = rows_below[j]
            for i in range(21, 24):
                outs[j][i] = jnp.zeros((8, 128), F32)

    @pl.when(section != 3)
    def _():
        half = upper_half()

        def halo(message, plane, pair, odd, upward):
            tile = message[plane // 2, 3 * (plane % 2) + pair]
            return swap(tile) if odd != upward else tile

        def build(plane, own, l, masked):
            pair, odd = l // 2, l % 2 == 1
            up = halo(above, plane, pair, odd, False)
            down = halo(below, plane, pair, not odd, False)
            if masked:
                up, down = up * low, down * high
            return extend(own, up, down, half)

        for l in range(levels):
            for a in range(nt):
                cells[a, l, 8:24] = build(a, tracers[a, l], l, True)
            winds[0, l, 8:24] = build(nt, forcing[0, l], l, False)
            winds[1, l, 8:24] = build(nt + 1, forcing[1, l], l, False)
            growth = jnp.exp(0.1 * forcing[2, l] - 0.05 * forcing[3, l])
            winds[2, l, 8:24] = build(nt + 2, growth, l, False)
            winds[3, l, 8:24] = build(nt + 3, edges[l], l, False)
        col = pl.ds(pl.multiple_of(section * 128, 128), 128)
        floor = jnp.concatenate([wet_rows[4:12, col], wet_rows[12:20, col]], axis=0)
        lane = lanes(16)

        def level(l, carry):
            border = winds[3, l, 8:24]
            v = winds[1, l, 8:24]
            v_east = jnp.where(lane == 127, roll_lanes(border, 63 - nt), roll_lanes(v, 127))
            v_west = jnp.where(lane == 0, roll_lanes(border, -nt), roll_lanes(v, 1))
            weights = tracer_weights(
                winds[0, l, 7:23], winds[0, l, 9:25], v_east, v_west, winds[2, l, 8:24], floor > l
            )
            inside = lax.broadcasted_iota(jnp.int32, (16, 128), 0) * (section * 0 + 1)
            results = tracer_level(
                [cells[a, l, 8:24] for a in range(nt)],
                [cells[a, l, 7:23] for a in range(nt)],
                [cells[a, l, 9:25] for a in range(nt)],
                border, weights, reaction,
            )
            for a in range(nt):
                tracers_next[a, l] = results[a]
            edge = edge_tile(results)
            shade = pigment_of(results[0], results[1])
            shade = jnp.where((inside > 0) & (inside < 15), shade, 0.0)
            for out in (out_a, out_b, out_c):
                out[2 * l] = shade[:8]
                out[2 * l + 1] = shade[8:]
                out[12 + 2 * l] = edge[:8]
                out[13 + 2 * l] = edge[8:]
            return carry

        lax.fori_loop(0, levels, level, 0)


def roll_rows(x, by):
    by = by % 8
    return x if by == 0 else pltpu.roll(x, by, 0)


def second_kernel(
    from_a, from_b, from_c, flow_next, tracers_next, wet_rows, reaction,
    out_a, out_b, out_c, flow_out, tracers_out, buffers, heat, winds,
):
    section, _, _ = place()
    levels = heat.shape[0]
    nt = tracers_next.shape[0]

    @pl.when(section == 3)
    def _():
        shades = (from_c, from_b, from_a)

        def load(l, tile, j):
            return shades[j][2 * l + tile]

        fill_heat(load, heat)
        substep(flow_next, buffers.at[0], heat, wet_rows, 2, 8, 8, 0, 4)
        substep(buffers.at[0], buffers.at[1], heat, wet_rows, 2, 8, 8, 0, 4)
        substep(buffers.at[1], buffers.at[2], heat, wet_rows, 2, 8, 8, 0, 4)
        substep(buffers.at[2], flow_out, heat, wet_rows, 1, 12, 0, 4, 8)
        outs = (out_a, out_b, out_c)
        for l in range(levels):
            for j in range(3):
                cols = slice(128 * j, 128 * j + 128)
                for f in range(2):
                    total = buffers[0, f, l, 12:20, cols] + buffers[1, f, l, 12:20, cols]
                    total = total + buffers[2, f, l, 12:20, cols]
                    outs[j][6 * f + l] = 0.25 * (total + flow_out[f, l, :, cols])
                outs[j][12 + l] = flow_out[2, l, :, cols]
                outs[j][18 + l] = flow_out[3, l, :, cols]

        def clear(l, carry):
            for a in range(nt):
                tracers_out[a, l] = jnp.zeros((8, 128), F32)
            return carry

        lax.fori_loop(0, levels, clear, 0)

    @pl.when(section != 3)
    def _():
        def driven(i):
            return jnp.where(
                section == 0, from_a[i], jnp.where(section == 1, from_b[i], from_c[i])
            )

        for i in range(18):
            winds[i] = driven(i)
        edge_v = driven(18)
        rows_above = driven(19)
        rows_below = driven(20)
        lane = lanes(8)
        sub = lax.broadcasted_iota(jnp.int32, (8, 128), 0)
        for l in range(levels):
            u, v = winds[l], winds[6 + l]
            winds[18 + l] = jnp.where(sub == 0, roll_rows(rows_above, -l), roll_rows(u, 1))
            winds[24 + l] = jnp.where(sub == 7, roll_rows(rows_below, 7 - l), roll_rows(u, 7))
            winds[30 + l] = jnp.where(
                lane == 127, roll_lanes(edge_v, 126 - 2 * l), roll_lanes(v, 127)
            )
            winds[36 + l] = jnp.where(lane == 0, roll_lanes(edge_v, -2 * l), roll_lanes(v, 1))
            borders = [
                open_edges(section, from_a[12 + 2 * l + i], from_c[12 + 2 * l + i], 8)
                for i in range(2)
            ]
            half = upper_half()
            winds[42 + l] = swap(jnp.where(half, borders[1], borders[0]))
        col = pl.ds(pl.multiple_of(section * 128, 128), 128)
        floor = wet_rows[8:16, col]

        def level(l, carry):
            weights = tracer_weights(
                winds[18 + l], winds[24 + l], winds[30 + l], winds[36 + l], winds[12 + l], floor > l
            )
            results = tracer_level(
                [tracers_next[a, l, 4:12] for a in range(nt)],
                [tracers_next[a, l, 3:11] for a in range(nt)],
                [tracers_next[a, l, 5:13] for a in range(nt)],
                winds[42 + l], weights, reaction,
            )
            for a in range(nt):
                tracers_out[a, l] = results[a]
            shade = pigment_of(results[0], results[1])
            for out in (out_a, out_b, out_c):
                out[l] = shade
                for i in range(1, 4):
                    out[6 * i + l] = jnp.zeros((8, 128), F32)
            for f in range(4):
                flow_out[f, l] = jnp.zeros_like(flow_out[f, l])
            return carry

        lax.fori_loop(0, levels, level, 0)


def last_kernel(from_a, from_b, from_c, light_out, forcing_out):
    section, _, _ = place()
    levels = light_out.shape[0]
    is_dynamics = section == 3
    for l in range(levels):
        for j, shade in enumerate((from_c, from_b, from_a)):
            light_out[l, :, 128 * j : 128 * j + 128] = jnp.where(is_dynamics, shade[l], 0.0)
        for f in range(4):
            i = 6 * f + l
            picked = jnp.where(
                section == 0, from_a[i], jnp.where(section == 1, from_b[i], from_c[i])
            )
            forcing_out[f, l] = jnp.where(is_dynamics, 0.0, picked)


def call(kernel, shapes, operands, spaces, scratch=()):
    return pl.pallas_call(
        kernel,
        out_shape=[jax.ShapeDtypeStruct(shape, dtype) for shape, dtype in shapes],
        in_specs=[pl.BlockSpec(memory_space=space) for space in spaces],
        out_specs=[pl.BlockSpec(memory_space=pltpu.VMEM) for _ in shapes],
        scratch_shapes=list(scratch),
        compiler_params=pltpu.CompilerParams(vmem_limit_bytes=VMEM_LIMIT),
    )(*operands)


def route(target):
    total = lax.axis_size("comp") * lax.axis_size("gy") * lax.axis_size("gx")
    group = total // SECTIONS
    pairs = []
    for moved in range(total):
        section, strip = target(moved // group, moved % group, group)
        pairs.append(((moved - 1) % total, (section * group + strip - 1) % total))
    return pairs


def across(value, by):
    return lax.ppermute(value, AXES, route(lambda k, s, g: ((k + by) % SECTIONS, s)))


def along(value, by):
    return lax.ppermute(value, AXES, route(lambda k, s, g: (k, (s + by) % g)))


def on_device(flow_fields, chlorophyll_lag, tracers, forcing, ocean_mask, bottom, reaction):
    levels = chlorophyll_lag.shape[0]
    nt = tracers.shape[0]
    breadth = flow_fields.shape[3]
    vmem, smem, anywhere = pltpu.VMEM, pltpu.SMEM, pl.ANY
    (border,) = call(edges_kernel, [((levels, 8, 128), F32)], (tracers, forcing), (vmem, vmem))
    from_left = across(border, 1)
    from_right = across(border, -1)
    (wet_rows,) = call(
        mask_kernel,
        [((24, breadth), jnp.int32)],
        (ocean_mask, bottom),
        (anywhere, anywhere),
        (
            pltpu.VMEM((3, 8, breadth), jnp.int32),
            pltpu.VMEM((3, 8, breadth), jnp.int32),
            pltpu.SemaphoreType.DMA((6,)),
        ),
    )
    message = (15, levels, 8, 128)
    to_next, to_prev, edges = call(
        rows_kernel,
        [(message, F32), (message, F32), ((levels, 8, 128), F32)],
        (flow_fields, chlorophyll_lag, tracers, forcing, from_left, from_right),
        (vmem,) * 6,
    )
    above = along(to_next, 1)
    below = along(to_prev, -1)
    exchange = ((24, 8, 128), F32)
    sent = call(
        first_kernel,
        [
            exchange, exchange, exchange,
            ((4, levels, 32, breadth), F32), ((nt, levels, 16, 128), F32),
        ],
        (flow_fields, chlorophyll_lag, tracers, forcing, edges, above, below, wet_rows, reaction),
        (vmem,) * 8 + (smem,),
        (
            pltpu.VMEM((4, 4, levels, 40, breadth), F32),
            pltpu.VMEM((levels, 24, breadth), F32),
            pltpu.VMEM((nt, levels, 32, 128), F32),
            pltpu.VMEM((4, levels, 32, 128), F32),
        ),
    )
    from_b = across(sent[1], 2)
    from_a = across(sent[0], 1)
    from_c = across(sent[2], -1)
    last = call(
        second_kernel,
        [
            exchange, exchange, exchange,
            ((4, levels, 8, breadth), F32), ((nt, levels, 8, 128), F32),
        ],
        (from_a, from_b, from_c, sent[3], sent[4], wet_rows, reaction),
        (vmem,) * 6 + (smem,),
        (
            pltpu.VMEM((3, 4, levels, 32, breadth), F32),
            pltpu.VMEM((levels, 16, breadth), F32),
            pltpu.VMEM((48, 8, 128), F32),
        ),
    )
    final_b = across(last[1], 2)
    final_a = across(last[0], 1)
    final_c = across(last[2], -1)
    light_out, forcing_out = call(
        last_kernel,
        [((levels, 8, breadth), F32), ((4, levels, 8, 128), F32)],
        (final_a, final_b, final_c),
        (vmem,) * 3,
    )
    return last[3], light_out, last[4], forcing_out


def solution(mesh):
    rows = P(None, None, AXES, None)
    light = P(None, AXES, None)
    return jax.shard_map(
        on_device,
        mesh=mesh,
        in_specs=(rows, light, rows, rows, P(), P(), P()),
        out_specs=(rows, light, rows, rows),
        check_vma=False,
    )
```

```python
import jax
import jax.numpy as jnp
from jax import lax
from jax.experimental import pallas as pl
from jax.experimental.pallas import tpu as pltpu
from jax.sharding import PartitionSpec as P

AXES = ("comp", "gy", "gx")
SECTIONS = 4
DT = 0.1
F32 = jnp.float32
UNROLL = 2
VMEM_LIMIT = 48 * 1024 * 1024


def place():
    gy = lax.axis_size("gy")
    gx = lax.axis_size("gx")
    total = lax.axis_size("comp") * gy * gx
    group = total // SECTIONS
    position = (lax.axis_index("comp") * gy + lax.axis_index("gy")) * gx + lax.axis_index("gx")
    moved = lax.rem(position + 1, total)
    return moved // group, lax.rem(moved, group), group


def lanes(rows):
    return lax.broadcasted_iota(jnp.int32, (rows, 128), 1)


def roll_lanes(x, by):
    by = by % 128
    return x if by == 0 else pltpu.roll(x, by, 1)


def swap(x):
    return pltpu.roll(x, 4, 0)


def upper_half():
    return lax.broadcasted_iota(jnp.int32, (8, 128), 0) < 4


def spread(flag):
    return jnp.where(flag, 1.0, 0.0).astype(F32)


def edge_tile(planes):
    lane = lanes(planes[0].shape[0])
    edges = jnp.zeros_like(planes[0])
    for a, x in enumerate(planes):
        edges = jnp.where(lane == a, roll_lanes(x, a + 1), edges)
        edges = jnp.where(lane == 64 + a, roll_lanes(x, 64 + a), edges)
    return edges


def load_kernel(
    flow, pigment, tracers, forcing, ocean, bottom,
    border, flow_in, pigment_in, tracers_in, forcing_in, wet_rows,
    ocean_rows, bottom_rows, mask_sems, sems,
):
    section, strip, group = place()
    levels = pigment.shape[0]
    nt = tracers.shape[0]
    starts = [jnp.maximum(strip - 1, 0), strip, jnp.minimum(strip + 1, group - 1)]
    masks = []
    for i, start in enumerate(starts):
        rows = pl.ds(pl.multiple_of(start * 8, 8), 8)
        masks.append(pltpu.make_async_copy(ocean.at[rows], ocean_rows.at[i], mask_sems.at[i]))
        masks.append(pltpu.make_async_copy(bottom.at[rows], bottom_rows.at[i], mask_sems.at[3 + i]))

    @pl.when(section == 3)
    def _():
        copies = []
        for j in range(3):
            cols = slice(128 * j, 128 * j + 128)
            copies.append(
                pltpu.make_async_copy(flow.at[:, :, :, cols], flow_in.at[:, :, j], sems.at[j])
            )
            copies.append(
                pltpu.make_async_copy(pigment.at[:, :, cols], pigment_in.at[:, j], sems.at[3 + j])
            )
        for copy in copies + masks:
            copy.start()
        border[...] = jnp.zeros_like(border)
        for copy in copies + masks:
            copy.wait()

    @pl.when(section != 3)
    def _():
        copies = []
        for l in range(levels):
            copies.append(
                pltpu.make_async_copy(tracers.at[:, l], tracers_in.at[:, l], sems.at[l])
            )
            copies.append(
                pltpu.make_async_copy(forcing.at[:, l], forcing_in.at[:, l], sems.at[levels + l])
            )
        for copy in copies + masks:
            copy.start()
        for l in range(levels):
            copies[2 * l].wait()
            copies[2 * l + 1].wait()
            border[l] = edge_tile([tracers_in[a, l] for a in range(nt)] + [forcing_in[1, l]])
        for copy in masks:
            copy.wait()

    inside = [(strip > 0).astype(jnp.int32), 1, (strip < group - 1).astype(jnp.int32)]
    for i in range(3):
        floor = jnp.where(ocean_rows[i] == 1, bottom_rows[i], 0) * inside[i]
        for j in range(3):
            wet_rows[j, 8 * i : 8 * i + 8] = floor[:, 128 * j : 128 * j + 128]


def open_edges(section, from_left, from_right, rows):
    lane = lanes(rows)
    left = jnp.where(section > 0, from_left, 0.0)
    right = jnp.where(section < 2, from_right, 0.0)
    return jnp.where(lane < 64, left, right)


def rows_kernel(flow, pigment, tracers, forcing, from_left, from_right, to_next, to_prev, edges):
    section, _, _ = place()
    levels = pigment.shape[0]
    nt = tracers.shape[0]

    @pl.when(section == 3)
    def _():
        def level(l, carry):
            for f in range(5):
                for j in range(3):
                    tile = flow[f, l, j] if f < 4 else pigment[l, j]
                    to_next[3 * f + j, l] = tile
                    to_prev[3 * f + j, l] = tile
            return carry

        lax.fori_loop(0, levels, level, 0)
        edges[...] = jnp.zeros_like(edges)

    @pl.when(section != 3)
    def _():
        half = upper_half()
        for l in range(levels):
            edges[l] = open_edges(section, from_left[l], from_right[l], 8)

        def put(plane, pair, even, odd):
            row, col = plane // 2, 3 * (plane % 2)
            to_next[row, col + pair] = jnp.where(half, swap(even), odd)
            to_prev[row, col + pair] = jnp.where(half, even, swap(odd))

        for pair in range(3):
            even, odd = 2 * pair, 2 * pair + 1
            for a in range(nt):
                put(a, pair, tracers[a, even], tracers[a, odd])
            put(nt, pair, forcing[0, even], forcing[0, odd])
            put(nt + 1, pair, forcing[1, even], forcing[1, odd])
            growth = [jnp.exp(0.1 * forcing[2, l] - 0.05 * forcing[3, l]) for l in (even, odd)]
            put(nt + 2, pair, growth[0], growth[1])
            put(nt + 3, pair, edges[even], edges[odd])
        for row in range(10, 15):
            for l in range(levels):
                to_next[row, l] = jnp.zeros((8, 128), F32)
                to_prev[row, l] = jnp.zeros((8, 128), F32)


def shifted(tiles):
    lane = lanes(tiles[0].shape[0])
    left = [roll_lanes(x, 127) for x in tiles]
    right = [roll_lanes(x, 1) for x in tiles]
    count = len(tiles)
    east = [
        jnp.where(lane == 127, left[j + 1] if j + 1 < count else 0.0, left[j]) for j in range(count)
    ]
    west = [jnp.where(lane == 0, right[j - 1] if j > 0 else 0.0, right[j]) for j in range(count)]
    return east, west


def substep(source, target, heat, wet_rows, tiles, read_at, write_at, heat_at, wet_at):
    levels = heat.shape[0]
    thirds = 3
    zero = jnp.zeros((8, 128), F32)

    def level(l, carry):
        slopes = []
        for tile in range(tiles):
            row = read_at + 8 * tile
            put = write_at + 8 * tile
            slope_x, slope_y = carry[tile]

            def load(f, by):
                return [source[f, l, j, row + by : row + by + 8] for j in range(thirds)]

            centre = [load(f, 0) for f in range(4)]
            up = [load(f, -1) for f in range(4)]
            down = [load(f, 1) for f in range(4)]
            sides = [shifted(centre[f]) for f in range(4)]
            new_x, new_y = [], []
            for j in range(thirds):
                u, v, t, s = (centre[f][j] for f in range(4))
                un, vn, tn, sn = (up[f][j] for f in range(4))
                us, vs, ts, ss = (down[f][j] for f in range(4))
                ue, ve, te, se = (sides[f][0][j] for f in range(4))
                uw, vw, tw, sw = (sides[f][1][j] for f in range(4))
                px = slope_x[j] + ((ss - sn) - (ts - tn))
                py = slope_y[j] + ((se - sw) - (te - tw))
                new_x.append(px)
                new_y.append(py)
                is_wet = wet_rows[j, wet_at + 8 * tile : wet_at + 8 * tile + 8] > l
                a = 0.05 - 0.05 * us
                b = 0.05 + 0.05 * un
                c = 0.05 - 0.05 * ve
                d = 0.05 + 0.05 * vw
                h = heat[l, j, heat_at + 8 * tile : heat_at + 8 * tile + 8]
                results = (
                    0.79 * u + 0.1 * v - 0.01 * px + 0.05 * ((un + us) + (ue + uw)),
                    0.79 * v - 0.1 * u - 0.01 * py + 0.05 * ((vn + vs) + (ve + vw)),
                    (0.8 * t + h) + ((ts * a + tn * b) + (te * c + tw * d)),
                    0.8 * s + ((ss * a + sn * b) + (se * c + sw * d)),
                )
                for f in range(4):
                    target[f, l, j, put : put + 8] = jnp.where(is_wet, results[f], 0.0)
            slopes.append((new_x, new_y))
        return slopes

    start = [([zero] * thirds, [zero] * thirds) for _ in range(tiles)]
    lax.fori_loop(0, levels, level, start, unroll=UNROLL)


def fill_heat(load, heat):
    levels, rows = heat.shape[0], heat.shape[2]
    for tile in range(rows // 8):
        for j in range(3):
            optical = jnp.zeros((8, 128), F32)
            light = jnp.ones((8, 128), F32)
            for l in range(levels):
                optical = optical + (0.05 + 0.3 * load(l, tile, j))
                lower = jnp.exp(-optical)
                heat[l, j, 8 * tile : 8 * tile + 8] = (5.0 * DT) * (light - lower)
                light = lower


def extend(own, above, below, half):
    turned = swap(own)
    return jnp.concatenate([jnp.where(half, above, turned), jnp.where(half, turned, below)], axis=0)


def tracer_weights(u_up, u_down, v_east, v_west, growth, is_wet):
    wet = spread(is_wet)
    scale = wet * 0.05
    return (
        scale - scale * u_down,
        scale + scale * u_up,
        scale - scale * v_east,
        scale + scale * v_west,
        wet * 0.8,
        (wet * DT) * growth,
    )


def tracer_level(centre, up, down, edges, weights, reaction):
    nt = len(centre)
    lane = lanes(edges.shape[0])
    a, b, c, d, keep, grow = weights
    results = []
    for i in range(nt):
        east = jnp.where(lane == 127, roll_lanes(edges, 63 - i), roll_lanes(centre[i], 127))
        west = jnp.where(lane == 0, roll_lanes(edges, -i), roll_lanes(centre[i], 1))
        mixed = reaction[i, 0] * centre[0]
        for k in range(1, nt):
            mixed = mixed + reaction[i, k] * centre[k]
        results.append(
            (keep * centre[i] + grow * mixed)
            + ((down[i] * a + up[i] * b) + (east * c + west * d))
        )
    return results


def pigment_of(first, second):
    return 0.25 * (first * first + second * second)


def first_kernel(
    flow, pigment, tracers, forcing, edges, above, below, wet_rows, reaction,
    out_a, out_b, out_c, flow_next, tracers_next, field_0, field_1, field_2, field_3, heat, cells, winds,
):
    section, strip, group = place()
    levels = pigment.shape[0]
    nt = tracers.shape[0]
    low = spread(strip > 0)
    high = spread(strip < group - 1)

    @pl.when(section == 3)
    def _():
        def fill(l, carry):
            for f in range(4):
                for j in range(3):
                    field_0[f, l, j, 8:16] = above[3 * f + j, l] * low
                    field_0[f, l, j, 16:24] = flow[f, l, j]
                    field_0[f, l, j, 24:32] = below[3 * f + j, l] * high
            return carry

        lax.fori_loop(0, levels, fill, 0)

        def load(l, tile, j):
            if tile == 1:
                return pigment[l, j]
            return (above if tile == 0 else below)[12 + j, l]

        fill_heat(load, heat)
        substep(field_0, field_1, heat, wet_rows, 3, 8, 8, 0, 0)
        substep(field_1, field_2, heat, wet_rows, 3, 8, 8, 0, 0)
        substep(field_2, field_3, heat, wet_rows, 3, 8, 8, 0, 0)
        substep(field_3, flow_next, heat, wet_rows, 2, 12, 8, 4, 4)
        lane = lanes(8)
        outs = (out_a, out_b, out_c)
        sub = lax.broadcasted_iota(jnp.int32, (8, 128), 0)

        def mean(f, l, row, j):
            total = field_1[f, l, j, row : row + 8] + field_2[f, l, j, row : row + 8]
            total = total + field_3[f, l, j, row : row + 8]
            return 0.25 * (total + flow_next[f, l, j, row - 4 : row + 4])

        edge_v = [jnp.zeros((8, 128), F32) for _ in range(3)]
        rows_above = [jnp.zeros((8, 128), F32) for _ in range(3)]
        rows_below = [jnp.zeros((8, 128), F32) for _ in range(3)]
        for l in range(levels):
            v_mean = []
            for j in range(3):
                outs[j][l] = mean(0, l, 16, j)
                v_mean.append(mean(1, l, 16, j))
                outs[j][6 + l] = v_mean[j]
                warm = flow_next[2, l, j, 12:20]
                salt = flow_next[3, l, j, 12:20]
                outs[j][12 + l] = jnp.exp(0.1 * warm - 0.05 * salt)
                first = mean(0, l, 15, j)
                last = mean(0, l, 17, j)
                rows_above[j] = jnp.where(sub == l, roll_rows(first, l), rows_above[j])
                rows_below[j] = jnp.where(sub == l, roll_rows(last, l + 1), rows_below[j])
            for j in range(3):
                if j > 0:
                    edge_v[j] = jnp.where(
                        lane == 2 * l, roll_lanes(v_mean[j - 1], 2 * l + 1), edge_v[j]
                    )
                if j < 2:
                    edge_v[j] = jnp.where(
                        lane == 2 * l + 1, roll_lanes(v_mean[j + 1], 2 * l + 1), edge_v[j]
                    )
        for j in range(3):
            outs[j][18] = edge_v[j]
            outs[j][19] = rows_above[j]
            outs[j][20] = rows_below[j]
            for i in range(21, 24):
                outs[j][i] = jnp.zeros((8, 128), F32)

    @pl.when(section != 3)
    def _():
        half = upper_half()

        def halo(message, plane, pair, odd, upward):
            tile = message[plane // 2, 3 * (plane % 2) + pair]
            return swap(tile) if odd != upward else tile

        def build(plane, own, l, masked):
            pair, odd = l // 2, l % 2 == 1
            up = halo(above, plane, pair, odd, False)
            down = halo(below, plane, pair, not odd, False)
            if masked:
                up, down = up * low, down * high
            return extend(own, up, down, half)

        for l in range(levels):
            for a in range(nt):
                cells[a, l, 8:24] = build(a, tracers[a, l], l, True)
            winds[0, l, 8:24] = build(nt, forcing[0, l], l, False)
            winds[1, l, 8:24] = build(nt + 1, forcing[1, l], l, False)
            growth = jnp.exp(0.1 * forcing[2, l] - 0.05 * forcing[3, l])
            winds[2, l, 8:24] = build(nt + 2, growth, l, False)
            winds[3, l, 8:24] = build(nt + 3, edges[l], l, False)
        floor = wet_rows[section, 4:20]
        lane = lanes(16)
        inside = lax.broadcasted_iota(jnp.int32, (16, 128), 0)

        def level(l, carry):
            border = winds[3, l, 8:24]
            v = winds[1, l, 8:24]
            v_east = jnp.where(lane == 127, roll_lanes(border, 63 - nt), roll_lanes(v, 127))
            v_west = jnp.where(lane == 0, roll_lanes(border, -nt), roll_lanes(v, 1))
            weights = tracer_weights(
                winds[0, l, 7:23], winds[0, l, 9:25], v_east, v_west, winds[2, l, 8:24], floor > l
            )
            results = tracer_level(
                [cells[a, l, 8:24] for a in range(nt)],
                [cells[a, l, 7:23] for a in range(nt)],
                [cells[a, l, 9:25] for a in range(nt)],
                border, weights, reaction,
            )
            for a in range(nt):
                tracers_next[a, l] = results[a]
            edge = edge_tile(results)
            shade = pigment_of(results[0], results[1])
            shade = jnp.where((inside > 0) & (inside < 15), shade, 0.0)
            for out in (out_a, out_b, out_c):
                out[2 * l] = shade[:8]
                out[2 * l + 1] = shade[8:]
                out[12 + 2 * l] = edge[:8]
                out[13 + 2 * l] = edge[8:]
            return carry

        lax.fori_loop(0, levels, level, 0)


def roll_rows(x, by):
    by = by % 8
    return x if by == 0 else pltpu.roll(x, by, 0)


def second_kernel(
    from_a, from_b, from_c, flow_next, tracers_next, wet_rows, reaction,
    out_a, out_b, out_c, flow_last, tracers_last, field_0, field_1, field_2, heat, winds,
):
    section, _, _ = place()
    levels = heat.shape[0]
    nt = tracers_next.shape[0]

    @pl.when(section == 3)
    def _():
        shades = (from_c, from_b, from_a)

        def load(l, tile, j):
            return shades[j][2 * l + tile]

        fill_heat(load, heat)
        substep(flow_next, field_0, heat, wet_rows, 2, 8, 8, 0, 4)
        substep(field_0, field_1, heat, wet_rows, 2, 8, 8, 0, 4)
        substep(field_1, field_2, heat, wet_rows, 2, 8, 8, 0, 4)
        substep(field_2, flow_last, heat, wet_rows, 1, 12, 0, 4, 8)
        outs = (out_a, out_b, out_c)
        for l in range(levels):
            for j in range(3):
                for f in range(2):
                    total = field_0[f, l, j, 12:20] + field_1[f, l, j, 12:20]
                    total = total + field_2[f, l, j, 12:20]
                    outs[j][6 * f + l] = 0.25 * (total + flow_last[f, l, j])
                outs[j][12 + l] = flow_last[2, l, j]
                outs[j][18 + l] = flow_last[3, l, j]

    @pl.when(section != 3)
    def _():
        def driven(i):
            return jnp.where(
                section == 0, from_a[i], jnp.where(section == 1, from_b[i], from_c[i])
            )

        for i in range(18):
            winds[i] = driven(i)
        edge_v = driven(18)
        rows_above = driven(19)
        rows_below = driven(20)
        lane = lanes(8)
        sub = lax.broadcasted_iota(jnp.int32, (8, 128), 0)
        for l in range(levels):
            u, v = winds[l], winds[6 + l]
            winds[18 + l] = jnp.where(sub == 0, roll_rows(rows_above, -l), roll_rows(u, 1))
            winds[24 + l] = jnp.where(sub == 7, roll_rows(rows_below, 7 - l), roll_rows(u, 7))
            winds[30 + l] = jnp.where(
                lane == 127, roll_lanes(edge_v, 126 - 2 * l), roll_lanes(v, 127)
            )
            winds[36 + l] = jnp.where(lane == 0, roll_lanes(edge_v, -2 * l), roll_lanes(v, 1))
            borders = [
                open_edges(section, from_a[12 + 2 * l + i], from_c[12 + 2 * l + i], 8)
                for i in range(2)
            ]
            half = upper_half()
            winds[42 + l] = swap(jnp.where(half, borders[1], borders[0]))
        floor = wet_rows[section, 8:16]

        def level(l, carry):
            weights = tracer_weights(
                winds[18 + l], winds[24 + l], winds[30 + l], winds[36 + l], winds[12 + l], floor > l
            )
            results = tracer_level(
                [tracers_next[a, l, 4:12] for a in range(nt)],
                [tracers_next[a, l, 3:11] for a in range(nt)],
                [tracers_next[a, l, 5:13] for a in range(nt)],
                winds[42 + l], weights, reaction,
            )
            for a in range(nt):
                tracers_last[a, l] = results[a]
            shade = pigment_of(results[0], results[1])
            for out in (out_a, out_b, out_c):
                out[l] = shade
                for i in range(1, 4):
                    out[6 * i + l] = jnp.zeros((8, 128), F32)
            return carry

        lax.fori_loop(0, levels, level, 0)


def store_kernel(flow_last, tracers_last, flow_out, tracers_out, blank, sems):
    section, _, _ = place()
    blank[...] = jnp.zeros_like(blank)

    def put(flow_of, tracers_from):
        copies = [pltpu.make_async_copy(tracers_from, tracers_out, sems.at[3])]
        for j in range(3):
            target = flow_out.at[:, :, :, 128 * j : 128 * j + 128]
            copies.append(pltpu.make_async_copy(flow_of(j), target, sems.at[j]))
        for copy in copies:
            copy.start()
        for copy in copies:
            copy.wait()

    @pl.when(section == 3)
    def _():
        put(lambda j: flow_last.at[:, :, j], blank)

    @pl.when(section != 3)
    def _():
        put(lambda j: blank.at[0:4], tracers_last)


def last_kernel(from_a, from_b, from_c, light_out, forcing_out):
    section, _, _ = place()
    levels = light_out.shape[0]
    is_dynamics = section == 3
    for l in range(levels):
        for j, shade in enumerate((from_c, from_b, from_a)):
            light_out[l, :, 128 * j : 128 * j + 128] = jnp.where(is_dynamics, shade[l], 0.0)
        for f in range(4):
            i = 6 * f + l
            picked = jnp.where(
                section == 0, from_a[i], jnp.where(section == 1, from_b[i], from_c[i])
            )
            forcing_out[f, l] = jnp.where(is_dynamics, 0.0, picked)


def call(kernel, shapes, operands, spaces, scratch=(), out_space=pltpu.VMEM):
    operands = [
        pltpu.with_memory_space_constraint(x, pltpu.HBM) if space == pltpu.HBM else x
        for x, space in zip(operands, spaces)
    ]
    return pl.pallas_call(
        kernel,
        out_shape=[jax.ShapeDtypeStruct(shape, dtype) for shape, dtype in shapes],
        in_specs=[pl.BlockSpec(memory_space=space) for space in spaces],
        out_specs=[pl.BlockSpec(memory_space=out_space) for _ in shapes],
        scratch_shapes=list(scratch),
        compiler_params=pltpu.CompilerParams(vmem_limit_bytes=VMEM_LIMIT),
    )(*operands)


def route(target):
    total = lax.axis_size("comp") * lax.axis_size("gy") * lax.axis_size("gx")
    group = total // SECTIONS
    pairs = []
    for moved in range(total):
        section, strip = target(moved // group, moved % group, group)
        pairs.append(((moved - 1) % total, (section * group + strip - 1) % total))
    return pairs


def across(value, by):
    return lax.ppermute(value, AXES, route(lambda k, s, g: ((k + by) % SECTIONS, s)))


def along(value, by):
    return lax.ppermute(value, AXES, route(lambda k, s, g: (k, (s + by) % g)))


def on_device(flow_fields, chlorophyll_lag, tracers, forcing, ocean_mask, bottom, reaction):
    levels = chlorophyll_lag.shape[0]
    nt = tracers.shape[0]
    breadth = flow_fields.shape[3]
    vmem, smem, hbm = pltpu.VMEM, pltpu.SMEM, pltpu.HBM
    border, flow, pigment, tracers, forcing, wet_rows = call(
        load_kernel,
        [
            ((levels, 8, 128), F32), ((4, levels, 3, 8, 128), F32), ((levels, 3, 8, 128), F32),
            (tracers.shape, F32), (forcing.shape, F32), ((3, 24, 128), jnp.int32),
        ],
        (flow_fields, chlorophyll_lag, tracers, forcing, ocean_mask, bottom),
        (hbm,) * 6,
        (
            pltpu.VMEM((3, 8, breadth), jnp.int32),
            pltpu.VMEM((3, 8, breadth), jnp.int32),
            pltpu.SemaphoreType.DMA((6,)),
            pltpu.SemaphoreType.DMA((2 * levels,)),
        ),
    )
    from_left = across(border, 1)
    from_right = across(border, -1)
    message = (15, levels, 8, 128)
    to_next, to_prev, edges = call(
        rows_kernel,
        [(message, F32), (message, F32), ((levels, 8, 128), F32)],
        (flow, pigment, tracers, forcing, from_left, from_right),
        (vmem,) * 6,
    )
    above = along(to_next, 1)
    below = along(to_prev, -1)
    exchange = ((24, 8, 128), F32)
    sent = call(
        first_kernel,
        [
            exchange, exchange, exchange,
            ((4, levels, 3, 32, 128), F32), ((nt, levels, 16, 128), F32),
        ],
        (flow, pigment, tracers, forcing, edges, above, below, wet_rows, reaction),
        (vmem,) * 8 + (smem,),
        (
            *[pltpu.VMEM((4, levels, 3, 40, 128), F32) for _ in range(4)],
            pltpu.VMEM((levels, 3, 24, 128), F32),
            pltpu.VMEM((nt, levels, 32, 128), F32),
            pltpu.VMEM((4, levels, 32, 128), F32),
        ),
    )
    from_b = across(sent[1], 2)
    from_a = across(sent[0], 1)
    from_c = across(sent[2], -1)
    last = call(
        second_kernel,
        [
            exchange, exchange, exchange,
            ((4, levels, 3, 8, 128), F32), ((nt, levels, 8, 128), F32),
        ],
        (from_a, from_b, from_c, sent[3], sent[4], wet_rows, reaction),
        (vmem,) * 6 + (smem,),
        (
            *[pltpu.VMEM((4, levels, 3, 32, 128), F32) for _ in range(3)],
            pltpu.VMEM((levels, 3, 16, 128), F32),
            pltpu.VMEM((48, 8, 128), F32),
        ),
    )
    final_b = across(last[1], 2)
    final_a = across(last[0], 1)
    final_c = across(last[2], -1)
    flow_out, tracers_out = call(
        store_kernel,
        [(flow_fields.shape, F32), (tracers.shape, F32)],
        (last[3], last[4]),
        (vmem, vmem),
        (pltpu.VMEM(tracers.shape, F32), pltpu.SemaphoreType.DMA((4,))),
        hbm,
    )
    light_out, forcing_out = call(
        last_kernel,
        [((levels, 8, breadth), F32), ((4, levels, 8, 128), F32)],
        (final_a, final_b, final_c),
        (vmem,) * 3,
    )
    return flow_out, light_out, tracers_out, forcing_out


def solution(mesh):
    rows = P(None, None, AXES, None)
    light = P(None, AXES, None)
    return jax.shard_map(
        on_device,
        mesh=mesh,
        in_specs=(rows, light, rows, rows, P(), P(), P()),
        out_specs=(rows, light, rows, rows),
        check_vma=False,
    )
```

```python
import jax
import jax.numpy as jnp
from jax import lax
from jax.experimental import pallas as pl
from jax.experimental.pallas import tpu as pltpu
from jax.sharding import PartitionSpec as P

AXES = ("comp", "gy", "gx")
SECTIONS = 4
DT = 0.1
F32 = jnp.float32
UNROLL = 2
VMEM_LIMIT = 48 * 1024 * 1024


def place():
    gy = lax.axis_size("gy")
    gx = lax.axis_size("gx")
    total = lax.axis_size("comp") * gy * gx
    group = total // SECTIONS
    position = (lax.axis_index("comp") * gy + lax.axis_index("gy")) * gx + lax.axis_index("gx")
    moved = lax.rem(position + 1, total)
    return moved // group, lax.rem(moved, group), group


def lanes(rows):
    return lax.broadcasted_iota(jnp.int32, (rows, 128), 1)


def roll_lanes(x, by):
    by = by % 128
    return x if by == 0 else pltpu.roll(x, by, 1)


def swap(x):
    return pltpu.roll(x, 4, 0)


def upper_half():
    return lax.broadcasted_iota(jnp.int32, (8, 128), 0) < 4


def spread(flag):
    return jnp.where(flag, 1.0, 0.0).astype(F32)


def edge_tile(planes):
    pair = lanes(planes[0].shape[0]) // 2
    edges = jnp.zeros_like(planes[0])
    for a, x in enumerate(planes):
        edges = jnp.where(pair == a, roll_lanes(x, 2 * a + 1), edges)
    return edges


def pack_rows(tracers, forcing, to_next, to_prev):
    half = upper_half()
    nt, levels = tracers.shape[0], tracers.shape[1]

    def put(plane, pair, even, odd):
        row, col = plane // 2, 3 * (plane % 2)
        to_next[row, col + pair] = jnp.where(half, swap(even), odd)
        to_prev[row, col + pair] = jnp.where(half, even, swap(odd))

    for pair in range(levels // 2):
        even, odd = 2 * pair, 2 * pair + 1
        for a in range(nt):
            put(a, pair, tracers[a, even], tracers[a, odd])
        put(nt, pair, forcing[0, even], forcing[0, odd])
        put(nt + 1, pair, forcing[1, even], forcing[1, odd])
        growth = [jnp.exp(0.1 * forcing[2, l] - 0.05 * forcing[3, l]) for l in (even, odd)]
        put(nt + 2, pair, growth[0], growth[1])
        put(nt + 3, pair, jnp.zeros((8, 128), F32), jnp.zeros((8, 128), F32))
    for row in range(10, 15):
        for l in range(levels):
            to_next[row, l] = jnp.zeros((8, 128), F32)
            to_prev[row, l] = jnp.zeros((8, 128), F32)


def load_kernel(
    flow, pigment, tracers, forcing, ocean, bottom,
    to_next, to_prev, flow_in, pigment_in, tracers_in, forcing_in, wet_rows,
    ocean_rows, bottom_rows, mask_sems, sems,
):
    section, strip, group = place()
    levels = pigment.shape[0]
    starts = [jnp.maximum(strip - 1, 0), strip, jnp.minimum(strip + 1, group - 1)]
    masks = []
    for i, start in enumerate(starts):
        rows = pl.ds(pl.multiple_of(start * 8, 8), 8)
        masks.append(pltpu.make_async_copy(ocean.at[rows], ocean_rows.at[i], mask_sems.at[i]))
        masks.append(pltpu.make_async_copy(bottom.at[rows], bottom_rows.at[i], mask_sems.at[3 + i]))

    @pl.when(section == 3)
    def _():
        copies = []
        for j in range(3):
            cols = slice(128 * j, 128 * j + 128)
            copies.append(
                pltpu.make_async_copy(flow.at[:, :, :, cols], flow_in.at[:, :, j], sems.at[j])
            )
            copies.append(
                pltpu.make_async_copy(pigment.at[:, :, cols], pigment_in.at[:, j], sems.at[3 + j])
            )
        for copy in copies + masks:
            copy.start()
        for copy in copies + masks:
            copy.wait()

        def level(l, carry):
            for f in range(5):
                for j in range(3):
                    tile = flow_in[f, l, j] if f < 4 else pigment_in[l, j]
                    to_next[3 * f + j, l] = tile
                    to_prev[3 * f + j, l] = tile
            return carry

        lax.fori_loop(0, levels, level, 0)

    @pl.when(section != 3)
    def _():
        copies = []
        for l in range(levels):
            copies.append(
                pltpu.make_async_copy(tracers.at[:, l], tracers_in.at[:, l], sems.at[l])
            )
            copies.append(
                pltpu.make_async_copy(forcing.at[:, l], forcing_in.at[:, l], sems.at[levels + l])
            )
        for copy in copies + masks:
            copy.start()
        for copy in copies + masks:
            copy.wait()
        pack_rows(tracers_in, forcing_in, to_next, to_prev)

    inside = [(strip > 0).astype(jnp.int32), 1, (strip < group - 1).astype(jnp.int32)]
    for i in range(3):
        floor = jnp.where(ocean_rows[i] == 1, bottom_rows[i], 0) * inside[i]
        for j in range(3):
            wet_rows[j, 8 * i : 8 * i + 8] = floor[:, 128 * j : 128 * j + 128]


def side_columns(section, from_left, from_right):
    even = lanes(from_left.shape[0]) % 2 == 0
    east = jnp.where(section < 2, roll_lanes(from_right, -1), 0.0)
    west = jnp.where(section > 0, roll_lanes(from_left, 1), 0.0)
    return jnp.where(even, east, west)


def shifted(tiles):
    lane = lanes(tiles[0].shape[0])
    left = [roll_lanes(x, 127) for x in tiles]
    right = [roll_lanes(x, 1) for x in tiles]
    count = len(tiles)
    east = [
        jnp.where(lane == 127, left[j + 1] if j + 1 < count else 0.0, left[j]) for j in range(count)
    ]
    west = [jnp.where(lane == 0, right[j - 1] if j > 0 else 0.0, right[j]) for j in range(count)]
    return east, west


def substep(source, target, heat, wet_rows, tiles, read_at, write_at, heat_at, wet_at):
    levels = target.shape[1]
    thirds = 3
    zero = jnp.zeros((8, 128), F32)

    def level(l, carry):
        slopes = []
        for tile in range(tiles):
            row = read_at + 8 * tile
            put = write_at + 8 * tile
            slope_x, slope_y = carry[tile]

            def load(f, by):
                return [source[f][l, j, row + by : row + by + 8] for j in range(thirds)]

            centre = [load(f, 0) for f in range(4)]
            up = [load(f, -1) for f in range(4)]
            down = [load(f, 1) for f in range(4)]
            sides = [shifted(centre[f]) for f in range(4)]
            new_x, new_y = [], []
            for j in range(thirds):
                u, v, t, s = (centre[f][j] for f in range(4))
                un, vn, tn, sn = (up[f][j] for f in range(4))
                us, vs, ts, ss = (down[f][j] for f in range(4))
                ue, ve, te, se = (sides[f][0][j] for f in range(4))
                uw, vw, tw, sw = (sides[f][1][j] for f in range(4))
                px = slope_x[j] + ((ss - sn) - (ts - tn))
                py = slope_y[j] + ((se - sw) - (te - tw))
                new_x.append(px)
                new_y.append(py)
                is_wet = wet_rows[j, wet_at + 8 * tile : wet_at + 8 * tile + 8] > l
                a = 0.05 - 0.05 * us
                b = 0.05 + 0.05 * un
                c = 0.05 - 0.05 * ve
                d = 0.05 + 0.05 * vw
                kept = 0.8 * t
                if heat is not None:
                    kept = kept + heat[l, j, heat_at + 8 * tile : heat_at + 8 * tile + 8]
                results = (
                    0.79 * u + 0.1 * v - 0.01 * px + 0.05 * ((un + us) + (ue + uw)),
                    0.79 * v - 0.1 * u - 0.01 * py + 0.05 * ((vn + vs) + (ve + vw)),
                    kept + ((ts * a + tn * b) + (te * c + tw * d)),
                    0.8 * s + ((ss * a + sn * b) + (se * c + sw * d)),
                )
                for f in range(4):
                    target[f, l, j, put : put + 8] = jnp.where(is_wet, results[f], 0.0)
            slopes.append((new_x, new_y))
        return slopes

    start = [([zero] * thirds, [zero] * thirds) for _ in range(tiles)]
    lax.fori_loop(0, levels, level, start, unroll=UNROLL)


def fill_heat(load, heat):
    levels, rows = heat.shape[0], heat.shape[2]
    for tile in range(rows // 8):
        for j in range(3):
            optical = jnp.zeros((8, 128), F32)
            light = jnp.ones((8, 128), F32)
            for l in range(levels):
                optical = optical + (0.05 + 0.3 * load(l, tile, j))
                lower = jnp.exp(-optical)
                heat[l, j, 8 * tile : 8 * tile + 8] = (5.0 * DT) * (light - lower)
                light = lower


def extend(own, above, below, half):
    turned = swap(own)
    return jnp.concatenate([jnp.where(half, above, turned), jnp.where(half, turned, below)], axis=0)


def tracer_weights(u_up, u_down, v_east, v_west, growth, is_wet):
    wet = spread(is_wet)
    scale = wet * 0.05
    return (
        scale - scale * u_down,
        scale + scale * u_up,
        scale - scale * v_east,
        scale + scale * v_west,
        wet * 0.8,
        (wet * DT) * growth,
    )


def tracer_level(centre, up, down, sides, weights, reaction):
    nt = len(centre)
    lane = lanes(centre[0].shape[0])
    a, b, c, d, keep, grow = weights
    results = []
    for i in range(nt):
        side = 0.0 if sides is None else roll_lanes(sides, -2 * i - 1)
        east = jnp.where(lane == 127, side, roll_lanes(centre[i], 127))
        west = jnp.where(lane == 0, side, roll_lanes(centre[i], 1))
        mixed = reaction[i, 0] * centre[0]
        for k in range(1, nt):
            mixed = mixed + reaction[i, k] * centre[k]
        results.append(
            (keep * centre[i] + grow * mixed)
            + ((down[i] * a + up[i] * b) + (east * c + west * d))
        )
    return results


def pigment_of(first, second):
    return 0.25 * (first * first + second * second)


def gather_kernel(tracers, forcing, above, below, cells, winds, border):
    section, strip, group = place()
    nt, levels = tracers.shape[0], tracers.shape[1]
    low = spread(strip > 0)
    high = spread(strip < group - 1)

    @pl.when(section == 3)
    def _():
        border[...] = jnp.zeros_like(border)

    @pl.when(section != 3)
    def _():
        half = upper_half()

        def halo(message, plane, pair, odd, upward):
            tile = message[plane // 2, 3 * (plane % 2) + pair]
            return swap(tile) if odd != upward else tile

        def build(plane, own, l, masked):
            pair, odd = l // 2, l % 2 == 1
            up = halo(above, plane, pair, odd, False)
            down = halo(below, plane, pair, not odd, False)
            if masked:
                up, down = up * low, down * high
            return extend(own, up, down, half)

        lane = lanes(16)
        for l in range(levels):
            v = build(nt + 1, forcing[1, l], l, False)
            scale = 0.05 + jnp.where(lane == 0, -0.05, 0.05) * v
            products = []
            for a in range(nt):
                cell = build(a, tracers[a, l], l, True)
                cells[a, l, 8:24] = cell
                products.append(scale * cell)
            winds[0, l, 8:24] = build(nt, forcing[0, l], l, False)
            winds[1, l, 8:24] = v
            growth = jnp.exp(0.1 * forcing[2, l] - 0.05 * forcing[3, l])
            winds[2, l, 8:24] = build(nt + 2, growth, l, False)
            border[l] = edge_tile(products)


def first_kernel(
    flow, pigment, above, below, cells, winds, wet_rows, reaction,
    send_a, send_b, send_c, flow_next, partial,
    field_0, field_1, field_2, field_3, heat,
):
    section, strip, group = place()
    levels = pigment.shape[0]
    nt = cells.shape[0]
    low = spread(strip > 0)
    high = spread(strip < group - 1)

    @pl.when(section == 3)
    def _():
        def fill(l, carry):
            for f in range(4):
                for j in range(3):
                    field_0[f, l, j, 8:16] = above[3 * f + j, l] * low
                    field_0[f, l, j, 16:24] = flow[f, l, j]
                    field_0[f, l, j, 24:32] = below[3 * f + j, l] * high
            return carry

        lax.fori_loop(0, levels, fill, 0)

        def load(l, tile, j):
            if tile == 1:
                return pigment[l, j]
            return (above if tile == 0 else below)[12 + j, l]

        fill_heat(load, heat)
        substep(planes(field_0), field_1, heat, wet_rows, 3, 8, 8, 0, 0)
        substep(planes(field_1), field_2, heat, wet_rows, 3, 8, 8, 0, 0)
        substep(planes(field_2), field_3, heat, wet_rows, 3, 8, 8, 0, 0)
        substep(planes(field_3), flow_next, heat, wet_rows, 2, 12, 8, 4, 4)
        lane = lanes(8)
        outs = (send_a, send_b, send_c)
        sub = lax.broadcasted_iota(jnp.int32, (8, 128), 0)

        def mean(f, l, row, j):
            total = field_1[f, l, j, row : row + 8] + field_2[f, l, j, row : row + 8]
            total = total + field_3[f, l, j, row : row + 8]
            return 0.25 * (total + flow_next[f, l, j, row - 4 : row + 4])

        edge_v = [jnp.zeros((8, 128), F32) for _ in range(3)]
        rows_above = [jnp.zeros((8, 128), F32) for _ in range(3)]
        rows_below = [jnp.zeros((8, 128), F32) for _ in range(3)]
        for l in range(levels):
            v_mean = []
            for j in range(3):
                outs[j][l] = mean(0, l, 16, j)
                v_mean.append(mean(1, l, 16, j))
                outs[j][6 + l] = v_mean[j]
                warm = flow_next[2, l, j, 12:20]
                salt = flow_next[3, l, j, 12:20]
                outs[j][12 + l] = jnp.exp(0.1 * warm - 0.05 * salt)
                first = mean(0, l, 15, j)
                last = mean(0, l, 17, j)
                rows_above[j] = jnp.where(sub == l, roll_rows(first, l), rows_above[j])
                rows_below[j] = jnp.where(sub == l, roll_rows(last, l + 1), rows_below[j])
            for j in range(3):
                if j > 0:
                    edge_v[j] = jnp.where(
                        lane == 2 * l, roll_lanes(v_mean[j - 1], 2 * l + 1), edge_v[j]
                    )
                if j < 2:
                    edge_v[j] = jnp.where(
                        lane == 2 * l + 1, roll_lanes(v_mean[j + 1], 2 * l + 1), edge_v[j]
                    )
        for j in range(3):
            outs[j][18] = edge_v[j]
            outs[j][19] = rows_above[j]
            outs[j][20] = rows_below[j]

    @pl.when(section != 3)
    def _():
        floor = wet_rows[section, 4:20]

        def level(l, carry):
            v = winds[1, l, 8:24]
            weights = tracer_weights(
                winds[0, l, 7:23], winds[0, l, 9:25], roll_lanes(v, 127), roll_lanes(v, 1),
                winds[2, l, 8:24], floor > l,
            )
            results = tracer_level(
                [cells[a, l, 8:24] for a in range(nt)],
                [cells[a, l, 7:23] for a in range(nt)],
                [cells[a, l, 9:25] for a in range(nt)],
                None, weights, reaction,
            )
            for a in range(nt):
                partial[a, l] = results[a]
            return carry

        lax.fori_loop(0, levels, level, 0)


def sides_kernel(
    from_left, from_right, send_a, send_b, send_c, partial, wet_rows,
    out_a, out_b, out_c, tracers_next,
):
    section, _, _ = place()
    nt, levels = partial.shape[0], partial.shape[1]
    outs = (out_a, out_b, out_c)

    @pl.when(section == 3)
    def _():
        for out, send in zip(outs, (send_a, send_b, send_c)):
            out[...] = send[...]

    @pl.when(section != 3)
    def _():
        floor = wet_rows[section, 4:20]
        lane = lanes(16)
        rim = (lane == 0) | (lane == 127)
        row = lax.broadcasted_iota(jnp.int32, (16, 128), 0)
        inside = (row > 0) & (row < 15)

        def level(l, carry):
            sides = side_columns(section, from_left[l], from_right[l])
            wet_rim = rim & (floor > l)
            shades = []
            for a in range(nt):
                side = jnp.where(wet_rim, roll_lanes(sides, -2 * a - 1), 0.0)
                cell = partial[a, l] + side
                tracers_next[a, l] = cell
                if a < 2:
                    shades.append(cell)
            edge = edge_tile([tracers_next[a, l, 4:12] for a in range(nt)])
            shade = jnp.where(inside, pigment_of(shades[0], shades[1]), 0.0)
            for out in outs:
                out[2 * l] = shade[:8]
                out[2 * l + 1] = shade[8:]
                out[12 + l] = edge
            return carry

        lax.fori_loop(0, levels, level, 0, unroll=2)
        for out in outs:
            for i in range(18, 21):
                out[i] = jnp.zeros((8, 128), F32)


def roll_rows(x, by):
    by = by % 8
    return x if by == 0 else pltpu.roll(x, by, 0)


def planes(buffer):
    return [buffer.at[f] for f in range(4)]


def early_kernel(flow_next, wet_rows, early):
    section, _, _ = place()

    @pl.when(section == 3)
    def _():
        substep(planes(flow_next), early, None, wet_rows, 2, 8, 8, 0, 4)


def second_kernel(
    from_a, from_b, from_c, early, tracers_next, wet_rows, reaction,
    out_a, out_b, out_c, flow_last, tracers_last, warm, field_1, field_2, heat, winds,
):
    section, _, _ = place()
    levels = heat.shape[0]
    nt = tracers_next.shape[0]

    @pl.when(section == 3)
    def _():
        shades = (from_c, from_b, from_a)

        def load(l, tile, j):
            return shades[j][2 * l + tile]

        fill_heat(load, heat)

        def warm_up(l, carry):
            for j in range(3):
                heated = jnp.where(wet_rows[j, 4:20] > l, heat[l, j], 0.0)
                warm[l, j, 8:24] = early[2, l, j, 8:24] + heated
            return carry

        lax.fori_loop(0, levels, warm_up, 0)
        first = planes(early)
        first[2] = warm
        substep(first, field_1, heat, wet_rows, 2, 8, 8, 0, 4)
        substep(planes(field_1), field_2, heat, wet_rows, 2, 8, 8, 0, 4)
        substep(planes(field_2), flow_last, heat, wet_rows, 1, 12, 0, 4, 8)
        outs = (out_a, out_b, out_c)
        for l in range(levels):
            for j in range(3):
                for f in range(2):
                    total = early[f, l, j, 12:20] + field_1[f, l, j, 12:20]
                    total = total + field_2[f, l, j, 12:20]
                    outs[j][6 * f + l] = 0.25 * (total + flow_last[f, l, j])
                outs[j][12 + l] = flow_last[2, l, j]
                outs[j][18 + l] = flow_last[3, l, j]

    @pl.when(section != 3)
    def _():
        def driven(i):
            return jnp.where(
                section == 0, from_a[i], jnp.where(section == 1, from_b[i], from_c[i])
            )

        for i in range(18):
            winds[i] = driven(i)
        edge_v = driven(18)
        rows_above = driven(19)
        rows_below = driven(20)
        lane = lanes(8)
        sub = lax.broadcasted_iota(jnp.int32, (8, 128), 0)
        for l in range(levels):
            u, v = winds[l], winds[6 + l]
            winds[18 + l] = jnp.where(sub == 0, roll_rows(rows_above, -l), roll_rows(u, 1))
            winds[24 + l] = jnp.where(sub == 7, roll_rows(rows_below, 7 - l), roll_rows(u, 7))
            winds[30 + l] = jnp.where(
                lane == 127, roll_lanes(edge_v, 126 - 2 * l), roll_lanes(v, 127)
            )
            winds[36 + l] = jnp.where(lane == 0, roll_lanes(edge_v, -2 * l), roll_lanes(v, 1))
            winds[42 + l] = side_columns(section, from_a[12 + l], from_c[12 + l])
        floor = wet_rows[section, 8:16]

        def level(l, carry):
            weights = tracer_weights(
                winds[18 + l], winds[24 + l], winds[30 + l], winds[36 + l], winds[12 + l], floor > l
            )
            results = tracer_level(
                [tracers_next[a, l, 4:12] for a in range(nt)],
                [tracers_next[a, l, 3:11] for a in range(nt)],
                [tracers_next[a, l, 5:13] for a in range(nt)],
                winds[42 + l], weights, reaction,
            )
            for a in range(nt):
                tracers_last[a, l] = results[a]
            shade = pigment_of(results[0], results[1])
            for out in (out_a, out_b, out_c):
                out[l] = shade
                for i in range(1, 4):
                    out[6 * i + l] = jnp.zeros((8, 128), F32)
            return carry

        lax.fori_loop(0, levels, level, 0)


def store_kernel(flow_last, tracers_last, flow_out, tracers_out, blank, sems):
    section, _, _ = place()
    blank[...] = jnp.zeros_like(blank)

    def put(flow_of, tracers_from):
        copies = [pltpu.make_async_copy(tracers_from, tracers_out, sems.at[3])]
        for j in range(3):
            target = flow_out.at[:, :, :, 128 * j : 128 * j + 128]
            copies.append(pltpu.make_async_copy(flow_of(j), target, sems.at[j]))
        for copy in copies:
            copy.start()
        for copy in copies:
            copy.wait()

    @pl.when(section == 3)
    def _():
        put(lambda j: flow_last.at[:, :, j], blank)

    @pl.when(section != 3)
    def _():
        put(lambda j: blank.at[0:4], tracers_last)


def last_kernel(from_a, from_b, from_c, light_out, forcing_out):
    section, _, _ = place()
    levels = light_out.shape[0]
    is_dynamics = section == 3
    for l in range(levels):
        for j, shade in enumerate((from_c, from_b, from_a)):
            light_out[l, :, 128 * j : 128 * j + 128] = jnp.where(is_dynamics, shade[l], 0.0)
        for f in range(4):
            i = 6 * f + l
            picked = jnp.where(
                section == 0, from_a[i], jnp.where(section == 1, from_b[i], from_c[i])
            )
            forcing_out[f, l] = jnp.where(is_dynamics, 0.0, picked)


def call(kernel, shapes, operands, spaces, scratch=(), out_space=pltpu.VMEM):
    operands = [
        pltpu.with_memory_space_constraint(x, pltpu.HBM) if space == pltpu.HBM else x
        for x, space in zip(operands, spaces)
    ]
    return pl.pallas_call(
        kernel,
        out_shape=[jax.ShapeDtypeStruct(shape, dtype) for shape, dtype in shapes],
        in_specs=[pl.BlockSpec(memory_space=space) for space in spaces],
        out_specs=[pl.BlockSpec(memory_space=out_space) for _ in shapes],
        scratch_shapes=list(scratch),
        compiler_params=pltpu.CompilerParams(vmem_limit_bytes=VMEM_LIMIT),
    )(*operands)


def route(target):
    total = lax.axis_size("comp") * lax.axis_size("gy") * lax.axis_size("gx")
    group = total // SECTIONS
    pairs = []
    for moved in range(total):
        section, strip = target(moved // group, moved % group, group)
        pairs.append(((moved - 1) % total, (section * group + strip - 1) % total))
    return pairs


def across(value, by):
    return lax.ppermute(value, AXES, route(lambda k, s, g: ((k + by) % SECTIONS, s)))


def opposite(value):
    def target(k, s, g):
        if k % 2 == 1:
            return (k + 2) % SECTIONS, s
        if s in (0, g - 1):
            return k, g - 1 - s
        return k, s + 1 if s % 2 == 1 else s - 1

    return lax.ppermute(value, AXES, route(target))


def along(value, by):
    return lax.ppermute(value, AXES, route(lambda k, s, g: divmod((k * g + s + by) % (SECTIONS * g), g)))


def on_device(flow_fields, chlorophyll_lag, tracers, forcing, ocean_mask, bottom, reaction):
    levels = chlorophyll_lag.shape[0]
    nt = tracers.shape[0]
    breadth = flow_fields.shape[3]
    vmem, smem, hbm = pltpu.VMEM, pltpu.SMEM, pltpu.HBM
    message = (15, levels, 8, 128)
    to_next, to_prev, flow, pigment, tracers, forcing, wet_rows = call(
        load_kernel,
        [
            (message, F32), (message, F32),
            ((4, levels, 3, 8, 128), F32), ((levels, 3, 8, 128), F32),
            (tracers.shape, F32), (forcing.shape, F32), ((3, 24, 128), jnp.int32),
        ],
        (flow_fields, chlorophyll_lag, tracers, forcing, ocean_mask, bottom),
        (hbm,) * 6,
        (
            pltpu.VMEM((3, 8, breadth), jnp.int32),
            pltpu.VMEM((3, 8, breadth), jnp.int32),
            pltpu.SemaphoreType.DMA((6,)),
            pltpu.SemaphoreType.DMA((2 * levels,)),
        ),
    )
    above = along(to_next, 1)
    below = along(to_prev, -1)
    cells, winds, border = call(
        gather_kernel,
        [((nt, levels, 32, 128), F32), ((3, levels, 32, 128), F32), ((levels, 16, 128), F32)],
        (tracers, forcing, above, below),
        (vmem,) * 4,
    )
    from_left = across(border, 1)
    from_right = across(border, -1)
    exchange = ((21, 8, 128), F32)
    *sends, flow_next, partial = call(
        first_kernel,
        [
            exchange, exchange, exchange,
            ((4, levels, 3, 32, 128), F32), ((nt, levels, 16, 128), F32),
        ],
        (flow, pigment, above, below, cells, winds, wet_rows, reaction),
        (vmem,) * 7 + (smem,),
        (
            *[pltpu.VMEM((4, levels, 3, 40, 128), F32) for _ in range(4)],
            pltpu.VMEM((levels, 3, 24, 128), F32),
        ),
    )
    *sent, tracers_next = call(
        sides_kernel,
        [exchange, exchange, exchange, ((nt, levels, 16, 128), F32)],
        (from_left, from_right, *sends, partial, wet_rows),
        (vmem,) * 7,
    )
    from_b = opposite(sent[1])
    from_a = across(sent[0], 1)
    from_c = across(sent[2], -1)
    (early,) = call(
        early_kernel,
        [((4, levels, 3, 32, 128), F32)],
        (flow_next, wet_rows),
        (vmem, vmem),
    )
    exchange = ((24, 8, 128), F32)
    last = call(
        second_kernel,
        [
            exchange, exchange, exchange,
            ((4, levels, 3, 8, 128), F32), ((nt, levels, 8, 128), F32),
        ],
        (from_a, from_b, from_c, early, tracers_next, wet_rows, reaction),
        (vmem,) * 6 + (smem,),
        (
            pltpu.VMEM((levels, 3, 32, 128), F32),
            *[pltpu.VMEM((4, levels, 3, 32, 128), F32) for _ in range(2)],
            pltpu.VMEM((levels, 3, 16, 128), F32),
            pltpu.VMEM((48, 8, 128), F32),
        ),
    )
    final_b = opposite(last[1])
    final_a = across(last[0], 1)
    final_c = across(last[2], -1)
    flow_out, tracers_out = call(
        store_kernel,
        [(flow_fields.shape, F32), (tracers.shape, F32)],
        (last[3], last[4]),
        (vmem, vmem),
        (pltpu.VMEM(tracers.shape, F32), pltpu.SemaphoreType.DMA((4,))),
        hbm,
    )
    light_out, forcing_out = call(
        last_kernel,
        [((levels, 8, breadth), F32), ((4, levels, 8, 128), F32)],
        (final_a, final_b, final_c),
        (vmem,) * 3,
    )
    return flow_out, light_out, tracers_out, forcing_out


def solution(mesh):
    rows = P(None, None, AXES, None)
    light = P(None, AXES, None)
    return jax.shard_map(
        on_device,
        mesh=mesh,
        in_specs=(rows, light, rows, rows, P(), P(), P()),
        out_specs=(rows, light, rows, rows),
        check_vma=False,
    )
```

```python
import jax
import jax.numpy as jnp
from jax import lax
from jax.experimental import pallas as pl
from jax.experimental.pallas import tpu as pltpu
from jax.sharding import PartitionSpec as P

AXES = ("comp", "gy", "gx")
SECTIONS = 4
SHARED = 10
DT = 0.1
F32 = jnp.float32
UNROLL = 2
VMEM_LIMIT = 48 * 1024 * 1024


def place():
    gy = lax.axis_size("gy")
    gx = lax.axis_size("gx")
    total = lax.axis_size("comp") * gy * gx
    group = total // SECTIONS
    position = (lax.axis_index("comp") * gy + lax.axis_index("gy")) * gx + lax.axis_index("gx")
    moved = lax.rem(position + 1, total)
    return moved // group, lax.rem(moved, group), group


def lanes(rows):
    return lax.broadcasted_iota(jnp.int32, (rows, 128), 1)


def roll_lanes(x, by):
    by = by % 128
    return x if by == 0 else pltpu.roll(x, by, 1)


def swap(x):
    return pltpu.roll(x, 4, 0)


def upper_half():
    return lax.broadcasted_iota(jnp.int32, (8, 128), 0) < 4


def spread(flag):
    return jnp.where(flag, 1.0, 0.0).astype(F32)


def edge_tile(planes):
    pair = lanes(planes[0].shape[0]) // 2
    edges = jnp.zeros_like(planes[0])
    for a, x in enumerate(planes):
        edges = jnp.where(pair == a, roll_lanes(x, 2 * a + 1), edges)
    return edges


def pack_rows(tracers, forcing, to_next, to_prev, copies):
    half = upper_half()
    nt, levels = tracers.shape[0], tracers.shape[1]

    def put(plane, pair, even, odd):
        row, col = plane // 2, 3 * (plane % 2)
        to_next[row, col + pair] = jnp.where(half, swap(even), odd)
        to_prev[row, col + pair] = jnp.where(half, even, swap(odd))

    for pair in range(levels // 2):
        even, odd = 2 * pair, 2 * pair + 1
        for copy in copies[4 * pair : 4 * pair + 4]:
            copy.wait()
        for a in range(nt):
            put(a, pair, tracers[a, even], tracers[a, odd])
        put(nt, pair, forcing[0, even], forcing[0, odd])
        put(nt + 1, pair, forcing[1, even], forcing[1, odd])
        growth = [jnp.exp(0.1 * forcing[2, l] - 0.05 * forcing[3, l]) for l in (even, odd)]
        put(nt + 2, pair, growth[0], growth[1])
        put(nt + 3, pair, jnp.zeros((8, 128), F32), jnp.zeros((8, 128), F32))


def load_kernel(
    flow, pigment, tracers, forcing,
    to_next, to_prev, more_next, more_prev, flow_in, pigment_in, tracers_in, forcing_in, sems,
):
    section, _, _ = place()
    levels = pigment.shape[0]

    @pl.when(section == 3)
    def _():
        copies = []
        for j in range(3):
            cols = slice(128 * j, 128 * j + 128)
            copies.append(
                pltpu.make_async_copy(flow.at[:, :, :, cols], flow_in.at[:, :, j], sems.at[j])
            )
            copies.append(
                pltpu.make_async_copy(pigment.at[:, :, cols], pigment_in.at[:, j], sems.at[3 + j])
            )
        for copy in copies:
            copy.start()
        for copy in copies:
            copy.wait()

        def level(l, carry):
            for f in range(5):
                for j in range(3):
                    tile = flow_in[f, l, j] if f < 4 else pigment_in[l, j]
                    row = 3 * f + j
                    if row < SHARED:
                        to_next[row, l] = tile
                        to_prev[row, l] = tile
                    else:
                        more_next[row - SHARED, l] = tile
                        more_prev[row - SHARED, l] = tile
            return carry

        lax.fori_loop(0, levels, level, 0)

    @pl.when(section != 3)
    def _():
        copies = []
        for l in range(levels):
            copies.append(
                pltpu.make_async_copy(tracers.at[:, l], tracers_in.at[:, l], sems.at[l])
            )
            copies.append(
                pltpu.make_async_copy(forcing.at[:, l], forcing_in.at[:, l], sems.at[levels + l])
            )
        for copy in copies:
            copy.start()
        pack_rows(tracers_in, forcing_in, to_next, to_prev, copies)
        more_next[...] = jnp.zeros_like(more_next)
        more_prev[...] = jnp.zeros_like(more_prev)


def mask_kernel(ocean, bottom, wet_rows, ocean_rows, bottom_rows, mask_sems):
    _, strip, group = place()
    starts = [jnp.maximum(strip - 1, 0), strip, jnp.minimum(strip + 1, group - 1)]
    masks = []
    for i, start in enumerate(starts):
        rows = pl.ds(pl.multiple_of(start * 8, 8), 8)
        masks.append(pltpu.make_async_copy(ocean.at[rows], ocean_rows.at[i], mask_sems.at[i]))
        masks.append(pltpu.make_async_copy(bottom.at[rows], bottom_rows.at[i], mask_sems.at[3 + i]))
    for copy in masks:
        copy.start()
    for copy in masks:
        copy.wait()
    inside = [(strip > 0).astype(jnp.int32), 1, (strip < group - 1).astype(jnp.int32)]
    for i in range(3):
        floor = jnp.where(ocean_rows[i] == 1, bottom_rows[i], 0) * inside[i]
        for j in range(3):
            wet_rows[j, 8 * i : 8 * i + 8] = floor[:, 128 * j : 128 * j + 128]


def side_columns(section, from_left, from_right):
    even = lanes(from_left.shape[0]) % 2 == 0
    east = jnp.where(section < 2, roll_lanes(from_right, -1), 0.0)
    west = jnp.where(section > 0, roll_lanes(from_left, 1), 0.0)
    return jnp.where(even, east, west)


def shifted(tiles):
    lane = lanes(tiles[0].shape[0])
    left = [roll_lanes(x, 127) for x in tiles]
    right = [roll_lanes(x, 1) for x in tiles]
    count = len(tiles)
    east = [
        jnp.where(lane == 127, left[j + 1] if j + 1 < count else 0.0, left[j]) for j in range(count)
    ]
    west = [jnp.where(lane == 0, right[j - 1] if j > 0 else 0.0, right[j]) for j in range(count)]
    return east, west


def substep(source, target, heat, wet_rows, tiles, read_at, write_at, heat_at, wet_at):
    levels = target.shape[1]
    thirds = 3
    zero = jnp.zeros((8, 128), F32)

    def level(l, carry):
        slopes = []
        for tile in range(tiles):
            row = read_at + 8 * tile
            put = write_at + 8 * tile
            slope_x, slope_y = carry[tile]

            def load(f, by):
                return [source[f][l, j, row + by : row + by + 8] for j in range(thirds)]

            centre = [load(f, 0) for f in range(4)]
            up = [load(f, -1) for f in range(4)]
            down = [load(f, 1) for f in range(4)]
            sides = [shifted(centre[f]) for f in range(4)]
            new_x, new_y = [], []
            for j in range(thirds):
                u, v, t, s = (centre[f][j] for f in range(4))
                un, vn, tn, sn = (up[f][j] for f in range(4))
                us, vs, ts, ss = (down[f][j] for f in range(4))
                ue, ve, te, se = (sides[f][0][j] for f in range(4))
                uw, vw, tw, sw = (sides[f][1][j] for f in range(4))
                px = slope_x[j] + ((ss - sn) - (ts - tn))
                py = slope_y[j] + ((se - sw) - (te - tw))
                new_x.append(px)
                new_y.append(py)
                is_wet = wet_rows[j, wet_at + 8 * tile : wet_at + 8 * tile + 8] > l
                a = 0.05 - 0.05 * us
                b = 0.05 + 0.05 * un
                c = 0.05 - 0.05 * ve
                d = 0.05 + 0.05 * vw
                kept = 0.8 * t
                if heat is not None:
                    kept = kept + heat[l, j, heat_at + 8 * tile : heat_at + 8 * tile + 8]
                results = (
                    0.79 * u + 0.1 * v - 0.01 * px + 0.05 * ((un + us) + (ue + uw)),
                    0.79 * v - 0.1 * u - 0.01 * py + 0.05 * ((vn + vs) + (ve + vw)),
                    kept + ((ts * a + tn * b) + (te * c + tw * d)),
                    0.8 * s + ((ss * a + sn * b) + (se * c + sw * d)),
                )
                for f in range(4):
                    target[f, l, j, put : put + 8] = jnp.where(is_wet, results[f], 0.0)
            slopes.append((new_x, new_y))
        return slopes

    start = [([zero] * thirds, [zero] * thirds) for _ in range(tiles)]
    lax.fori_loop(0, levels, level, start, unroll=UNROLL)


def fill_heat(load, heat):
    levels, rows = heat.shape[0], heat.shape[2]
    for tile in range(rows // 8):
        for j in range(3):
            optical = jnp.zeros((8, 128), F32)
            light = jnp.ones((8, 128), F32)
            for l in range(levels):
                optical = optical + (0.05 + 0.3 * load(l, tile, j))
                lower = jnp.exp(-optical)
                heat[l, j, 8 * tile : 8 * tile + 8] = (5.0 * DT) * (light - lower)
                light = lower


def extend(own, above, below, half):
    turned = swap(own)
    return jnp.concatenate([jnp.where(half, above, turned), jnp.where(half, turned, below)], axis=0)


def tracer_weights(u_up, u_down, v_east, v_west, growth, is_wet):
    wet = spread(is_wet)
    scale = wet * 0.05
    return (
        scale - scale * u_down,
        scale + scale * u_up,
        scale - scale * v_east,
        scale + scale * v_west,
        wet * 0.8,
        (wet * DT) * growth,
    )


def tracer_level(centre, up, down, sides, weights, reaction):
    nt = len(centre)
    lane = lanes(centre[0].shape[0])
    a, b, c, d, keep, grow = weights
    results = []
    for i in range(nt):
        side = 0.0 if sides is None else roll_lanes(sides, -2 * i - 1)
        east = jnp.where(lane == 127, side, roll_lanes(centre[i], 127))
        west = jnp.where(lane == 0, side, roll_lanes(centre[i], 1))
        mixed = reaction[i, 0] * centre[0]
        for k in range(1, nt):
            mixed = mixed + reaction[i, k] * centre[k]
        results.append(
            (keep * centre[i] + grow * mixed)
            + ((down[i] * a + up[i] * b) + (east * c + west * d))
        )
    return results


def pigment_of(first, second):
    return 0.25 * (first * first + second * second)


def gather_kernel(tracers, forcing, above, below, wet_rows, cells, winds, border):
    section, strip, group = place()
    nt, levels = tracers.shape[0], tracers.shape[1]
    low = spread(strip > 0)
    high = spread(strip < group - 1)

    @pl.when(section == 3)
    def _():
        border[...] = jnp.zeros_like(border)

    @pl.when(section != 3)
    def _():
        half = upper_half()

        def halo(message, plane, pair, odd, upward):
            tile = message[plane // 2, 3 * (plane % 2) + pair]
            return swap(tile) if odd != upward else tile

        def build(plane, own, l, masked):
            pair, odd = l // 2, l % 2 == 1
            up = halo(above, plane, pair, odd, False)
            down = halo(below, plane, pair, not odd, False)
            if masked:
                up, down = up * low, down * high
            return extend(own, up, down, half)

        lane = lanes(16)
        for l in range(levels):
            v = build(nt + 1, forcing[1, l], l, False)
            scale = 0.05 + jnp.where(lane == 0, -0.05, 0.05) * v
            products = []
            for a in range(nt):
                cell = build(a, tracers[a, l], l, True)
                cells[a, l, 8:24] = cell
                products.append(scale * cell)
            winds[0, l, 8:24] = build(nt, forcing[0, l], l, False)
            winds[1, l, 8:24] = v
            growth = jnp.exp(0.1 * forcing[2, l] - 0.05 * forcing[3, l])
            winds[2, l, 8:24] = build(nt + 2, growth, l, False)
            border[l] = edge_tile(products)


def first_kernel(
    flow, pigment, above, below, more_above, more_below, cells, winds, wet_rows, reaction,
    send_a, send_b, send_c, flow_next, partial, rim_edges, rim_wet,
    field_0, field_1, field_2, field_3, heat,
):
    section, strip, group = place()
    levels = pigment.shape[0]
    nt = cells.shape[0]
    low = spread(strip > 0)
    high = spread(strip < group - 1)

    @pl.when(section == 3)
    def _():
        def over(row, l):
            return above[row, l] if row < SHARED else more_above[row - SHARED, l]

        def under(row, l):
            return below[row, l] if row < SHARED else more_below[row - SHARED, l]

        def fill(l, carry):
            for f in range(4):
                for j in range(3):
                    field_0[f, l, j, 8:16] = over(3 * f + j, l) * low
                    field_0[f, l, j, 16:24] = flow[f, l, j]
                    field_0[f, l, j, 24:32] = under(3 * f + j, l) * high
            return carry

        lax.fori_loop(0, levels, fill, 0)

        def load(l, tile, j):
            if tile == 1:
                return pigment[l, j]
            return (over if tile == 0 else under)(12 + j, l)

        fill_heat(load, heat)
        substep(planes(field_0), field_1, heat, wet_rows, 3, 8, 8, 0, 0)
        substep(planes(field_1), field_2, heat, wet_rows, 3, 8, 8, 0, 0)
        substep(planes(field_2), field_3, heat, wet_rows, 3, 8, 8, 0, 0)
        substep(planes(field_3), flow_next, heat, wet_rows, 2, 12, 8, 4, 4)
        lane = lanes(8)
        outs = (send_a, send_b, send_c)
        sub = lax.broadcasted_iota(jnp.int32, (8, 128), 0)

        def mean(f, l, row, j):
            total = field_1[f, l, j, row : row + 8] + field_2[f, l, j, row : row + 8]
            total = total + field_3[f, l, j, row : row + 8]
            return 0.25 * (total + flow_next[f, l, j, row - 4 : row + 4])

        edge_v = [jnp.zeros((8, 128), F32) for _ in range(3)]
        rows_above = [jnp.zeros((8, 128), F32) for _ in range(3)]
        rows_below = [jnp.zeros((8, 128), F32) for _ in range(3)]
        for l in range(levels):
            v_mean = []
            for j in range(3):
                outs[j][l] = mean(0, l, 16, j)
                v_mean.append(mean(1, l, 16, j))
                outs[j][6 + l] = v_mean[j]
                warm = flow_next[2, l, j, 12:20]
                salt = flow_next[3, l, j, 12:20]
                outs[j][12 + l] = jnp.exp(0.1 * warm - 0.05 * salt)
                first = mean(0, l, 15, j)
                last = mean(0, l, 17, j)
                rows_above[j] = jnp.where(sub == l, roll_rows(first, l), rows_above[j])
                rows_below[j] = jnp.where(sub == l, roll_rows(last, l + 1), rows_below[j])
            for j in range(3):
                if j > 0:
                    edge_v[j] = jnp.where(
                        lane == 2 * l, roll_lanes(v_mean[j - 1], 2 * l + 1), edge_v[j]
                    )
                if j < 2:
                    edge_v[j] = jnp.where(
                        lane == 2 * l + 1, roll_lanes(v_mean[j + 1], 2 * l + 1), edge_v[j]
                    )
        for j in range(3):
            outs[j][18] = edge_v[j]
            outs[j][19] = rows_above[j]
            outs[j][20] = rows_below[j]

    @pl.when(section != 3)
    def _():
        floor = wet_rows[section, 4:20]

        def level(l, carry):
            v = winds[1, l, 8:24]
            weights = tracer_weights(
                winds[0, l, 7:23], winds[0, l, 9:25], roll_lanes(v, 127), roll_lanes(v, 1),
                winds[2, l, 8:24], floor > l,
            )
            results = tracer_level(
                [cells[a, l, 8:24] for a in range(nt)],
                [cells[a, l, 7:23] for a in range(nt)],
                [cells[a, l, 9:25] for a in range(nt)],
                None, weights, reaction,
            )
            for a in range(nt):
                partial[a, l] = results[a]
            rim_edges[l] = edge_tile([partial[a, l, 4:12] for a in range(nt)])
            wet = spread(wet_rows[section, 8:16] > l)
            first = jnp.broadcast_to(wet[:, :1], (8, 128))
            last = jnp.broadcast_to(wet[:, 127:], (8, 128))
            rim_wet[l] = jnp.where(lanes(8) % 2 == 0, last, first)
            return carry

        lax.fori_loop(0, levels, level, 0)


def sides_kernel(
    from_left, from_right, send_a, send_b, send_c, partial, rim_edges, rim_wet, wet_rows,
    out_a, out_b, out_c,
):
    section, _, _ = place()
    levels = partial.shape[1]
    outs = (out_a, out_b, out_c)

    @pl.when(section == 3)
    def _():
        for out, send in zip(outs, (send_a, send_b, send_c)):
            out[...] = send[...]

    @pl.when(section != 3)
    def _():
        floor = wet_rows[section, 4:20]
        lane = lanes(16)
        rim = (lane == 0) | (lane == 127)
        row = lax.broadcasted_iota(jnp.int32, (16, 128), 0)
        inside = (row > 0) & (row < 15)
        for l in range(levels):
            sides = side_columns(section, from_left[l], from_right[l])
            wet_rim = rim & (floor > l)
            pair = [
                partial[a, l] + jnp.where(wet_rim, roll_lanes(sides, -2 * a - 1), 0.0)
                for a in range(2)
            ]
            own = side_columns(section, from_left[l, 4:12], from_right[l, 4:12])
            edge = rim_edges[l] + jnp.where(rim_wet[l] > 0.0, own, 0.0)
            shade = jnp.where(inside, pigment_of(pair[0], pair[1]), 0.0)
            for out in outs:
                out[2 * l] = shade[:8]
                out[2 * l + 1] = shade[8:]
                out[12 + l] = edge
        for out in outs:
            for i in range(18, 21):
                out[i] = jnp.zeros((8, 128), F32)


def roll_rows(x, by):
    by = by % 8
    return x if by == 0 else pltpu.roll(x, by, 0)


def planes(buffer):
    return [buffer.at[f] for f in range(4)]


def early_kernel(flow_next, wet_rows, partial, from_left, from_right, early, tracers_next):
    section, _, _ = place()
    nt, levels = partial.shape[0], partial.shape[1]

    @pl.when(section != 3)
    def _():
        floor = wet_rows[section, 4:20]
        lane = lanes(16)
        rim = (lane == 0) | (lane == 127)

        def level(l, carry):
            sides = side_columns(section, from_left[l], from_right[l])
            wet_rim = rim & (floor > l)
            for a in range(nt):
                side = jnp.where(wet_rim, roll_lanes(sides, -2 * a - 1), 0.0)
                tracers_next[a, l] = partial[a, l] + side
            return carry

        lax.fori_loop(0, levels, level, 0, unroll=2)

    @pl.when(section == 3)
    def _():
        substep(planes(flow_next), early, None, wet_rows, 2, 8, 8, 0, 4)


def second_kernel(
    from_b, from_a, from_c, early, tracers_next, wet_rows, reaction,
    out_a, out_b, out_c, flow_last, tracers_last, warm, field_1, field_2, heat, winds,
):
    section, _, _ = place()
    levels = heat.shape[0]
    nt = tracers_next.shape[0]

    @pl.when(section == 3)
    def _():
        shades = (from_c, from_b, from_a)

        def load(l, tile, j):
            return shades[j][2 * l + tile]

        fill_heat(load, heat)

        def warm_up(l, carry):
            for j in range(3):
                heated = jnp.where(wet_rows[j, 4:20] > l, heat[l, j], 0.0)
                warm[l, j, 8:24] = early[2, l, j, 8:24] + heated
            return carry

        lax.fori_loop(0, levels, warm_up, 0)
        first = planes(early)
        first[2] = warm
        substep(first, field_1, heat, wet_rows, 2, 8, 8, 0, 4)
        substep(planes(field_1), field_2, heat, wet_rows, 2, 8, 8, 0, 4)
        substep(planes(field_2), flow_last, heat, wet_rows, 1, 12, 0, 4, 8)
        outs = (out_a, out_b, out_c)
        for l in range(levels):
            for j in range(3):
                for f in range(2):
                    total = early[f, l, j, 12:20] + field_1[f, l, j, 12:20]
                    total = total + field_2[f, l, j, 12:20]
                    outs[j][6 * f + l] = 0.25 * (total + flow_last[f, l, j])
                outs[j][12 + l] = flow_last[2, l, j]
                outs[j][18 + l] = flow_last[3, l, j]

    @pl.when(section != 3)
    def _():
        def driven(i):
            return jnp.where(
                section == 0, from_a[i], jnp.where(section == 1, from_b[i], from_c[i])
            )

        for i in range(18):
            winds[i] = driven(i)
        edge_v = driven(18)
        rows_above = driven(19)
        rows_below = driven(20)
        lane = lanes(8)
        sub = lax.broadcasted_iota(jnp.int32, (8, 128), 0)
        for l in range(levels):
            u, v = winds[l], winds[6 + l]
            winds[18 + l] = jnp.where(sub == 0, roll_rows(rows_above, -l), roll_rows(u, 1))
            winds[24 + l] = jnp.where(sub == 7, roll_rows(rows_below, 7 - l), roll_rows(u, 7))
            winds[30 + l] = jnp.where(
                lane == 127, roll_lanes(edge_v, 126 - 2 * l), roll_lanes(v, 127)
            )
            winds[36 + l] = jnp.where(lane == 0, roll_lanes(edge_v, -2 * l), roll_lanes(v, 1))
            winds[42 + l] = side_columns(section, from_a[12 + l], from_c[12 + l])
        floor = wet_rows[section, 8:16]

        def level(l, carry):
            weights = tracer_weights(
                winds[18 + l], winds[24 + l], winds[30 + l], winds[36 + l], winds[12 + l], floor > l
            )
            results = tracer_level(
                [tracers_next[a, l, 4:12] for a in range(nt)],
                [tracers_next[a, l, 3:11] for a in range(nt)],
                [tracers_next[a, l, 5:13] for a in range(nt)],
                winds[42 + l], weights, reaction,
            )
            for a in range(nt):
                tracers_last[a, l] = results[a]
            shade = pigment_of(results[0], results[1])
            for out in (out_a, out_b, out_c):
                out[l] = shade
                for i in range(1, 4):
                    out[6 * i + l] = jnp.zeros((8, 128), F32)
            return carry

        lax.fori_loop(0, levels, level, 0)


def store_kernel(flow_last, tracers_last, flow_out, tracers_out, blank, sems):
    section, _, _ = place()
    blank[...] = jnp.zeros_like(blank)

    def put(flow_of, tracers_from):
        copies = [pltpu.make_async_copy(tracers_from, tracers_out, sems.at[3])]
        for j in range(3):
            target = flow_out.at[:, :, :, 128 * j : 128 * j + 128]
            copies.append(pltpu.make_async_copy(flow_of(j), target, sems.at[j]))
        for copy in copies:
            copy.start()
        for copy in copies:
            copy.wait()

    @pl.when(section == 3)
    def _():
        put(lambda j: flow_last.at[:, :, j], blank)

    @pl.when(section != 3)
    def _():
        put(lambda j: blank.at[0:4], tracers_last)


def last_kernel(from_b, from_a, from_c, light_out, forcing_out):
    section, _, _ = place()
    levels = light_out.shape[0]
    is_dynamics = section == 3
    for l in range(levels):
        for j, shade in enumerate((from_c, from_b, from_a)):
            light_out[l, :, 128 * j : 128 * j + 128] = jnp.where(is_dynamics, shade[l], 0.0)
        for f in range(4):
            i = 6 * f + l
            picked = jnp.where(
                section == 0, from_a[i], jnp.where(section == 1, from_b[i], from_c[i])
            )
            forcing_out[f, l] = jnp.where(is_dynamics, 0.0, picked)


def call(kernel, shapes, operands, spaces, scratch=(), out_space=pltpu.VMEM):
    operands = [
        pltpu.with_memory_space_constraint(x, pltpu.HBM) if space == pltpu.HBM else x
        for x, space in zip(operands, spaces)
    ]
    return pl.pallas_call(
        kernel,
        out_shape=[jax.ShapeDtypeStruct(shape, dtype) for shape, dtype in shapes],
        in_specs=[pl.BlockSpec(memory_space=space) for space in spaces],
        out_specs=[pl.BlockSpec(memory_space=out_space) for _ in shapes],
        scratch_shapes=list(scratch),
        compiler_params=pltpu.CompilerParams(vmem_limit_bytes=VMEM_LIMIT),
    )(*operands)


def route(target):
    total = lax.axis_size("comp") * lax.axis_size("gy") * lax.axis_size("gx")
    group = total // SECTIONS
    pairs = []
    for moved in range(total):
        section, strip = target(moved // group, moved % group, group)
        pairs.append(((moved - 1) % total, (section * group + strip - 1) % total))
    return pairs


def across(value, by):
    return lax.ppermute(value, AXES, route(lambda k, s, g: ((k + by) % SECTIONS, s)))


def partner(strip, group):
    if strip in (0, group - 1):
        return group - 1 - strip
    return strip + 1 if strip % 2 == 1 else strip - 1


def opposite(value):
    def target(k, s, g):
        return ((k + 2) % SECTIONS, s) if k % 2 == 1 else (k, partner(s, g))

    return lax.ppermute(value, AXES, route(target))


def along_dynamics(value, by):
    def target(k, s, g):
        return (k, (s + by) % g) if k == 3 else (k, partner(s, g))

    return lax.ppermute(value, AXES, route(target))


def beside(value, by):
    def target(k, s, g):
        return ((k + by) % 3, s) if k < 3 else (k, partner(s, g))

    return lax.ppermute(value, AXES, route(target))


def along(value, by):
    return lax.ppermute(value, AXES, route(lambda k, s, g: divmod((k * g + s + by) % (SECTIONS * g), g)))


def on_device(flow_fields, chlorophyll_lag, tracers, forcing, ocean_mask, bottom, reaction):
    levels = chlorophyll_lag.shape[0]
    nt = tracers.shape[0]
    breadth = flow_fields.shape[3]
    vmem, smem, hbm = pltpu.VMEM, pltpu.SMEM, pltpu.HBM
    message = (SHARED, levels, 8, 128)
    more = (15 - SHARED, levels, 8, 128)
    to_next, to_prev, more_next, more_prev, flow, pigment, tracers, forcing = call(
        load_kernel,
        [
            (message, F32), (message, F32), (more, F32), (more, F32),
            ((4, levels, 3, 8, 128), F32), ((levels, 3, 8, 128), F32),
            (tracers.shape, F32), (forcing.shape, F32),
        ],
        (flow_fields, chlorophyll_lag, tracers, forcing),
        (hbm,) * 4,
        (pltpu.SemaphoreType.DMA((2 * levels,)),),
    )
    above = along(to_next, 1)
    below = along(to_prev, -1)
    more_above = along_dynamics(more_next, 1)
    more_below = along_dynamics(more_prev, -1)
    (wet_rows,) = call(
        mask_kernel,
        [((3, 24, 128), jnp.int32)],
        (ocean_mask, bottom),
        (hbm,) * 2,
        (
            pltpu.VMEM((3, 8, breadth), jnp.int32),
            pltpu.VMEM((3, 8, breadth), jnp.int32),
            pltpu.SemaphoreType.DMA((6,)),
        ),
    )
    cells, winds, border = call(
        gather_kernel,
        [((nt, levels, 32, 128), F32), ((3, levels, 32, 128), F32), ((levels, 16, 128), F32)],
        (tracers, forcing, above, below, wet_rows),
        (vmem,) * 5,
    )
    from_left = beside(border, 1)
    from_right = beside(border, -1)
    exchange = ((21, 8, 128), F32)
    *sends, flow_next, partial, rim_edges, rim_wet = call(
        first_kernel,
        [
            exchange, exchange, exchange,
            ((4, levels, 3, 32, 128), F32), ((nt, levels, 16, 128), F32),
            ((levels, 8, 128), F32), ((levels, 8, 128), F32),
        ],
        (
            flow, pigment, above, below, more_above, more_below, cells, winds, wet_rows,
            reaction,
        ),
        (vmem,) * 9 + (smem,),
        (
            *[pltpu.VMEM((4, levels, 3, 40, 128), F32) for _ in range(4)],
            pltpu.VMEM((levels, 3, 24, 128), F32),
        ),
    )
    sent = call(
        sides_kernel,
        [exchange, exchange, exchange],
        (from_left, from_right, *sends, partial, rim_edges, rim_wet, wet_rows),
        (vmem,) * 9,
    )
    from_b = opposite(sent[1])
    from_a = across(sent[0], 1)
    from_c = across(sent[2], -1)
    early, tracers_next = call(
        early_kernel,
        [((4, levels, 3, 32, 128), F32), ((nt, levels, 16, 128), F32)],
        (flow_next, wet_rows, partial, from_left, from_right),
        (vmem,) * 5,
    )
    exchange = ((24, 8, 128), F32)
    last = call(
        second_kernel,
        [
            exchange, exchange, exchange,
            ((4, levels, 3, 8, 128), F32), ((nt, levels, 8, 128), F32),
        ],
        (from_b, from_a, from_c, early, tracers_next, wet_rows, reaction),
        (vmem,) * 6 + (smem,),
        (
            pltpu.VMEM((levels, 3, 32, 128), F32),
            *[pltpu.VMEM((4, levels, 3, 32, 128), F32) for _ in range(2)],
            pltpu.VMEM((levels, 3, 16, 128), F32),
            pltpu.VMEM((48, 8, 128), F32),
        ),
    )
    final_b = opposite(last[1])
    final_a = across(last[0], 1)
    final_c = across(last[2], -1)
    flow_out, tracers_out = call(
        store_kernel,
        [(flow_fields.shape, F32), (tracers.shape, F32)],
        (last[3], last[4]),
        (vmem, vmem),
        (pltpu.VMEM(tracers.shape, F32), pltpu.SemaphoreType.DMA((4,))),
        hbm,
    )
    light_out, forcing_out = call(
        last_kernel,
        [((levels, 8, breadth), F32), ((4, levels, 8, 128), F32)],
        (final_b, final_a, final_c),
        (vmem,) * 3,
    )
    return flow_out, light_out, tracers_out, forcing_out


def solution(mesh):
    rows = P(None, None, AXES, None)
    light = P(None, AXES, None)
    return jax.shard_map(
        on_device,
        mesh=mesh,
        in_specs=(rows, light, rows, rows, P(), P(), P()),
        out_specs=(rows, light, rows, rows),
        check_vma=False,
    )
```

```python
import jax
import jax.numpy as jnp
from jax import lax
from jax.experimental import pallas as pl
from jax.experimental.pallas import tpu as pltpu
from jax.sharding import PartitionSpec as P

AXES = ("comp", "gy", "gx")
SECTIONS = 4
SHARED = 10
DT = 0.1
F32 = jnp.float32
UNROLL = 2
VMEM_LIMIT = 48 * 1024 * 1024


def place():
    gy = lax.axis_size("gy")
    gx = lax.axis_size("gx")
    total = lax.axis_size("comp") * gy * gx
    group = total // SECTIONS
    position = (lax.axis_index("comp") * gy + lax.axis_index("gy")) * gx + lax.axis_index("gx")
    moved = lax.rem(position + 1, total)
    return moved // group, lax.rem(moved, group), group


def lanes(rows):
    return lax.broadcasted_iota(jnp.int32, (rows, 128), 1)


def roll_lanes(x, by):
    by = by % 128
    return x if by == 0 else pltpu.roll(x, by, 1)


def swap(x):
    return pltpu.roll(x, 4, 0)


def upper_half():
    return lax.broadcasted_iota(jnp.int32, (8, 128), 0) < 4


def spread(flag):
    return jnp.where(flag, 1.0, 0.0).astype(F32)


def edge_tile(planes):
    pair = lanes(planes[0].shape[0]) // 2
    edges = jnp.zeros_like(planes[0])
    for a, x in enumerate(planes):
        edges = jnp.where(pair == a, roll_lanes(x, 2 * a + 1), edges)
    return edges


def pack_rows(tracers, forcing, to_next, to_prev, copies):
    half = upper_half()
    nt, levels = tracers.shape[0], tracers.shape[1]

    def put(plane, pair, even, odd):
        row, col = plane // 2, 3 * (plane % 2)
        to_next[row, col + pair] = jnp.where(half, swap(even), odd)
        to_prev[row, col + pair] = jnp.where(half, even, swap(odd))

    for pair in range(levels // 2):
        even, odd = 2 * pair, 2 * pair + 1
        for copy in copies[4 * pair : 4 * pair + 4]:
            copy.wait()
        for a in range(nt):
            put(a, pair, tracers[a, even], tracers[a, odd])
        put(nt, pair, forcing[0, even], forcing[0, odd])
        put(nt + 1, pair, forcing[1, even], forcing[1, odd])
        growth = [jnp.exp(0.1 * forcing[2, l] - 0.05 * forcing[3, l]) for l in (even, odd)]
        put(nt + 2, pair, growth[0], growth[1])
        put(nt + 3, pair, jnp.zeros((8, 128), F32), jnp.zeros((8, 128), F32))


def load_kernel(
    flow, pigment, tracers, forcing,
    to_next, to_prev, more_next, more_prev, flow_in, pigment_in, tracers_in, forcing_in, sems,
):
    section, _, _ = place()
    levels = pigment.shape[0]

    @pl.when(section == 3)
    def _():
        copies = []
        for j in range(3):
            cols = slice(128 * j, 128 * j + 128)
            copies.append(
                pltpu.make_async_copy(flow.at[:, :, :, cols], flow_in.at[:, :, j], sems.at[j])
            )
            copies.append(
                pltpu.make_async_copy(pigment.at[:, :, cols], pigment_in.at[:, j], sems.at[3 + j])
            )
        for copy in copies:
            copy.start()
        for copy in copies:
            copy.wait()

        def level(l, carry):
            for f in range(5):
                for j in range(3):
                    tile = flow_in[f, l, j] if f < 4 else pigment_in[l, j]
                    row = 3 * f + j
                    if row < SHARED:
                        to_next[row, l] = tile
                        to_prev[row, l] = tile
                    else:
                        more_next[row - SHARED, l] = tile
                        more_prev[row - SHARED, l] = tile
            return carry

        lax.fori_loop(0, levels, level, 0)

    @pl.when(section != 3)
    def _():
        copies = []
        for l in range(levels):
            copies.append(
                pltpu.make_async_copy(tracers.at[:, l], tracers_in.at[:, l], sems.at[l])
            )
            copies.append(
                pltpu.make_async_copy(forcing.at[:, l], forcing_in.at[:, l], sems.at[levels + l])
            )
        for copy in copies:
            copy.start()
        pack_rows(tracers_in, forcing_in, to_next, to_prev, copies)
        more_next[...] = jnp.zeros_like(more_next)
        more_prev[...] = jnp.zeros_like(more_prev)


def mask_kernel(ocean, bottom, wet_rows, ocean_rows, bottom_rows, mask_sems):
    _, strip, group = place()
    starts = [jnp.maximum(strip - 1, 0), strip, jnp.minimum(strip + 1, group - 1)]
    masks = []
    for i, start in enumerate(starts):
        rows = pl.ds(pl.multiple_of(start * 8, 8), 8)
        masks.append(pltpu.make_async_copy(ocean.at[rows], ocean_rows.at[i], mask_sems.at[i]))
        masks.append(pltpu.make_async_copy(bottom.at[rows], bottom_rows.at[i], mask_sems.at[3 + i]))
    for copy in masks:
        copy.start()
    for copy in masks:
        copy.wait()
    inside = [(strip > 0).astype(jnp.int32), 1, (strip < group - 1).astype(jnp.int32)]
    for i in range(3):
        floor = jnp.where(ocean_rows[i] == 1, bottom_rows[i], 0) * inside[i]
        for j in range(3):
            wet_rows[j, 8 * i : 8 * i + 8] = floor[:, 128 * j : 128 * j + 128]


def side_columns(section, inner, outer):
    even = lanes(inner.shape[0]) % 2 == 0
    east = roll_lanes(jnp.where(section == 0, inner, outer), -1)
    west = roll_lanes(jnp.where(section == 1, inner, outer), 1)
    east = jnp.where(section < 2, east, 0.0)
    west = jnp.where(section > 0, west, 0.0)
    return jnp.where(even, east, west)


def shifted(tiles):
    lane = lanes(tiles[0].shape[0])
    left = [roll_lanes(x, 127) for x in tiles]
    right = [roll_lanes(x, 1) for x in tiles]
    count = len(tiles)
    east = [
        jnp.where(lane == 127, left[j + 1] if j + 1 < count else 0.0, left[j]) for j in range(count)
    ]
    west = [jnp.where(lane == 0, right[j - 1] if j > 0 else 0.0, right[j]) for j in range(count)]
    return east, west


def substep(source, target, heat, wet_rows, tiles, read_at, write_at, heat_at, wet_at):
    levels = target.shape[1]
    thirds = 3
    zero = jnp.zeros((8, 128), F32)

    def level(l, carry):
        slopes = []
        for tile in range(tiles):
            row = read_at + 8 * tile
            put = write_at + 8 * tile
            slope_x, slope_y = carry[tile]

            def load(f, by):
                return [source[f][l, j, row + by : row + by + 8] for j in range(thirds)]

            centre = [load(f, 0) for f in range(4)]
            up = [load(f, -1) for f in range(4)]
            down = [load(f, 1) for f in range(4)]
            sides = [shifted(centre[f]) for f in range(4)]
            new_x, new_y = [], []
            for j in range(thirds):
                u, v, t, s = (centre[f][j] for f in range(4))
                un, vn, tn, sn = (up[f][j] for f in range(4))
                us, vs, ts, ss = (down[f][j] for f in range(4))
                ue, ve, te, se = (sides[f][0][j] for f in range(4))
                uw, vw, tw, sw = (sides[f][1][j] for f in range(4))
                px = slope_x[j] + ((ss - sn) - (ts - tn))
                py = slope_y[j] + ((se - sw) - (te - tw))
                new_x.append(px)
                new_y.append(py)
                is_wet = wet_rows[j, wet_at + 8 * tile : wet_at + 8 * tile + 8] > l
                a = 0.05 - 0.05 * us
                b = 0.05 + 0.05 * un
                c = 0.05 - 0.05 * ve
                d = 0.05 + 0.05 * vw
                kept = 0.8 * t
                if heat is not None:
                    kept = kept + heat[l, j, heat_at + 8 * tile : heat_at + 8 * tile + 8]
                results = (
                    0.79 * u + 0.1 * v - 0.01 * px + 0.05 * ((un + us) + (ue + uw)),
                    0.79 * v - 0.1 * u - 0.01 * py + 0.05 * ((vn + vs) + (ve + vw)),
                    kept + ((ts * a + tn * b) + (te * c + tw * d)),
                    0.8 * s + ((ss * a + sn * b) + (se * c + sw * d)),
                )
                for f in range(4):
                    target[f, l, j, put : put + 8] = jnp.where(is_wet, results[f], 0.0)
            slopes.append((new_x, new_y))
        return slopes

    start = [([zero] * thirds, [zero] * thirds) for _ in range(tiles)]
    lax.fori_loop(0, levels, level, start, unroll=UNROLL)


def fill_heat(load, heat):
    levels, rows = heat.shape[0], heat.shape[2]
    for tile in range(rows // 8):
        for j in range(3):
            optical = jnp.zeros((8, 128), F32)
            light = jnp.ones((8, 128), F32)
            for l in range(levels):
                optical = optical + (0.05 + 0.3 * load(l, tile, j))
                lower = jnp.exp(-optical)
                heat[l, j, 8 * tile : 8 * tile + 8] = (5.0 * DT) * (light - lower)
                light = lower


def extend(own, above, below, half):
    turned = swap(own)
    return jnp.concatenate([jnp.where(half, above, turned), jnp.where(half, turned, below)], axis=0)


def tracer_weights(u_up, u_down, v_east, v_west, growth, is_wet):
    wet = spread(is_wet)
    scale = wet * 0.05
    return (
        scale - scale * u_down,
        scale + scale * u_up,
        scale - scale * v_east,
        scale + scale * v_west,
        wet * 0.8,
        (wet * DT) * growth,
    )


def tracer_level(centre, up, down, sides, weights, reaction):
    nt = len(centre)
    lane = lanes(centre[0].shape[0])
    a, b, c, d, keep, grow = weights
    results = []
    for i in range(nt):
        side = 0.0 if sides is None else roll_lanes(sides, -2 * i - 1)
        east = jnp.where(lane == 127, side, roll_lanes(centre[i], 127))
        west = jnp.where(lane == 0, side, roll_lanes(centre[i], 1))
        mixed = reaction[i, 0] * centre[0]
        for k in range(1, nt):
            mixed = mixed + reaction[i, k] * centre[k]
        results.append(
            (keep * centre[i] + grow * mixed)
            + ((down[i] * a + up[i] * b) + (east * c + west * d))
        )
    return results


def pigment_of(first, second):
    return 0.25 * (first * first + second * second)


def gather_kernel(tracers, forcing, above, below, wet_rows, cells, winds, border):
    section, strip, group = place()
    nt, levels = tracers.shape[0], tracers.shape[1]
    low = spread(strip > 0)
    high = spread(strip < group - 1)

    @pl.when(section == 3)
    def _():
        border[...] = jnp.zeros_like(border)

    @pl.when(section != 3)
    def _():
        half = upper_half()

        def halo(message, plane, pair, odd, upward):
            tile = message[plane // 2, 3 * (plane % 2) + pair]
            return swap(tile) if odd != upward else tile

        def build(plane, own, l, masked):
            pair, odd = l // 2, l % 2 == 1
            up = halo(above, plane, pair, odd, False)
            down = halo(below, plane, pair, not odd, False)
            if masked:
                up, down = up * low, down * high
            return extend(own, up, down, half)

        lane = lanes(16)
        for l in range(levels):
            v = build(nt + 1, forcing[1, l], l, False)
            scale = 0.05 + jnp.where(lane == 0, -0.05, 0.05) * v
            products = []
            for a in range(nt):
                cell = build(a, tracers[a, l], l, True)
                cells[a, l, 8:24] = cell
                products.append(scale * cell)
            winds[0, l, 8:24] = build(nt, forcing[0, l], l, False)
            winds[1, l, 8:24] = v
            growth = jnp.exp(0.1 * forcing[2, l] - 0.05 * forcing[3, l])
            winds[2, l, 8:24] = build(nt + 2, growth, l, False)
            border[l] = edge_tile(products)


def first_kernel(
    flow, pigment, above, below, more_above, more_below, cells, winds, wet_rows, reaction,
    send_a, send_b, send_c, flow_next, partial, rim_edges, rim_wet,
    field_0, field_1, field_2, field_3, heat,
):
    section, strip, group = place()
    levels = pigment.shape[0]
    nt = cells.shape[0]
    low = spread(strip > 0)
    high = spread(strip < group - 1)

    @pl.when(section == 3)
    def _():
        def over(row, l):
            return above[row, l] if row < SHARED else more_above[row - SHARED, l]

        def under(row, l):
            return below[row, l] if row < SHARED else more_below[row - SHARED, l]

        def fill(l, carry):
            for f in range(4):
                for j in range(3):
                    field_0[f, l, j, 8:16] = over(3 * f + j, l) * low
                    field_0[f, l, j, 16:24] = flow[f, l, j]
                    field_0[f, l, j, 24:32] = under(3 * f + j, l) * high
            return carry

        lax.fori_loop(0, levels, fill, 0)

        def load(l, tile, j):
            if tile == 1:
                return pigment[l, j]
            return (over if tile == 0 else under)(12 + j, l)

        fill_heat(load, heat)
        substep(planes(field_0), field_1, heat, wet_rows, 3, 8, 8, 0, 0)
        substep(planes(field_1), field_2, heat, wet_rows, 3, 8, 8, 0, 0)
        substep(planes(field_2), field_3, heat, wet_rows, 3, 8, 8, 0, 0)
        substep(planes(field_3), flow_next, heat, wet_rows, 2, 12, 8, 4, 4)
        lane = lanes(8)
        outs = (send_a, send_b, send_c)
        sub = lax.broadcasted_iota(jnp.int32, (8, 128), 0)

        def mean(f, l, row, j):
            total = field_1[f, l, j, row : row + 8] + field_2[f, l, j, row : row + 8]
            total = total + field_3[f, l, j, row : row + 8]
            return 0.25 * (total + flow_next[f, l, j, row - 4 : row + 4])

        edge_v = [jnp.zeros((8, 128), F32) for _ in range(3)]
        rows_above = [jnp.zeros((8, 128), F32) for _ in range(3)]
        rows_below = [jnp.zeros((8, 128), F32) for _ in range(3)]
        for l in range(levels):
            v_mean = []
            for j in range(3):
                outs[j][l] = mean(0, l, 16, j)
                v_mean.append(mean(1, l, 16, j))
                outs[j][6 + l] = v_mean[j]
                warm = flow_next[2, l, j, 12:20]
                salt = flow_next[3, l, j, 12:20]
                outs[j][12 + l] = jnp.exp(0.1 * warm - 0.05 * salt)
                first = mean(0, l, 15, j)
                last = mean(0, l, 17, j)
                rows_above[j] = jnp.where(sub == l, roll_rows(first, l), rows_above[j])
                rows_below[j] = jnp.where(sub == l, roll_rows(last, l + 1), rows_below[j])
            for j in range(3):
                if j > 0:
                    edge_v[j] = jnp.where(
                        lane == 2 * l, roll_lanes(v_mean[j - 1], 2 * l + 1), edge_v[j]
                    )
                if j < 2:
                    edge_v[j] = jnp.where(
                        lane == 2 * l + 1, roll_lanes(v_mean[j + 1], 2 * l + 1), edge_v[j]
                    )
        for j in range(3):
            outs[j][18] = edge_v[j]
            outs[j][19] = rows_above[j]
            outs[j][20] = rows_below[j]

    @pl.when(section != 3)
    def _():
        floor = wet_rows[section, 4:20]

        def level(l, carry):
            v = winds[1, l, 8:24]
            weights = tracer_weights(
                winds[0, l, 7:23], winds[0, l, 9:25], roll_lanes(v, 127), roll_lanes(v, 1),
                winds[2, l, 8:24], floor > l,
            )
            results = tracer_level(
                [cells[a, l, 8:24] for a in range(nt)],
                [cells[a, l, 7:23] for a in range(nt)],
                [cells[a, l, 9:25] for a in range(nt)],
                None, weights, reaction,
            )
            for a in range(nt):
                partial[a, l] = results[a]
            rim_edges[l] = edge_tile([partial[a, l, 4:12] for a in range(nt)])
            wet = spread(wet_rows[section, 8:16] > l)
            first = jnp.broadcast_to(wet[:, :1], (8, 128))
            last = jnp.broadcast_to(wet[:, 127:], (8, 128))
            rim_wet[l] = jnp.where(lanes(8) % 2 == 0, last, first)
            return carry

        lax.fori_loop(0, levels, level, 0)


def sides_kernel(
    inner, outer, send_a, send_b, send_c, partial, rim_edges, rim_wet, wet_rows,
    out_a, out_b, out_c,
):
    section, _, _ = place()
    levels = partial.shape[1]
    outs = (out_a, out_b, out_c)

    @pl.when(section == 3)
    def _():
        for out, send in zip(outs, (send_a, send_b, send_c)):
            out[...] = send[...]

    @pl.when(section != 3)
    def _():
        floor = wet_rows[section, 4:20]
        lane = lanes(16)
        rim = (lane == 0) | (lane == 127)
        row = lax.broadcasted_iota(jnp.int32, (16, 128), 0)
        inside = (row > 0) & (row < 15)
        for l in range(levels):
            sides = side_columns(section, inner[l], outer[l])
            wet_rim = rim & (floor > l)
            pair = [
                partial[a, l] + jnp.where(wet_rim, roll_lanes(sides, -2 * a - 1), 0.0)
                for a in range(2)
            ]
            own = side_columns(section, inner[l, 4:12], outer[l, 4:12])
            edge = rim_edges[l] + jnp.where(rim_wet[l] > 0.0, own, 0.0)
            shade = jnp.where(inside, pigment_of(pair[0], pair[1]), 0.0)
            for out in outs:
                out[2 * l] = shade[:8]
                out[2 * l + 1] = shade[8:]
                out[12 + l] = edge
        for out in outs:
            for i in range(18, 21):
                out[i] = jnp.zeros((8, 128), F32)


def roll_rows(x, by):
    by = by % 8
    return x if by == 0 else pltpu.roll(x, by, 0)


def planes(buffer):
    return [buffer.at[f] for f in range(4)]


def early_kernel(flow_next, wet_rows, partial, inner, outer, early, tracers_next):
    section, _, _ = place()
    nt, levels = partial.shape[0], partial.shape[1]

    @pl.when(section != 3)
    def _():
        floor = wet_rows[section, 4:20]
        lane = lanes(16)
        rim = (lane == 0) | (lane == 127)

        def level(l, carry):
            sides = side_columns(section, inner[l], outer[l])
            wet_rim = rim & (floor > l)
            for a in range(nt):
                side = jnp.where(wet_rim, roll_lanes(sides, -2 * a - 1), 0.0)
                tracers_next[a, l] = partial[a, l] + side
            return carry

        lax.fori_loop(0, levels, level, 0, unroll=2)

    @pl.when(section == 3)
    def _():
        substep(planes(flow_next), early, None, wet_rows, 2, 8, 8, 0, 4)


def second_kernel(
    from_b, from_a, from_c, early, tracers_next, wet_rows, reaction,
    out_a, out_b, out_c, flow_last, tracers_last, warm, field_1, field_2, heat, winds,
):
    section, _, _ = place()
    levels = heat.shape[0]
    nt = tracers_next.shape[0]

    @pl.when(section == 3)
    def _():
        shades = (from_a, from_b, from_c)

        def load(l, tile, j):
            return shades[j][2 * l + tile]

        fill_heat(load, heat)

        def warm_up(l, carry):
            for j in range(3):
                heated = jnp.where(wet_rows[j, 4:20] > l, heat[l, j], 0.0)
                warm[l, j, 8:24] = early[2, l, j, 8:24] + heated
            return carry

        lax.fori_loop(0, levels, warm_up, 0)
        first = planes(early)
        first[2] = warm
        substep(first, field_1, heat, wet_rows, 2, 8, 8, 0, 4)
        substep(planes(field_1), field_2, heat, wet_rows, 2, 8, 8, 0, 4)
        substep(planes(field_2), flow_last, heat, wet_rows, 1, 12, 0, 4, 8)
        outs = (out_a, out_b, out_c)
        for l in range(levels):
            for j in range(3):
                for f in range(2):
                    total = early[f, l, j, 12:20] + field_1[f, l, j, 12:20]
                    total = total + field_2[f, l, j, 12:20]
                    outs[j][6 * f + l] = 0.25 * (total + flow_last[f, l, j])
                outs[j][12 + l] = flow_last[2, l, j]
                outs[j][18 + l] = flow_last[3, l, j]

    @pl.when(section != 3)
    def _():
        def driven(i):
            return jnp.where(
                section == 0, from_a[i], jnp.where(section == 1, from_b[i], from_c[i])
            )

        for i in range(18):
            winds[i] = driven(i)
        edge_v = driven(18)
        rows_above = driven(19)
        rows_below = driven(20)
        lane = lanes(8)
        sub = lax.broadcasted_iota(jnp.int32, (8, 128), 0)
        for l in range(levels):
            u, v = winds[l], winds[6 + l]
            winds[18 + l] = jnp.where(sub == 0, roll_rows(rows_above, -l), roll_rows(u, 1))
            winds[24 + l] = jnp.where(sub == 7, roll_rows(rows_below, 7 - l), roll_rows(u, 7))
            winds[30 + l] = jnp.where(
                lane == 127, roll_lanes(edge_v, 126 - 2 * l), roll_lanes(v, 127)
            )
            winds[36 + l] = jnp.where(lane == 0, roll_lanes(edge_v, -2 * l), roll_lanes(v, 1))
            winds[42 + l] = side_columns(section, from_c[12 + l], from_a[12 + l])
        floor = wet_rows[section, 8:16]

        def level(l, carry):
            weights = tracer_weights(
                winds[18 + l], winds[24 + l], winds[30 + l], winds[36 + l], winds[12 + l], floor > l
            )
            results = tracer_level(
                [tracers_next[a, l, 4:12] for a in range(nt)],
                [tracers_next[a, l, 3:11] for a in range(nt)],
                [tracers_next[a, l, 5:13] for a in range(nt)],
                winds[42 + l], weights, reaction,
            )
            for a in range(nt):
                tracers_last[a, l] = results[a]
            shade = pigment_of(results[0], results[1])
            for out in (out_a, out_b, out_c):
                out[l] = shade
                for i in range(1, 4):
                    out[6 * i + l] = jnp.zeros((8, 128), F32)
            return carry

        lax.fori_loop(0, levels, level, 0)


def store_kernel(flow_last, tracers_last, flow_out, tracers_out, blank, sems):
    section, _, _ = place()
    blank[...] = jnp.zeros_like(blank)

    def put(flow_of, tracers_from):
        copies = [pltpu.make_async_copy(tracers_from, tracers_out, sems.at[3])]
        for j in range(3):
            target = flow_out.at[:, :, :, 128 * j : 128 * j + 128]
            copies.append(pltpu.make_async_copy(flow_of(j), target, sems.at[j]))
        for copy in copies:
            copy.start()
        for copy in copies:
            copy.wait()

    @pl.when(section == 3)
    def _():
        put(lambda j: flow_last.at[:, :, j], blank)

    @pl.when(section != 3)
    def _():
        put(lambda j: blank.at[0:4], tracers_last)


def last_kernel(from_b, from_a, from_c, light_out, forcing_out):
    section, _, _ = place()
    levels = light_out.shape[0]
    is_dynamics = section == 3
    for l in range(levels):
        for j, shade in enumerate((from_a, from_b, from_c)):
            light_out[l, :, 128 * j : 128 * j + 128] = jnp.where(is_dynamics, shade[l], 0.0)
        for f in range(4):
            i = 6 * f + l
            picked = jnp.where(
                section == 0, from_a[i], jnp.where(section == 1, from_b[i], from_c[i])
            )
            forcing_out[f, l] = jnp.where(is_dynamics, 0.0, picked)


def call(kernel, shapes, operands, spaces, scratch=(), out_space=pltpu.VMEM):
    operands = [
        pltpu.with_memory_space_constraint(x, pltpu.HBM) if space == pltpu.HBM else x
        for x, space in zip(operands, spaces)
    ]
    return pl.pallas_call(
        kernel,
        out_shape=[jax.ShapeDtypeStruct(shape, dtype) for shape, dtype in shapes],
        in_specs=[pl.BlockSpec(memory_space=space) for space in spaces],
        out_specs=[pl.BlockSpec(memory_space=out_space) for _ in shapes],
        scratch_shapes=list(scratch),
        compiler_params=pltpu.CompilerParams(vmem_limit_bytes=VMEM_LIMIT),
    )(*operands)


def route(target):
    total = lax.axis_size("comp") * lax.axis_size("gy") * lax.axis_size("gx")
    group = total // SECTIONS
    pairs = []
    for moved in range(total):
        section, strip = target(moved // group, moved % group, group)
        pairs.append(((moved - 1) % total, (section * group + strip - 1) % total))
    return pairs


def partner(strip, group):
    if strip in (0, group - 1):
        return group - 1 - strip
    return strip + 1 if strip % 2 == 1 else strip - 1


def trade(value, *pairs):
    other = {}
    for a, b in pairs:
        other[a], other[b] = b, a

    def target(k, s, g):
        return (other[k], s) if k in other else (k, partner(s, g))

    return lax.ppermute(value, AXES, route(target))


def along_dynamics(value, by):
    def target(k, s, g):
        return (k, (s + by) % g) if k == 3 else (k, partner(s, g))

    return lax.ppermute(value, AXES, route(target))


def along(value, by):
    return lax.ppermute(value, AXES, route(lambda k, s, g: divmod((k * g + s + by) % (SECTIONS * g), g)))


def on_device(flow_fields, chlorophyll_lag, tracers, forcing, ocean_mask, bottom, reaction):
    levels = chlorophyll_lag.shape[0]
    nt = tracers.shape[0]
    breadth = flow_fields.shape[3]
    vmem, smem, hbm = pltpu.VMEM, pltpu.SMEM, pltpu.HBM
    message = (SHARED, levels, 8, 128)
    more = (15 - SHARED, levels, 8, 128)
    to_next, to_prev, more_next, more_prev, flow, pigment, tracers, forcing = call(
        load_kernel,
        [
            (message, F32), (message, F32), (more, F32), (more, F32),
            ((4, levels, 3, 8, 128), F32), ((levels, 3, 8, 128), F32),
            (tracers.shape, F32), (forcing.shape, F32),
        ],
        (flow_fields, chlorophyll_lag, tracers, forcing),
        (hbm,) * 4,
        (pltpu.SemaphoreType.DMA((2 * levels,)),),
    )
    above = along(to_next, 1)
    below = along(to_prev, -1)
    more_above = along_dynamics(more_next, 1)
    more_below = along_dynamics(more_prev, -1)
    (wet_rows,) = call(
        mask_kernel,
        [((3, 24, 128), jnp.int32)],
        (ocean_mask, bottom),
        (hbm,) * 2,
        (
            pltpu.VMEM((3, 8, breadth), jnp.int32),
            pltpu.VMEM((3, 8, breadth), jnp.int32),
            pltpu.SemaphoreType.DMA((6,)),
        ),
    )
    cells, winds, border = call(
        gather_kernel,
        [((nt, levels, 32, 128), F32), ((3, levels, 32, 128), F32), ((levels, 16, 128), F32)],
        (tracers, forcing, above, below, wet_rows),
        (vmem,) * 5,
    )
    inner = trade(border, (0, 1))
    outer = trade(border, (1, 2))
    exchange = ((21, 8, 128), F32)
    *sends, flow_next, partial, rim_edges, rim_wet = call(
        first_kernel,
        [
            exchange, exchange, exchange,
            ((4, levels, 3, 32, 128), F32), ((nt, levels, 16, 128), F32),
            ((levels, 8, 128), F32), ((levels, 8, 128), F32),
        ],
        (
            flow, pigment, above, below, more_above, more_below, cells, winds, wet_rows,
            reaction,
        ),
        (vmem,) * 9 + (smem,),
        (
            *[pltpu.VMEM((4, levels, 3, 40, 128), F32) for _ in range(4)],
            pltpu.VMEM((levels, 3, 24, 128), F32),
        ),
    )
    sent = call(
        sides_kernel,
        [exchange, exchange, exchange],
        (inner, outer, *sends, partial, rim_edges, rim_wet, wet_rows),
        (vmem,) * 9,
    )
    from_b = trade(sent[1], (3, 1))
    from_a = trade(sent[0], (3, 0), (1, 2))
    from_c = trade(sent[2], (3, 2), (0, 1))
    early, tracers_next = call(
        early_kernel,
        [((4, levels, 3, 32, 128), F32), ((nt, levels, 16, 128), F32)],
        (flow_next, wet_rows, partial, inner, outer),
        (vmem,) * 5,
    )
    exchange = ((24, 8, 128), F32)
    last = call(
        second_kernel,
        [
            exchange, exchange, exchange,
            ((4, levels, 3, 8, 128), F32), ((nt, levels, 8, 128), F32),
        ],
        (from_b, from_a, from_c, early, tracers_next, wet_rows, reaction),
        (vmem,) * 6 + (smem,),
        (
            pltpu.VMEM((levels, 3, 32, 128), F32),
            *[pltpu.VMEM((4, levels, 3, 32, 128), F32) for _ in range(2)],
            pltpu.VMEM((levels, 3, 16, 128), F32),
            pltpu.VMEM((48, 8, 128), F32),
        ),
    )
    final_b = trade(last[1], (3, 1))
    final_a = trade(last[0], (3, 0))
    final_c = trade(last[2], (3, 2))
    flow_out, tracers_out = call(
        store_kernel,
        [(flow_fields.shape, F32), (tracers.shape, F32)],
        (last[3], last[4]),
        (vmem, vmem),
        (pltpu.VMEM(tracers.shape, F32), pltpu.SemaphoreType.DMA((4,))),
        hbm,
    )
    light_out, forcing_out = call(
        last_kernel,
        [((levels, 8, breadth), F32), ((4, levels, 8, 128), F32)],
        (final_b, final_a, final_c),
        (vmem,) * 3,
    )
    return flow_out, light_out, tracers_out, forcing_out


def solution(mesh):
    rows = P(None, None, AXES, None)
    light = P(None, AXES, None)
    return jax.shard_map(
        on_device,
        mesh=mesh,
        in_specs=(rows, light, rows, rows, P(), P(), P()),
        out_specs=(rows, light, rows, rows),
        check_vma=False,
    )
```

```python
import jax
import jax.numpy as jnp
from jax import lax
from jax.experimental import pallas as pl
from jax.experimental.pallas import tpu as pltpu
from jax.sharding import PartitionSpec as P

AXES = ("comp", "gy", "gx")
SECTIONS = 4
SHARED = 10
DT = 0.1
F32 = jnp.float32
UNROLL = 2
VMEM_LIMIT = 24 * 1024 * 1024


def place():
    gy = lax.axis_size("gy")
    gx = lax.axis_size("gx")
    total = lax.axis_size("comp") * gy * gx
    group = total // SECTIONS
    position = (lax.axis_index("comp") * gy + lax.axis_index("gy")) * gx + lax.axis_index("gx")
    moved = lax.rem(position + 1, total)
    return moved // group, lax.rem(moved, group), group


def lanes(rows):
    return lax.broadcasted_iota(jnp.int32, (rows, 128), 1)


def roll_lanes(x, by):
    by = by % 128
    return x if by == 0 else pltpu.roll(x, by, 1)


def swap(x):
    return pltpu.roll(x, 4, 0)


def upper_half():
    return lax.broadcasted_iota(jnp.int32, (8, 128), 0) < 4


def spread(flag):
    return jnp.where(flag, 1.0, 0.0).astype(F32)


def edge_tile(planes):
    pair = lanes(planes[0].shape[0]) // 2
    edges = jnp.zeros_like(planes[0])
    for a, x in enumerate(planes):
        edges = jnp.where(pair == a, roll_lanes(x, 2 * a + 1), edges)
    return edges


def pack_rows(tracers, forcing, to_next, to_prev, copies):
    half = upper_half()
    nt, levels = tracers.shape[0], tracers.shape[1]

    def put(plane, pair, even, odd):
        row, col = plane // 2, 3 * (plane % 2)
        to_next[row, col + pair] = jnp.where(half, swap(even), odd)
        to_prev[row, col + pair] = jnp.where(half, even, swap(odd))

    for pair in range(levels // 2):
        even, odd = 2 * pair, 2 * pair + 1
        for copy in copies[4 * pair : 4 * pair + 4]:
            copy.wait()
        for a in range(nt):
            put(a, pair, tracers[a, even], tracers[a, odd])
        put(nt, pair, forcing[0, even], forcing[0, odd])
        put(nt + 1, pair, forcing[1, even], forcing[1, odd])
        growth = [jnp.exp(0.1 * forcing[2, l] - 0.05 * forcing[3, l]) for l in (even, odd)]
        put(nt + 2, pair, growth[0], growth[1])
        put(nt + 3, pair, jnp.zeros((8, 128), F32), jnp.zeros((8, 128), F32))


def load_kernel(
    flow, pigment, tracers, forcing,
    to_next, to_prev, more_next, more_prev, flow_in, pigment_in, tracers_in, forcing_in, sems,
):
    section, _, _ = place()
    levels = pigment.shape[0]

    @pl.when(section == 3)
    def _():
        copies = []
        for j in range(3):
            cols = slice(128 * j, 128 * j + 128)
            copies.append(
                pltpu.make_async_copy(flow.at[:, :, :, cols], flow_in.at[:, :, j], sems.at[j])
            )
            copies.append(
                pltpu.make_async_copy(pigment.at[:, :, cols], pigment_in.at[:, j], sems.at[3 + j])
            )
        for copy in copies:
            copy.start()
        for copy in copies:
            copy.wait()

        def level(l, carry):
            for f in range(5):
                for j in range(3):
                    tile = flow_in[f, l, j] if f < 4 else pigment_in[l, j]
                    row = 3 * f + j
                    if row < SHARED:
                        to_next[row, l] = tile
                        to_prev[row, l] = tile
                    else:
                        more_next[row - SHARED, l] = tile
                        more_prev[row - SHARED, l] = tile
            return carry

        lax.fori_loop(0, levels, level, 0)

    @pl.when(section != 3)
    def _():
        copies = []
        for l in range(levels):
            copies.append(
                pltpu.make_async_copy(tracers.at[:, l], tracers_in.at[:, l], sems.at[l])
            )
            copies.append(
                pltpu.make_async_copy(forcing.at[:, l], forcing_in.at[:, l], sems.at[levels + l])
            )
        for copy in copies:
            copy.start()
        pack_rows(tracers_in, forcing_in, to_next, to_prev, copies)
        more_next[...] = jnp.zeros_like(more_next)
        more_prev[...] = jnp.zeros_like(more_prev)


def mask_kernel(ocean, bottom, reaction, wet_rows, rates, ocean_rows, bottom_rows, mask_sems):
    _, strip, group = place()
    starts = [jnp.maximum(strip - 1, 0), strip, jnp.minimum(strip + 1, group - 1)]
    masks = []
    for i, start in enumerate(starts):
        rows = pl.ds(pl.multiple_of(start * 8, 8), 8)
        masks.append(pltpu.make_async_copy(ocean.at[rows], ocean_rows.at[i], mask_sems.at[i]))
        masks.append(pltpu.make_async_copy(bottom.at[rows], bottom_rows.at[i], mask_sems.at[3 + i]))
    for copy in masks:
        copy.start()
    nt = reaction.shape[0]
    for k in range(nt):
        rates[k] = jnp.broadcast_to(reaction[:, k : k + 1], (nt, 128))
    for copy in masks:
        copy.wait()
    inside = [(strip > 0).astype(jnp.int32), 1, (strip < group - 1).astype(jnp.int32)]
    for i in range(3):
        floor = jnp.where(ocean_rows[i] == 1, bottom_rows[i], 0) * inside[i]
        for j in range(3):
            wet_rows[j, 8 * i : 8 * i + 8] = floor[:, 128 * j : 128 * j + 128]


def side_columns(section, inner, outer):
    even = lanes(inner.shape[0]) % 2 == 0
    east = roll_lanes(jnp.where(section == 0, inner, outer), -1)
    west = roll_lanes(jnp.where(section == 1, inner, outer), 1)
    east = jnp.where(section < 2, east, 0.0)
    west = jnp.where(section > 0, west, 0.0)
    return jnp.where(even, east, west)


def shifted(tiles):
    lane = lanes(tiles[0].shape[0])
    left = [roll_lanes(x, 127) for x in tiles]
    right = [roll_lanes(x, 1) for x in tiles]
    count = len(tiles)
    east = [
        jnp.where(lane == 127, left[j + 1] if j + 1 < count else 0.0, left[j]) for j in range(count)
    ]
    west = [jnp.where(lane == 0, right[j - 1] if j > 0 else 0.0, right[j]) for j in range(count)]
    return east, west


def substep(source, target, heat, wet_rows, tiles, read_at, write_at, heat_at, wet_at):
    levels = target.shape[1]
    thirds = 3
    zero = jnp.zeros((8, 128), F32)

    def level(l, carry):
        slopes = []
        for tile in range(tiles):
            row = read_at + 8 * tile
            put = write_at + 8 * tile
            slope_x, slope_y = carry[tile]

            def load(f, by):
                return [source[f][l, j, row + by : row + by + 8] for j in range(thirds)]

            centre = [load(f, 0) for f in range(4)]
            up = [load(f, -1) for f in range(4)]
            down = [load(f, 1) for f in range(4)]
            sides = [shifted(centre[f]) for f in range(4)]
            new_x, new_y = [], []
            for j in range(thirds):
                u, v, t, s = (centre[f][j] for f in range(4))
                un, vn, tn, sn = (up[f][j] for f in range(4))
                us, vs, ts, ss = (down[f][j] for f in range(4))
                ue, ve, te, se = (sides[f][0][j] for f in range(4))
                uw, vw, tw, sw = (sides[f][1][j] for f in range(4))
                px = slope_x[j] + ((ss - sn) - (ts - tn))
                py = slope_y[j] + ((se - sw) - (te - tw))
                new_x.append(px)
                new_y.append(py)
                is_wet = wet_rows[j, wet_at + 8 * tile : wet_at + 8 * tile + 8] > l
                a = 0.05 - 0.05 * us
                b = 0.05 + 0.05 * un
                c = 0.05 - 0.05 * ve
                d = 0.05 + 0.05 * vw
                kept = 0.8 * t
                if heat is not None:
                    kept = kept + heat[l, j, heat_at + 8 * tile : heat_at + 8 * tile + 8]
                results = (
                    0.79 * u + 0.1 * v - 0.01 * px + 0.05 * ((un + us) + (ue + uw)),
                    0.79 * v - 0.1 * u - 0.01 * py + 0.05 * ((vn + vs) + (ve + vw)),
                    kept + ((ts * a + tn * b) + (te * c + tw * d)),
                    0.8 * s + ((ss * a + sn * b) + (se * c + sw * d)),
                )
                for f in range(4):
                    target[f, l, j, put : put + 8] = jnp.where(is_wet, results[f], 0.0)
            slopes.append((new_x, new_y))
        return slopes

    start = [([zero] * thirds, [zero] * thirds) for _ in range(tiles)]
    lax.fori_loop(0, levels, level, start, unroll=UNROLL)


def fill_heat(load, heat):
    levels, rows = heat.shape[0], heat.shape[2]
    for tile in range(rows // 8):
        for j in range(3):
            optical = jnp.zeros((8, 128), F32)
            light = jnp.ones((8, 128), F32)
            for l in range(levels):
                optical = optical + (0.05 + 0.3 * load(l, tile, j))
                lower = jnp.exp(-optical)
                heat[l, j, 8 * tile : 8 * tile + 8] = (5.0 * DT) * (light - lower)
                light = lower


def extend(own, above, below, half):
    turned = swap(own)
    return jnp.concatenate([jnp.where(half, above, turned), jnp.where(half, turned, below)], axis=0)


def tracer_weights(u_up, u_down, v_east, v_west, growth, is_wet):
    wet = spread(is_wet)
    scale = wet * 0.05
    return (
        scale - scale * u_down,
        scale + scale * u_up,
        scale - scale * v_east,
        scale + scale * v_west,
        wet * 0.8,
        (wet * DT) * growth,
    )


def tracer_level(centre, up, down, sides, weights, reaction):
    nt = len(centre)
    lane = lanes(centre[0].shape[0])
    a, b, c, d, keep, grow = weights
    results = []

    def rate(k, i):
        return jnp.broadcast_to(reaction[k, i : i + 1], centre[0].shape)

    for i in range(nt):
        side = 0.0 if sides is None else roll_lanes(sides, -2 * i - 1)
        east = jnp.where(lane == 127, side, roll_lanes(centre[i], 127))
        west = jnp.where(lane == 0, side, roll_lanes(centre[i], 1))
        mixed = rate(0, i) * centre[0]
        for k in range(1, nt):
            mixed = mixed + rate(k, i) * centre[k]
        results.append(
            (keep * centre[i] + grow * mixed)
            + ((down[i] * a + up[i] * b) + (east * c + west * d))
        )
    return results


def pigment_of(first, second):
    return 0.25 * (first * first + second * second)


def gather_kernel(tracers, forcing, above, below, wet_rows, cells, winds, border):
    section, strip, group = place()
    nt, levels = tracers.shape[0], tracers.shape[1]
    low = spread(strip > 0)
    high = spread(strip < group - 1)

    @pl.when(section == 3)
    def _():
        border[...] = jnp.zeros_like(border)

    @pl.when(section != 3)
    def _():
        half = upper_half()

        def halo(message, plane, pair, odd, upward):
            tile = message[plane // 2, 3 * (plane % 2) + pair]
            return swap(tile) if odd != upward else tile

        def build(plane, own, l, masked):
            pair, odd = l // 2, l % 2 == 1
            up = halo(above, plane, pair, odd, False)
            down = halo(below, plane, pair, not odd, False)
            if masked:
                up, down = up * low, down * high
            return extend(own, up, down, half)

        lane = lanes(16)
        for l in range(levels):
            v = build(nt + 1, forcing[1, l], l, False)
            scale = 0.05 + jnp.where(lane == 0, -0.05, 0.05) * v
            products = []
            for a in range(nt):
                cell = build(a, tracers[a, l], l, True)
                cells[a, l, 8:24] = cell
                products.append(scale * cell)
            winds[0, l, 8:24] = build(nt, forcing[0, l], l, False)
            winds[1, l, 8:24] = v
            growth = jnp.exp(0.1 * forcing[2, l] - 0.05 * forcing[3, l])
            winds[2, l, 8:24] = build(nt + 2, growth, l, False)
            border[l] = edge_tile(products)


def first_kernel(
    flow, pigment, above, below, more_above, more_below, cells, winds, wet_rows, reaction,
    send_a, send_b, send_c, flow_next, partial, rim_edges, rim_wet,
    field_0, field_1, field_2, field_3, heat,
):
    section, strip, group = place()
    levels = pigment.shape[0]
    nt = cells.shape[0]
    low = spread(strip > 0)
    high = spread(strip < group - 1)

    @pl.when(section == 3)
    def _():
        def over(row, l):
            return above[row, l] if row < SHARED else more_above[row - SHARED, l]

        def under(row, l):
            return below[row, l] if row < SHARED else more_below[row - SHARED, l]

        def fill(l, carry):
            for f in range(4):
                for j in range(3):
                    field_0[f, l, j, 8:16] = over(3 * f + j, l) * low
                    field_0[f, l, j, 16:24] = flow[f, l, j]
                    field_0[f, l, j, 24:32] = under(3 * f + j, l) * high
            return carry

        lax.fori_loop(0, levels, fill, 0)

        def load(l, tile, j):
            if tile == 1:
                return pigment[l, j]
            return (over if tile == 0 else under)(12 + j, l)

        fill_heat(load, heat)
        substep(planes(field_0), field_1, heat, wet_rows, 3, 8, 8, 0, 0)
        substep(planes(field_1), field_2, heat, wet_rows, 3, 8, 8, 0, 0)
        substep(planes(field_2), field_3, heat, wet_rows, 3, 8, 8, 0, 0)
        substep(planes(field_3), flow_next, heat, wet_rows, 2, 12, 8, 4, 4)
        lane = lanes(8)
        outs = (send_a, send_b, send_c)
        sub = lax.broadcasted_iota(jnp.int32, (8, 128), 0)

        def mean(f, l, row, j):
            total = field_1[f, l, j, row : row + 8] + field_2[f, l, j, row : row + 8]
            total = total + field_3[f, l, j, row : row + 8]
            return 0.25 * (total + flow_next[f, l, j, row - 4 : row + 4])

        edge_v = [jnp.zeros((8, 128), F32) for _ in range(3)]
        rows_above = [jnp.zeros((8, 128), F32) for _ in range(3)]
        rows_below = [jnp.zeros((8, 128), F32) for _ in range(3)]
        for l in range(levels):
            v_mean = []
            for j in range(3):
                outs[j][l] = mean(0, l, 16, j)
                v_mean.append(mean(1, l, 16, j))
                outs[j][6 + l] = v_mean[j]
                warm = flow_next[2, l, j, 12:20]
                salt = flow_next[3, l, j, 12:20]
                outs[j][12 + l] = jnp.exp(0.1 * warm - 0.05 * salt)
                first = mean(0, l, 15, j)
                last = mean(0, l, 17, j)
                rows_above[j] = jnp.where(sub == l, roll_rows(first, l), rows_above[j])
                rows_below[j] = jnp.where(sub == l, roll_rows(last, l + 1), rows_below[j])
            for j in range(3):
                if j > 0:
                    edge_v[j] = jnp.where(
                        lane == 2 * l, roll_lanes(v_mean[j - 1], 2 * l + 1), edge_v[j]
                    )
                if j < 2:
                    edge_v[j] = jnp.where(
                        lane == 2 * l + 1, roll_lanes(v_mean[j + 1], 2 * l + 1), edge_v[j]
                    )
        for j in range(3):
            outs[j][18] = edge_v[j]
            outs[j][19] = rows_above[j]
            outs[j][20] = rows_below[j]

    @pl.when(section != 3)
    def _():
        floor = wet_rows[section, 4:20]

        def level(l, carry):
            v = winds[1, l, 8:24]
            weights = tracer_weights(
                winds[0, l, 7:23], winds[0, l, 9:25], roll_lanes(v, 127), roll_lanes(v, 1),
                winds[2, l, 8:24], floor > l,
            )
            results = tracer_level(
                [cells[a, l, 8:24] for a in range(nt)],
                [cells[a, l, 7:23] for a in range(nt)],
                [cells[a, l, 9:25] for a in range(nt)],
                None, weights, reaction,
            )
            for a in range(nt):
                partial[a, l] = results[a]
            rim_edges[l] = edge_tile([partial[a, l, 4:12] for a in range(nt)])
            wet = spread(wet_rows[section, 8:16] > l)
            first = jnp.broadcast_to(wet[:, :1], (8, 128))
            last = jnp.broadcast_to(wet[:, 127:], (8, 128))
            rim_wet[l] = jnp.where(lanes(8) % 2 == 0, last, first)
            return carry

        lax.fori_loop(0, levels, level, 0)


def sides_kernel(
    inner, outer, send_a, send_b, send_c, partial, rim_edges, rim_wet, wet_rows,
    out_a, out_b, out_c,
):
    section, _, _ = place()
    levels = partial.shape[1]
    outs = (out_a, out_b, out_c)

    @pl.when(section == 3)
    def _():
        for out, send in zip(outs, (send_a, send_b, send_c)):
            out[...] = send[...]

    @pl.when(section != 3)
    def _():
        floor = wet_rows[section, 4:20]
        lane = lanes(16)
        rim = (lane == 0) | (lane == 127)
        row = lax.broadcasted_iota(jnp.int32, (16, 128), 0)
        inside = (row > 0) & (row < 15)
        for l in range(levels):
            sides = side_columns(section, inner[l], outer[l])
            wet_rim = rim & (floor > l)
            pair = [
                partial[a, l] + jnp.where(wet_rim, roll_lanes(sides, -2 * a - 1), 0.0)
                for a in range(2)
            ]
            own = side_columns(section, inner[l, 4:12], outer[l, 4:12])
            edge = rim_edges[l] + jnp.where(rim_wet[l] > 0.0, own, 0.0)
            shade = jnp.where(inside, pigment_of(pair[0], pair[1]), 0.0)
            for out in outs:
                out[2 * l] = shade[:8]
                out[2 * l + 1] = shade[8:]
                out[12 + l] = edge
        for out in outs:
            for i in range(18, 21):
                out[i] = jnp.zeros((8, 128), F32)


def roll_rows(x, by):
    by = by % 8
    return x if by == 0 else pltpu.roll(x, by, 0)


def planes(buffer):
    return [buffer.at[f] for f in range(4)]


def early_kernel(flow_next, wet_rows, partial, inner, outer, early, tracers_next):
    section, _, _ = place()
    nt, levels = partial.shape[0], partial.shape[1]

    @pl.when(section != 3)
    def _():
        floor = wet_rows[section, 4:20]
        lane = lanes(16)
        rim = (lane == 0) | (lane == 127)

        def level(l, carry):
            sides = side_columns(section, inner[l], outer[l])
            wet_rim = rim & (floor > l)
            for a in range(nt):
                side = jnp.where(wet_rim, roll_lanes(sides, -2 * a - 1), 0.0)
                tracers_next[a, l] = partial[a, l] + side
            return carry

        lax.fori_loop(0, levels, level, 0, unroll=2)

    @pl.when(section == 3)
    def _():
        substep(planes(flow_next), early, None, wet_rows, 2, 8, 8, 0, 4)


def second_kernel(
    from_b, from_a, from_c, early, tracers_next, wet_rows, reaction,
    out_a, out_b, out_c, flow_last, tracers_last, warm, field_1, field_2, heat, winds,
):
    section, _, _ = place()
    levels = heat.shape[0]
    nt = tracers_next.shape[0]

    @pl.when(section == 3)
    def _():
        shades = (from_a, from_b, from_c)

        def load(l, tile, j):
            return shades[j][2 * l + tile]

        fill_heat(load, heat)

        def warm_up(l, carry):
            for j in range(3):
                heated = jnp.where(wet_rows[j, 4:20] > l, heat[l, j], 0.0)
                warm[l, j, 8:24] = early[2, l, j, 8:24] + heated
            return carry

        lax.fori_loop(0, levels, warm_up, 0)
        first = planes(early)
        first[2] = warm
        substep(first, field_1, heat, wet_rows, 2, 8, 8, 0, 4)
        substep(planes(field_1), field_2, heat, wet_rows, 2, 8, 8, 0, 4)
        substep(planes(field_2), flow_last, heat, wet_rows, 1, 12, 0, 4, 8)
        outs = (out_a, out_b, out_c)
        for l in range(levels):
            for j in range(3):
                for f in range(2):
                    total = early[f, l, j, 12:20] + field_1[f, l, j, 12:20]
                    total = total + field_2[f, l, j, 12:20]
                    outs[j][6 * f + l] = 0.25 * (total + flow_last[f, l, j])
                outs[j][12 + l] = flow_last[2, l, j]
                outs[j][18 + l] = flow_last[3, l, j]

    @pl.when(section != 3)
    def _():
        def driven(i):
            return jnp.where(
                section == 0, from_a[i], jnp.where(section == 1, from_b[i], from_c[i])
            )

        for i in range(18):
            winds[i] = driven(i)
        edge_v = driven(18)
        rows_above = driven(19)
        rows_below = driven(20)
        lane = lanes(8)
        sub = lax.broadcasted_iota(jnp.int32, (8, 128), 0)
        for l in range(levels):
            u, v = winds[l], winds[6 + l]
            winds[18 + l] = jnp.where(sub == 0, roll_rows(rows_above, -l), roll_rows(u, 1))
            winds[24 + l] = jnp.where(sub == 7, roll_rows(rows_below, 7 - l), roll_rows(u, 7))
            winds[30 + l] = jnp.where(
                lane == 127, roll_lanes(edge_v, 126 - 2 * l), roll_lanes(v, 127)
            )
            winds[36 + l] = jnp.where(lane == 0, roll_lanes(edge_v, -2 * l), roll_lanes(v, 1))
            winds[42 + l] = side_columns(section, from_c[12 + l], from_a[12 + l])
        floor = wet_rows[section, 8:16]

        def level(l, carry):
            weights = tracer_weights(
                winds[18 + l], winds[24 + l], winds[30 + l], winds[36 + l], winds[12 + l], floor > l
            )
            results = tracer_level(
                [tracers_next[a, l, 4:12] for a in range(nt)],
                [tracers_next[a, l, 3:11] for a in range(nt)],
                [tracers_next[a, l, 5:13] for a in range(nt)],
                winds[42 + l], weights, reaction,
            )
            for a in range(nt):
                tracers_last[a, l] = results[a]
            shade = pigment_of(results[0], results[1])
            for out in (out_a, out_b, out_c):
                out[l] = shade
                for i in range(1, 4):
                    out[6 * i + l] = jnp.zeros((8, 128), F32)
            return carry

        lax.fori_loop(0, levels, level, 0)


def store_kernel(flow_last, tracers_last, flow_out, tracers_out, blank, sems):
    section, _, _ = place()
    blank[...] = jnp.zeros_like(blank)

    def put(flow_of, tracers_from):
        copies = [pltpu.make_async_copy(tracers_from, tracers_out, sems.at[3])]
        for j in range(3):
            target = flow_out.at[:, :, :, 128 * j : 128 * j + 128]
            copies.append(pltpu.make_async_copy(flow_of(j), target, sems.at[j]))
        for copy in copies:
            copy.start()
        for copy in copies:
            copy.wait()

    @pl.when(section == 3)
    def _():
        put(lambda j: flow_last.at[:, :, j], blank)

    @pl.when(section != 3)
    def _():
        put(lambda j: blank.at[0:4], tracers_last)


def last_kernel(from_b, from_a, from_c, light_out, forcing_out):
    section, _, _ = place()
    levels = light_out.shape[0]
    is_dynamics = section == 3
    for l in range(levels):
        for j, shade in enumerate((from_a, from_b, from_c)):
            light_out[l, :, 128 * j : 128 * j + 128] = jnp.where(is_dynamics, shade[l], 0.0)
        for f in range(4):
            i = 6 * f + l
            picked = jnp.where(
                section == 0, from_a[i], jnp.where(section == 1, from_b[i], from_c[i])
            )
            forcing_out[f, l] = jnp.where(is_dynamics, 0.0, picked)


def call(kernel, shapes, operands, spaces, scratch=(), out_space=pltpu.VMEM):
    operands = [
        pltpu.with_memory_space_constraint(x, pltpu.HBM) if space == pltpu.HBM else x
        for x, space in zip(operands, spaces)
    ]
    return pl.pallas_call(
        kernel,
        out_shape=[jax.ShapeDtypeStruct(shape, dtype) for shape, dtype in shapes],
        in_specs=[pl.BlockSpec(memory_space=space) for space in spaces],
        out_specs=[pl.BlockSpec(memory_space=out_space) for _ in shapes],
        scratch_shapes=list(scratch),
        compiler_params=pltpu.CompilerParams(vmem_limit_bytes=VMEM_LIMIT),
    )(*operands)


def route(target):
    total = lax.axis_size("comp") * lax.axis_size("gy") * lax.axis_size("gx")
    group = total // SECTIONS
    pairs = []
    for moved in range(total):
        section, strip = target(moved // group, moved % group, group)
        pairs.append(((moved - 1) % total, (section * group + strip - 1) % total))
    return pairs


def partner(strip, group):
    if strip in (0, group - 1):
        return group - 1 - strip
    return strip + 1 if strip % 2 == 1 else strip - 1


def trade(value, *pairs):
    other = {}
    for a, b in pairs:
        other[a], other[b] = b, a

    def target(k, s, g):
        return (other[k], s) if k in other else (k, partner(s, g))

    return lax.ppermute(value, AXES, route(target))


def along_dynamics(value, by):
    def target(k, s, g):
        return (k, (s + by) % g) if k == 3 else (k, partner(s, g))

    return lax.ppermute(value, AXES, route(target))


def along(value, by):
    return lax.ppermute(value, AXES, route(lambda k, s, g: divmod((k * g + s + by) % (SECTIONS * g), g)))


def on_device(flow_fields, chlorophyll_lag, tracers, forcing, ocean_mask, bottom, reaction):
    levels = chlorophyll_lag.shape[0]
    nt = tracers.shape[0]
    breadth = flow_fields.shape[3]
    vmem, hbm = pltpu.VMEM, pltpu.HBM
    message = (SHARED, levels, 8, 128)
    more = (15 - SHARED, levels, 8, 128)
    to_next, to_prev, more_next, more_prev, flow, pigment, tracers, forcing = call(
        load_kernel,
        [
            (message, F32), (message, F32), (more, F32), (more, F32),
            ((4, levels, 3, 8, 128), F32), ((levels, 3, 8, 128), F32),
            (tracers.shape, F32), (forcing.shape, F32),
        ],
        (flow_fields, chlorophyll_lag, tracers, forcing),
        (hbm,) * 4,
        (pltpu.SemaphoreType.DMA((2 * levels,)),),
    )
    above = along(to_next, 1)
    below = along(to_prev, -1)
    more_above = along_dynamics(more_next, 1)
    more_below = along_dynamics(more_prev, -1)
    wet_rows, rates = call(
        mask_kernel,
        [((3, 24, 128), jnp.int32), ((nt, nt, 128), F32)],
        (ocean_mask, bottom, reaction),
        (hbm, hbm, vmem),
        (
            pltpu.VMEM((3, 8, breadth), jnp.int32),
            pltpu.VMEM((3, 8, breadth), jnp.int32),
            pltpu.SemaphoreType.DMA((6,)),
        ),
    )
    cells, winds, border = call(
        gather_kernel,
        [((nt, levels, 32, 128), F32), ((3, levels, 32, 128), F32), ((levels, 16, 128), F32)],
        (tracers, forcing, above, below, wet_rows),
        (vmem,) * 5,
    )
    inner = trade(border, (0, 1))
    outer = trade(border, (1, 2))
    exchange = ((21, 8, 128), F32)
    *sends, flow_next, partial, rim_edges, rim_wet = call(
        first_kernel,
        [
            exchange, exchange, exchange,
            ((4, levels, 3, 32, 128), F32), ((nt, levels, 16, 128), F32),
            ((levels, 8, 128), F32), ((levels, 8, 128), F32),
        ],
        (
            flow, pigment, above, below, more_above, more_below, cells, winds, wet_rows,
            rates,
        ),
        (vmem,) * 10,
        (
            *[pltpu.VMEM((4, levels, 3, 40, 128), F32) for _ in range(4)],
            pltpu.VMEM((levels, 3, 24, 128), F32),
        ),
    )
    sent = call(
        sides_kernel,
        [exchange, exchange, exchange],
        (inner, outer, *sends, partial, rim_edges, rim_wet, wet_rows),
        (vmem,) * 9,
    )
    from_b = trade(sent[1], (3, 1))
    from_a = trade(sent[0], (3, 0), (1, 2))
    from_c = trade(sent[2], (3, 2), (0, 1))
    early, tracers_next = call(
        early_kernel,
        [((4, levels, 3, 32, 128), F32), ((nt, levels, 16, 128), F32)],
        (flow_next, wet_rows, partial, inner, outer),
        (vmem,) * 5,
    )
    exchange = ((24, 8, 128), F32)
    last = call(
        second_kernel,
        [
            exchange, exchange, exchange,
            ((4, levels, 3, 8, 128), F32), ((nt, levels, 8, 128), F32),
        ],
        (from_b, from_a, from_c, early, tracers_next, wet_rows, rates),
        (vmem,) * 7,
        (
            pltpu.VMEM((levels, 3, 32, 128), F32),
            *[pltpu.VMEM((4, levels, 3, 32, 128), F32) for _ in range(2)],
            pltpu.VMEM((levels, 3, 16, 128), F32),
            pltpu.VMEM((48, 8, 128), F32),
        ),
    )
    final_b = trade(last[1], (3, 1))
    final_a = trade(last[0], (3, 0))
    final_c = trade(last[2], (3, 2))
    flow_out, tracers_out = call(
        store_kernel,
        [(flow_fields.shape, F32), (tracers.shape, F32)],
        (last[3], last[4]),
        (vmem, vmem),
        (pltpu.VMEM(tracers.shape, F32), pltpu.SemaphoreType.DMA((4,))),
        hbm,
    )
    light_out, forcing_out = call(
        last_kernel,
        [((levels, 8, breadth), F32), ((4, levels, 8, 128), F32)],
        (final_b, final_a, final_c),
        (vmem,) * 3,
    )
    return flow_out, light_out, tracers_out, forcing_out


def solution(mesh):
    rows = P(None, None, AXES, None)
    light = P(None, AXES, None)
    return jax.shard_map(
        on_device,
        mesh=mesh,
        in_specs=(rows, light, rows, rows, P(), P(), P()),
        out_specs=(rows, light, rows, rows),
        check_vma=False,
    )
```

```python
import jax
import jax.numpy as jnp
from jax import lax
from jax.experimental import pallas as pl
from jax.experimental.pallas import tpu as pltpu
from jax.sharding import PartitionSpec as P

AXES = ("comp", "gy", "gx")
SECTIONS = 4
SHARED = 10
DT = 0.1
F32 = jnp.float32
UNROLL = 6
VMEM_LIMIT = 24 * 1024 * 1024


def place():
    gy = lax.axis_size("gy")
    gx = lax.axis_size("gx")
    total = lax.axis_size("comp") * gy * gx
    group = total // SECTIONS
    position = (lax.axis_index("comp") * gy + lax.axis_index("gy")) * gx + lax.axis_index("gx")
    moved = lax.rem(position + 1, total)
    return moved // group, lax.rem(moved, group), group


def lanes(rows):
    return lax.broadcasted_iota(jnp.int32, (rows, 128), 1)


def roll_lanes(x, by):
    by = by % 128
    return x if by == 0 else pltpu.roll(x, by, 1)


def swap(x):
    return pltpu.roll(x, 4, 0)


def upper_half():
    return lax.broadcasted_iota(jnp.int32, (8, 128), 0) < 4


def spread(flag):
    return jnp.where(flag, 1.0, 0.0).astype(F32)


def edge_tile(planes):
    pair = lanes(planes[0].shape[0]) // 2
    edges = jnp.zeros_like(planes[0])
    for a, x in enumerate(planes):
        edges = jnp.where(pair == a, roll_lanes(x, 2 * a + 1), edges)
    return edges


def pack_rows(tracers, forcing, to_next, to_prev, copies):
    half = upper_half()
    nt, levels = tracers.shape[0], tracers.shape[1]

    def put(plane, pair, even, odd):
        row, col = plane // 2, 3 * (plane % 2)
        to_next[row, col + pair] = jnp.where(half, swap(even), odd)
        to_prev[row, col + pair] = jnp.where(half, even, swap(odd))

    for pair in range(levels // 2):
        even, odd = 2 * pair, 2 * pair + 1
        for copy in copies[4 * pair : 4 * pair + 4]:
            copy.wait()
        for a in range(nt):
            put(a, pair, tracers[a, even], tracers[a, odd])
        put(nt, pair, forcing[0, even], forcing[0, odd])
        put(nt + 1, pair, forcing[1, even], forcing[1, odd])
        growth = [jnp.exp(0.1 * forcing[2, l] - 0.05 * forcing[3, l]) for l in (even, odd)]
        put(nt + 2, pair, growth[0], growth[1])
        put(nt + 3, pair, jnp.zeros((8, 128), F32), jnp.zeros((8, 128), F32))


def load_kernel(
    flow, pigment, tracers, forcing,
    to_next, to_prev, more_next, more_prev, flow_in, pigment_in, tracers_in, forcing_in, sems,
):
    section, _, _ = place()
    levels = pigment.shape[0]

    @pl.when(section == 3)
    def _():
        copies = []
        for j in range(3):
            cols = slice(128 * j, 128 * j + 128)
            copies.append(
                pltpu.make_async_copy(flow.at[:, :, :, cols], flow_in.at[:, :, j], sems.at[j])
            )
            copies.append(
                pltpu.make_async_copy(pigment.at[:, :, cols], pigment_in.at[:, j], sems.at[3 + j])
            )
        for copy in copies:
            copy.start()
        for copy in copies:
            copy.wait()

        def level(l, carry):
            for f in range(5):
                for j in range(3):
                    tile = flow_in[f, l, j] if f < 4 else pigment_in[l, j]
                    row = 3 * f + j
                    if row < SHARED:
                        to_next[row, l] = tile
                        to_prev[row, l] = tile
                    else:
                        more_next[row - SHARED, l] = tile
                        more_prev[row - SHARED, l] = tile
            return carry

        lax.fori_loop(0, levels, level, 0)

    @pl.when(section != 3)
    def _():
        copies = []
        for l in range(levels):
            copies.append(
                pltpu.make_async_copy(tracers.at[:, l], tracers_in.at[:, l], sems.at[l])
            )
            copies.append(
                pltpu.make_async_copy(forcing.at[:, l], forcing_in.at[:, l], sems.at[levels + l])
            )
        for copy in copies:
            copy.start()
        pack_rows(tracers_in, forcing_in, to_next, to_prev, copies)
        more_next[...] = jnp.zeros_like(more_next)
        more_prev[...] = jnp.zeros_like(more_prev)


def mask_kernel(ocean, bottom, reaction, wet_rows, rates, ocean_rows, bottom_rows, mask_sems):
    _, strip, group = place()
    starts = [jnp.maximum(strip - 1, 0), strip, jnp.minimum(strip + 1, group - 1)]
    masks = []
    for i, start in enumerate(starts):
        rows = pl.ds(pl.multiple_of(start * 8, 8), 8)
        masks.append(pltpu.make_async_copy(ocean.at[rows], ocean_rows.at[i], mask_sems.at[i]))
        masks.append(pltpu.make_async_copy(bottom.at[rows], bottom_rows.at[i], mask_sems.at[3 + i]))
    for copy in masks:
        copy.start()
    nt = reaction.shape[0]
    for k in range(nt):
        rates[k] = jnp.broadcast_to(reaction[:, k : k + 1], (nt, 128))
    for copy in masks:
        copy.wait()
    inside = [(strip > 0).astype(jnp.int32), 1, (strip < group - 1).astype(jnp.int32)]
    for i in range(3):
        floor = jnp.where(ocean_rows[i] == 1, bottom_rows[i], 0) * inside[i]
        for j in range(3):
            wet_rows[j, 8 * i : 8 * i + 8] = floor[:, 128 * j : 128 * j + 128]


def side_columns(section, inner, outer):
    even = lanes(inner.shape[0]) % 2 == 0
    east = roll_lanes(jnp.where(section == 0, inner, outer), -1)
    west = roll_lanes(jnp.where(section == 1, inner, outer), 1)
    east = jnp.where(section < 2, east, 0.0)
    west = jnp.where(section > 0, west, 0.0)
    return jnp.where(even, east, west)


def shifted(tiles):
    lane = lanes(tiles[0].shape[0])
    left = [roll_lanes(x, 127) for x in tiles]
    right = [roll_lanes(x, 1) for x in tiles]
    count = len(tiles)
    east = [
        jnp.where(lane == 127, left[j + 1] if j + 1 < count else 0.0, left[j]) for j in range(count)
    ]
    west = [jnp.where(lane == 0, right[j - 1] if j > 0 else 0.0, right[j]) for j in range(count)]
    return east, west


def substep(source, target, heat, wet_rows, tiles, read_at, write_at, heat_at, wet_at):
    levels = target.shape[1]
    thirds = 3
    zero = jnp.zeros((8, 128), F32)

    def level(l, carry):
        slopes = []
        for tile in range(tiles):
            row = read_at + 8 * tile
            put = write_at + 8 * tile
            slope_x, slope_y = carry[tile]

            def load(f, by):
                return [source[f][l, j, row + by : row + by + 8] for j in range(thirds)]

            centre = [load(f, 0) for f in range(4)]
            up = [load(f, -1) for f in range(4)]
            down = [load(f, 1) for f in range(4)]
            sides = [shifted(centre[f]) for f in range(4)]
            new_x, new_y = [], []
            for j in range(thirds):
                u, v, t, s = (centre[f][j] for f in range(4))
                un, vn, tn, sn = (up[f][j] for f in range(4))
                us, vs, ts, ss = (down[f][j] for f in range(4))
                ue, ve, te, se = (sides[f][0][j] for f in range(4))
                uw, vw, tw, sw = (sides[f][1][j] for f in range(4))
                px = slope_x[j] + ((ss - sn) - (ts - tn))
                py = slope_y[j] + ((se - sw) - (te - tw))
                new_x.append(px)
                new_y.append(py)
                is_wet = wet_rows[j, wet_at + 8 * tile : wet_at + 8 * tile + 8] > l
                a = 0.05 - 0.05 * us
                b = 0.05 + 0.05 * un
                c = 0.05 - 0.05 * ve
                d = 0.05 + 0.05 * vw
                kept = 0.8 * t
                if heat is not None:
                    kept = kept + heat[l, j, heat_at + 8 * tile : heat_at + 8 * tile + 8]
                results = (
                    0.79 * u + 0.1 * v - 0.01 * px + 0.05 * ((un + us) + (ue + uw)),
                    0.79 * v - 0.1 * u - 0.01 * py + 0.05 * ((vn + vs) + (ve + vw)),
                    kept + ((ts * a + tn * b) + (te * c + tw * d)),
                    0.8 * s + ((ss * a + sn * b) + (se * c + sw * d)),
                )
                for f in range(4):
                    target[f, l, j, put : put + 8] = jnp.where(is_wet, results[f], 0.0)
            slopes.append((new_x, new_y))
        return slopes

    start = [([zero] * thirds, [zero] * thirds) for _ in range(tiles)]
    lax.fori_loop(0, levels, level, start, unroll=UNROLL)


def fill_heat(load, heat):
    levels, rows = heat.shape[0], heat.shape[2]
    for tile in range(rows // 8):
        for j in range(3):
            optical = jnp.zeros((8, 128), F32)
            light = jnp.ones((8, 128), F32)
            for l in range(levels):
                optical = optical + (0.05 + 0.3 * load(l, tile, j))
                lower = jnp.exp(-optical)
                heat[l, j, 8 * tile : 8 * tile + 8] = (5.0 * DT) * (light - lower)
                light = lower


def extend(own, above, below, half):
    turned = swap(own)
    return jnp.concatenate([jnp.where(half, above, turned), jnp.where(half, turned, below)], axis=0)


def tracer_weights(u_up, u_down, v_east, v_west, growth, is_wet):
    wet = spread(is_wet)
    scale = wet * 0.05
    return (
        scale - scale * u_down,
        scale + scale * u_up,
        scale - scale * v_east,
        scale + scale * v_west,
        wet * 0.8,
        (wet * DT) * growth,
    )


def tracer_level(centre, up, down, sides, weights, reaction):
    nt = len(centre)
    lane = lanes(centre[0].shape[0])
    a, b, c, d, keep, grow = weights
    results = []

    def rate(k, i):
        return jnp.broadcast_to(reaction[k, i : i + 1], centre[0].shape)

    for i in range(nt):
        side = 0.0 if sides is None else roll_lanes(sides, -2 * i - 1)
        east = jnp.where(lane == 127, side, roll_lanes(centre[i], 127))
        west = jnp.where(lane == 0, side, roll_lanes(centre[i], 1))
        mixed = rate(0, i) * centre[0]
        for k in range(1, nt):
            mixed = mixed + rate(k, i) * centre[k]
        results.append(
            (keep * centre[i] + grow * mixed)
            + ((down[i] * a + up[i] * b) + (east * c + west * d))
        )
    return results


def pigment_of(first, second):
    return 0.25 * (first * first + second * second)


def gather_kernel(tracers, forcing, above, below, wet_rows, cells, winds, border):
    section, strip, group = place()
    nt, levels = tracers.shape[0], tracers.shape[1]
    low = spread(strip > 0)
    high = spread(strip < group - 1)

    @pl.when(section == 3)
    def _():
        border[...] = jnp.zeros_like(border)

    @pl.when(section != 3)
    def _():
        half = upper_half()

        def halo(message, plane, pair, odd, upward):
            tile = message[plane // 2, 3 * (plane % 2) + pair]
            return swap(tile) if odd != upward else tile

        def build(plane, own, l, masked):
            pair, odd = l // 2, l % 2 == 1
            up = halo(above, plane, pair, odd, False)
            down = halo(below, plane, pair, not odd, False)
            if masked:
                up, down = up * low, down * high
            return extend(own, up, down, half)

        lane = lanes(16)
        for l in range(levels):
            v = build(nt + 1, forcing[1, l], l, False)
            scale = 0.05 + jnp.where(lane == 0, -0.05, 0.05) * v
            products = []
            for a in range(nt):
                cell = build(a, tracers[a, l], l, True)
                cells[a, l, 8:24] = cell
                products.append(scale * cell)
            winds[0, l, 8:24] = build(nt, forcing[0, l], l, False)
            winds[1, l, 8:24] = v
            growth = jnp.exp(0.1 * forcing[2, l] - 0.05 * forcing[3, l])
            winds[2, l, 8:24] = build(nt + 2, growth, l, False)
            border[l] = edge_tile(products)


def first_kernel(
    flow, pigment, above, below, more_above, more_below, cells, winds, wet_rows, reaction,
    send_a, send_b, send_c, flow_next, partial, rim_edges, rim_wet,
    field_0, field_1, field_2, field_3, heat,
):
    section, strip, group = place()
    levels = pigment.shape[0]
    nt = cells.shape[0]
    low = spread(strip > 0)
    high = spread(strip < group - 1)

    @pl.when(section == 3)
    def _():
        def over(row, l):
            return above[row, l] if row < SHARED else more_above[row - SHARED, l]

        def under(row, l):
            return below[row, l] if row < SHARED else more_below[row - SHARED, l]

        def fill(l, carry):
            for f in range(4):
                for j in range(3):
                    field_0[f, l, j, 8:16] = over(3 * f + j, l) * low
                    field_0[f, l, j, 16:24] = flow[f, l, j]
                    field_0[f, l, j, 24:32] = under(3 * f + j, l) * high
            return carry

        lax.fori_loop(0, levels, fill, 0)

        def load(l, tile, j):
            if tile == 1:
                return pigment[l, j]
            return (over if tile == 0 else under)(12 + j, l)

        fill_heat(load, heat)
        substep(planes(field_0), field_1, heat, wet_rows, 3, 8, 8, 0, 0)
        substep(planes(field_1), field_2, heat, wet_rows, 3, 8, 8, 0, 0)
        substep(planes(field_2), field_3, heat, wet_rows, 3, 8, 8, 0, 0)
        substep(planes(field_3), flow_next, heat, wet_rows, 2, 12, 8, 4, 4)
        lane = lanes(8)
        outs = (send_a, send_b, send_c)
        sub = lax.broadcasted_iota(jnp.int32, (8, 128), 0)

        def mean(f, l, row, j):
            total = field_1[f, l, j, row : row + 8] + field_2[f, l, j, row : row + 8]
            total = total + field_3[f, l, j, row : row + 8]
            return 0.25 * (total + flow_next[f, l, j, row - 4 : row + 4])

        edge_v = [jnp.zeros((8, 128), F32) for _ in range(3)]
        rows_above = [jnp.zeros((8, 128), F32) for _ in range(3)]
        rows_below = [jnp.zeros((8, 128), F32) for _ in range(3)]
        for l in range(levels):
            v_mean = []
            for j in range(3):
                outs[j][l] = mean(0, l, 16, j)
                v_mean.append(mean(1, l, 16, j))
                outs[j][6 + l] = v_mean[j]
                warm = flow_next[2, l, j, 12:20]
                salt = flow_next[3, l, j, 12:20]
                outs[j][12 + l] = jnp.exp(0.1 * warm - 0.05 * salt)
                first = mean(0, l, 15, j)
                last = mean(0, l, 17, j)
                rows_above[j] = jnp.where(sub == l, roll_rows(first, l), rows_above[j])
                rows_below[j] = jnp.where(sub == l, roll_rows(last, l + 1), rows_below[j])
            for j in range(3):
                if j > 0:
                    edge_v[j] = jnp.where(
                        lane == 2 * l, roll_lanes(v_mean[j - 1], 2 * l + 1), edge_v[j]
                    )
                if j < 2:
                    edge_v[j] = jnp.where(
                        lane == 2 * l + 1, roll_lanes(v_mean[j + 1], 2 * l + 1), edge_v[j]
                    )
        for j in range(3):
            outs[j][18] = edge_v[j]
            outs[j][19] = rows_above[j]
            outs[j][20] = rows_below[j]

    @pl.when(section != 3)
    def _():
        floor = wet_rows[section, 4:20]

        def level(l, carry):
            v = winds[1, l, 8:24]
            weights = tracer_weights(
                winds[0, l, 7:23], winds[0, l, 9:25], roll_lanes(v, 127), roll_lanes(v, 1),
                winds[2, l, 8:24], floor > l,
            )
            results = tracer_level(
                [cells[a, l, 8:24] for a in range(nt)],
                [cells[a, l, 7:23] for a in range(nt)],
                [cells[a, l, 9:25] for a in range(nt)],
                None, weights, reaction,
            )
            for a in range(nt):
                partial[a, l] = results[a]
            rim_edges[l] = edge_tile([partial[a, l, 4:12] for a in range(nt)])
            wet = spread(wet_rows[section, 8:16] > l)
            first = jnp.broadcast_to(wet[:, :1], (8, 128))
            last = jnp.broadcast_to(wet[:, 127:], (8, 128))
            rim_wet[l] = jnp.where(lanes(8) % 2 == 0, last, first)
            return carry

        lax.fori_loop(0, levels, level, 0)


def sides_kernel(
    outer, inner, send_a, send_b, send_c, partial, rim_edges, rim_wet, wet_rows,
    out_a, out_b, out_c,
):
    section, _, _ = place()
    levels = partial.shape[1]
    outs = (out_a, out_b, out_c)

    @pl.when(section == 3)
    def _():
        for out, send in zip(outs, (send_a, send_b, send_c)):
            out[...] = send[...]

    @pl.when(section != 3)
    def _():
        floor = wet_rows[section, 4:20]
        lane = lanes(16)
        rim = (lane == 0) | (lane == 127)
        row = lax.broadcasted_iota(jnp.int32, (16, 128), 0)
        inside = (row > 0) & (row < 15)
        for l in range(levels):
            sides = side_columns(section, inner[l], outer[l])
            wet_rim = rim & (floor > l)
            pair = [
                partial[a, l] + jnp.where(wet_rim, roll_lanes(sides, -2 * a - 1), 0.0)
                for a in range(2)
            ]
            own = side_columns(section, inner[l, 4:12], outer[l, 4:12])
            edge = rim_edges[l] + jnp.where(rim_wet[l] > 0.0, own, 0.0)
            shade = jnp.where(inside, pigment_of(pair[0], pair[1]), 0.0)
            for out in outs:
                out[2 * l] = shade[:8]
                out[2 * l + 1] = shade[8:]
                out[12 + l] = edge
        for out in outs:
            for i in range(18, 21):
                out[i] = jnp.zeros((8, 128), F32)


def roll_rows(x, by):
    by = by % 8
    return x if by == 0 else pltpu.roll(x, by, 0)


def planes(buffer):
    return [buffer.at[f] for f in range(4)]


def early_kernel(flow_next, wet_rows, partial, outer, inner, early, tracers_next):
    section, _, _ = place()
    nt, levels = partial.shape[0], partial.shape[1]

    @pl.when(section != 3)
    def _():
        floor = wet_rows[section, 4:20]
        lane = lanes(16)
        rim = (lane == 0) | (lane == 127)

        def level(l, carry):
            sides = side_columns(section, inner[l], outer[l])
            wet_rim = rim & (floor > l)
            for a in range(nt):
                side = jnp.where(wet_rim, roll_lanes(sides, -2 * a - 1), 0.0)
                tracers_next[a, l] = partial[a, l] + side
            return carry

        lax.fori_loop(0, levels, level, 0, unroll=2)

    @pl.when(section == 3)
    def _():
        substep(planes(flow_next), early, None, wet_rows, 2, 8, 8, 0, 4)


def second_kernel(
    from_b, from_a, from_c, early, tracers_next, wet_rows, reaction,
    out_a, out_b, out_c, flow_last, tracers_last, warm, field_1, field_2, heat, winds,
):
    section, _, _ = place()
    levels = heat.shape[0]
    nt = tracers_next.shape[0]

    @pl.when(section == 3)
    def _():
        shades = (from_a, from_b, from_c)

        def load(l, tile, j):
            return shades[j][2 * l + tile]

        fill_heat(load, heat)

        def warm_up(l, carry):
            for j in range(3):
                heated = jnp.where(wet_rows[j, 4:20] > l, heat[l, j], 0.0)
                warm[l, j, 8:24] = early[2, l, j, 8:24] + heated
            return carry

        lax.fori_loop(0, levels, warm_up, 0)
        first = planes(early)
        first[2] = warm
        substep(first, field_1, heat, wet_rows, 2, 8, 8, 0, 4)
        substep(planes(field_1), field_2, heat, wet_rows, 2, 8, 8, 0, 4)
        substep(planes(field_2), flow_last, heat, wet_rows, 1, 12, 0, 4, 8)
        outs = (out_a, out_b, out_c)
        for l in range(levels):
            for j in range(3):
                for f in range(2):
                    total = early[f, l, j, 12:20] + field_1[f, l, j, 12:20]
                    total = total + field_2[f, l, j, 12:20]
                    outs[j][6 * f + l] = 0.25 * (total + flow_last[f, l, j])
                outs[j][12 + l] = flow_last[2, l, j]
                outs[j][18 + l] = flow_last[3, l, j]

    @pl.when(section != 3)
    def _():
        def driven(i):
            return jnp.where(
                section == 0, from_a[i], jnp.where(section == 1, from_b[i], from_c[i])
            )

        for i in range(18):
            winds[i] = driven(i)
        edge_v = driven(18)
        rows_above = driven(19)
        rows_below = driven(20)
        lane = lanes(8)
        sub = lax.broadcasted_iota(jnp.int32, (8, 128), 0)
        for l in range(levels):
            u, v = winds[l], winds[6 + l]
            winds[18 + l] = jnp.where(sub == 0, roll_rows(rows_above, -l), roll_rows(u, 1))
            winds[24 + l] = jnp.where(sub == 7, roll_rows(rows_below, 7 - l), roll_rows(u, 7))
            winds[30 + l] = jnp.where(
                lane == 127, roll_lanes(edge_v, 126 - 2 * l), roll_lanes(v, 127)
            )
            winds[36 + l] = jnp.where(lane == 0, roll_lanes(edge_v, -2 * l), roll_lanes(v, 1))
            winds[42 + l] = side_columns(section, from_c[12 + l], from_a[12 + l])
        floor = wet_rows[section, 8:16]

        def level(l, carry):
            weights = tracer_weights(
                winds[18 + l], winds[24 + l], winds[30 + l], winds[36 + l], winds[12 + l], floor > l
            )
            results = tracer_level(
                [tracers_next[a, l, 4:12] for a in range(nt)],
                [tracers_next[a, l, 3:11] for a in range(nt)],
                [tracers_next[a, l, 5:13] for a in range(nt)],
                winds[42 + l], weights, reaction,
            )
            for a in range(nt):
                tracers_last[a, l] = results[a]
            shade = pigment_of(results[0], results[1])
            for out in (out_a, out_b, out_c):
                out[l] = shade
                for i in range(1, 4):
                    out[6 * i + l] = jnp.zeros((8, 128), F32)
            return carry

        lax.fori_loop(0, levels, level, 0)


def store_kernel(flow_last, tracers_last, flow_out, tracers_out, blank, sems):
    section, _, _ = place()
    blank[...] = jnp.zeros_like(blank)

    def put(flow_of, tracers_from):
        copies = [pltpu.make_async_copy(tracers_from, tracers_out, sems.at[3])]
        for j in range(3):
            target = flow_out.at[:, :, :, 128 * j : 128 * j + 128]
            copies.append(pltpu.make_async_copy(flow_of(j), target, sems.at[j]))
        for copy in copies:
            copy.start()
        for copy in copies:
            copy.wait()

    @pl.when(section == 3)
    def _():
        put(lambda j: flow_last.at[:, :, j], blank)

    @pl.when(section != 3)
    def _():
        put(lambda j: blank.at[0:4], tracers_last)


def last_kernel(from_b, from_a, from_c, light_out, forcing_out):
    section, _, _ = place()
    levels = light_out.shape[0]
    is_dynamics = section == 3
    for l in range(levels):
        for j, shade in enumerate((from_a, from_b, from_c)):
            light_out[l, :, 128 * j : 128 * j + 128] = jnp.where(is_dynamics, shade[l], 0.0)
        for f in range(4):
            i = 6 * f + l
            picked = jnp.where(
                section == 0, from_a[i], jnp.where(section == 1, from_b[i], from_c[i])
            )
            forcing_out[f, l] = jnp.where(is_dynamics, 0.0, picked)


def call(kernel, shapes, operands, spaces, scratch=(), out_space=pltpu.VMEM):
    operands = [
        pltpu.with_memory_space_constraint(x, pltpu.HBM) if space == pltpu.HBM else x
        for x, space in zip(operands, spaces)
    ]
    return pl.pallas_call(
        kernel,
        out_shape=[jax.ShapeDtypeStruct(shape, dtype) for shape, dtype in shapes],
        in_specs=[pl.BlockSpec(memory_space=space) for space in spaces],
        out_specs=[pl.BlockSpec(memory_space=out_space) for _ in shapes],
        scratch_shapes=list(scratch),
        compiler_params=pltpu.CompilerParams(vmem_limit_bytes=VMEM_LIMIT),
    )(*operands)


def route(target):
    total = lax.axis_size("comp") * lax.axis_size("gy") * lax.axis_size("gx")
    group = total // SECTIONS
    pairs = []
    for moved in range(total):
        section, strip = target(moved // group, moved % group, group)
        pairs.append(((moved - 1) % total, (section * group + strip - 1) % total))
    return pairs


def partner(strip, group):
    if strip in (0, group - 1):
        return group - 1 - strip
    return strip + 1 if strip % 2 == 1 else strip - 1


def trade(value, *pairs):
    other = {}
    for a, b in pairs:
        other[a], other[b] = b, a

    def target(k, s, g):
        return (other[k], s) if k in other else (k, partner(s, g))

    return lax.ppermute(value, AXES, route(target))


def along_dynamics(value, by):
    def target(k, s, g):
        return (k, (s + by) % g) if k == 3 else (k, partner(s, g))

    return lax.ppermute(value, AXES, route(target))


def along(value, by):
    return lax.ppermute(value, AXES, route(lambda k, s, g: divmod((k * g + s + by) % (SECTIONS * g), g)))


def on_device(flow_fields, chlorophyll_lag, tracers, forcing, ocean_mask, bottom, reaction):
    levels = chlorophyll_lag.shape[0]
    nt = tracers.shape[0]
    breadth = flow_fields.shape[3]
    vmem, hbm = pltpu.VMEM, pltpu.HBM
    message = (SHARED, levels, 8, 128)
    more = (15 - SHARED, levels, 8, 128)
    to_next, to_prev, more_next, more_prev, flow, pigment, tracers, forcing = call(
        load_kernel,
        [
            (message, F32), (message, F32), (more, F32), (more, F32),
            ((4, levels, 3, 8, 128), F32), ((levels, 3, 8, 128), F32),
            (tracers.shape, F32), (forcing.shape, F32),
        ],
        (flow_fields, chlorophyll_lag, tracers, forcing),
        (hbm,) * 4,
        (pltpu.SemaphoreType.DMA((2 * levels,)),),
    )
    above = along(to_next, 1)
    below = along(to_prev, -1)
    more_above = along_dynamics(more_next, 1)
    more_below = along_dynamics(more_prev, -1)
    wet_rows, rates = call(
        mask_kernel,
        [((3, 24, 128), jnp.int32), ((nt, nt, 128), F32)],
        (ocean_mask, bottom, reaction),
        (hbm, hbm, vmem),
        (
            pltpu.VMEM((3, 8, breadth), jnp.int32),
            pltpu.VMEM((3, 8, breadth), jnp.int32),
            pltpu.SemaphoreType.DMA((6,)),
        ),
    )
    cells, winds, border = call(
        gather_kernel,
        [((nt, levels, 32, 128), F32), ((3, levels, 32, 128), F32), ((levels, 16, 128), F32)],
        (tracers, forcing, above, below, wet_rows),
        (vmem,) * 5,
    )
    inner = trade(border, (0, 1))
    outer = trade(border, (1, 2))
    exchange = ((21, 8, 128), F32)
    *sends, flow_next, partial, rim_edges, rim_wet = call(
        first_kernel,
        [
            exchange, exchange, exchange,
            ((4, levels, 3, 32, 128), F32), ((nt, levels, 16, 128), F32),
            ((levels, 8, 128), F32), ((levels, 8, 128), F32),
        ],
        (
            flow, pigment, above, below, more_above, more_below, cells, winds, wet_rows,
            rates,
        ),
        (vmem,) * 10,
        (
            *[pltpu.VMEM((4, levels, 3, 40, 128), F32) for _ in range(4)],
            pltpu.VMEM((levels, 3, 24, 128), F32),
        ),
    )
    sent = call(
        sides_kernel,
        [exchange, exchange, exchange],
        (outer, inner, *sends, partial, rim_edges, rim_wet, wet_rows),
        (vmem,) * 9,
    )
    from_b = trade(sent[1], (3, 1))
    from_a = trade(sent[0], (3, 0), (1, 2))
    from_c = trade(sent[2], (3, 2), (0, 1))
    early, tracers_next = call(
        early_kernel,
        [((4, levels, 3, 32, 128), F32), ((nt, levels, 16, 128), F32)],
        (flow_next, wet_rows, partial, outer, inner),
        (vmem,) * 5,
    )
    exchange = ((24, 8, 128), F32)
    last = call(
        second_kernel,
        [
            exchange, exchange, exchange,
            ((4, levels, 3, 8, 128), F32), ((nt, levels, 8, 128), F32),
        ],
        (from_b, from_a, from_c, early, tracers_next, wet_rows, rates),
        (vmem,) * 7,
        (
            pltpu.VMEM((levels, 3, 32, 128), F32),
            *[pltpu.VMEM((4, levels, 3, 32, 128), F32) for _ in range(2)],
            pltpu.VMEM((levels, 3, 16, 128), F32),
            pltpu.VMEM((48, 8, 128), F32),
        ),
    )
    final_b = trade(last[1], (3, 1))
    final_a = trade(last[0], (3, 0))
    final_c = trade(last[2], (3, 2))
    flow_out, tracers_out = call(
        store_kernel,
        [(flow_fields.shape, F32), (tracers.shape, F32)],
        (last[3], last[4]),
        (vmem, vmem),
        (pltpu.VMEM(tracers.shape, F32), pltpu.SemaphoreType.DMA((4,))),
        hbm,
    )
    light_out, forcing_out = call(
        last_kernel,
        [((levels, 8, breadth), F32), ((4, levels, 8, 128), F32)],
        (final_b, final_a, final_c),
        (vmem,) * 3,
    )
    return flow_out, light_out, tracers_out, forcing_out


def solution(mesh):
    rows = P(None, None, AXES, None)
    light = P(None, AXES, None)
    return jax.shard_map(
        on_device,
        mesh=mesh,
        in_specs=(rows, light, rows, rows, P(), P(), P()),
        out_specs=(rows, light, rows, rows),
        check_vma=False,
    )
```

```python
import jax
import jax.numpy as jnp
from jax import lax
from jax.experimental import pallas as pl
from jax.experimental.pallas import tpu as pltpu
from jax.sharding import PartitionSpec as P

AXES = ("comp", "gy", "gx")
SECTIONS = 4
SHARED = 10
DT = 0.1
F32 = jnp.float32
UNROLL = 6
VMEM_LIMIT = 24 * 1024 * 1024


def place():
    gy = lax.axis_size("gy")
    gx = lax.axis_size("gx")
    total = lax.axis_size("comp") * gy * gx
    group = total // SECTIONS
    position = (lax.axis_index("comp") * gy + lax.axis_index("gy")) * gx + lax.axis_index("gx")
    moved = lax.rem(position + 1, total)
    return moved // group, lax.rem(moved, group), group


def lanes(rows):
    return lax.broadcasted_iota(jnp.int32, (rows, 128), 1)


def roll_lanes(x, by):
    by = by % 128
    return x if by == 0 else pltpu.roll(x, by, 1)


def swap(x):
    return pltpu.roll(x, 4, 0)


def upper_half():
    return lax.broadcasted_iota(jnp.int32, (8, 128), 0) < 4


def spread(flag):
    return jnp.where(flag, 1.0, 0.0).astype(F32)


def edge_tile(planes):
    pair = lanes(planes[0].shape[0]) // 2
    edges = jnp.zeros_like(planes[0])
    for a, x in enumerate(planes):
        edges = jnp.where(pair == a, roll_lanes(x, 2 * a + 1), edges)
    return edges


def pack_rows(tracers, forcing, to_next, to_prev, copies):
    half = upper_half()
    nt, levels = tracers.shape[0], tracers.shape[1]

    def put(plane, pair, even, odd):
        row, col = plane // 2, 3 * (plane % 2)
        to_next[row, col + pair] = jnp.where(half, swap(even), odd)
        to_prev[row, col + pair] = jnp.where(half, even, swap(odd))

    for pair in range(levels // 2):
        even, odd = 2 * pair, 2 * pair + 1
        for copy in copies[4 * pair : 4 * pair + 4]:
            copy.wait()
        for a in range(nt):
            put(a, pair, tracers[a, even], tracers[a, odd])
        put(nt, pair, forcing[0, even], forcing[0, odd])
        put(nt + 1, pair, forcing[1, even], forcing[1, odd])
        growth = [jnp.exp(0.1 * forcing[2, l] - 0.05 * forcing[3, l]) for l in (even, odd)]
        put(nt + 2, pair, growth[0], growth[1])
        put(nt + 3, pair, jnp.zeros((8, 128), F32), jnp.zeros((8, 128), F32))


def load_kernel(
    flow, pigment, tracers, forcing,
    to_next, to_prev, more_next, more_prev, flow_in, pigment_in, tracers_in, forcing_in, sems,
):
    section, _, _ = place()
    levels = pigment.shape[0]

    @pl.when(section == 3)
    def _():
        copies = []
        for j in range(3):
            cols = slice(128 * j, 128 * j + 128)
            copies.append(
                pltpu.make_async_copy(flow.at[:, :, :, cols], flow_in.at[:, :, j], sems.at[j])
            )
            copies.append(
                pltpu.make_async_copy(pigment.at[:, :, cols], pigment_in.at[:, j], sems.at[3 + j])
            )
        for copy in copies:
            copy.start()
        for copy in copies:
            copy.wait()

        def level(l, carry):
            for f in range(5):
                for j in range(3):
                    tile = flow_in[f, l, j] if f < 4 else pigment_in[l, j]
                    row = 3 * f + j
                    if row < SHARED:
                        to_next[row, l] = tile
                        to_prev[row, l] = tile
                    else:
                        more_next[row - SHARED, l] = tile
                        more_prev[row - SHARED, l] = tile
            return carry

        lax.fori_loop(0, levels, level, 0)

    @pl.when(section != 3)
    def _():
        copies = []
        for l in range(levels):
            copies.append(
                pltpu.make_async_copy(tracers.at[:, l], tracers_in.at[:, l], sems.at[l])
            )
            copies.append(
                pltpu.make_async_copy(forcing.at[:, l], forcing_in.at[:, l], sems.at[levels + l])
            )
        for copy in copies:
            copy.start()
        pack_rows(tracers_in, forcing_in, to_next, to_prev, copies)
        more_next[...] = jnp.zeros_like(more_next)
        more_prev[...] = jnp.zeros_like(more_prev)


def mask_kernel(ocean, bottom, reaction, wet_rows, rates, ocean_rows, bottom_rows, mask_sems):
    _, strip, group = place()
    starts = [jnp.maximum(strip - 1, 0), strip, jnp.minimum(strip + 1, group - 1)]
    masks = []
    for i, start in enumerate(starts):
        rows = pl.ds(pl.multiple_of(start * 8, 8), 8)
        masks.append(pltpu.make_async_copy(ocean.at[rows], ocean_rows.at[i], mask_sems.at[i]))
        masks.append(pltpu.make_async_copy(bottom.at[rows], bottom_rows.at[i], mask_sems.at[3 + i]))
    for copy in masks:
        copy.start()
    nt = reaction.shape[0]
    for k in range(nt):
        rates[k] = jnp.broadcast_to(reaction[:, k : k + 1], (nt, 128))
    for copy in masks:
        copy.wait()
    inside = [(strip > 0).astype(jnp.int32), 1, (strip < group - 1).astype(jnp.int32)]
    for i in range(3):
        floor = jnp.where(ocean_rows[i] == 1, bottom_rows[i], 0) * inside[i]
        for j in range(3):
            wet_rows[j, 8 * i : 8 * i + 8] = floor[:, 128 * j : 128 * j + 128]


def side_columns(section, inner, outer):
    even = lanes(inner.shape[0]) % 2 == 0
    east = roll_lanes(jnp.where(section == 0, inner, outer), -1)
    west = roll_lanes(jnp.where(section == 1, inner, outer), 1)
    east = jnp.where(section < 2, east, 0.0)
    west = jnp.where(section > 0, west, 0.0)
    return jnp.where(even, east, west)


def shifted(tiles):
    lane = lanes(tiles[0].shape[0])
    left = [roll_lanes(x, 127) for x in tiles]
    right = [roll_lanes(x, 1) for x in tiles]
    count = len(tiles)
    east = [
        jnp.where(lane == 127, left[j + 1] if j + 1 < count else 0.0, left[j]) for j in range(count)
    ]
    west = [jnp.where(lane == 0, right[j - 1] if j > 0 else 0.0, right[j]) for j in range(count)]
    return east, west


def substep(source, target, heat, wet_rows, tiles, read_at, write_at, heat_at, wet_at):
    levels = target.shape[1]
    thirds = 3
    zero = jnp.zeros((8, 128), F32)

    def level(l, carry):
        slopes = []
        for tile in range(tiles):
            row = read_at + 8 * tile
            put = write_at + 8 * tile
            slope_x, slope_y = carry[tile]

            def load(f, by):
                return [source[f][l, j, row + by : row + by + 8] for j in range(thirds)]

            centre = [load(f, 0) for f in range(4)]
            up = [load(f, -1) for f in range(4)]
            down = [load(f, 1) for f in range(4)]
            sides = [shifted(centre[f]) for f in range(4)]
            new_x, new_y = [], []
            for j in range(thirds):
                u, v, t, s = (centre[f][j] for f in range(4))
                un, vn, tn, sn = (up[f][j] for f in range(4))
                us, vs, ts, ss = (down[f][j] for f in range(4))
                ue, ve, te, se = (sides[f][0][j] for f in range(4))
                uw, vw, tw, sw = (sides[f][1][j] for f in range(4))
                px = slope_x[j] + ((ss - sn) - (ts - tn))
                py = slope_y[j] + ((se - sw) - (te - tw))
                new_x.append(px)
                new_y.append(py)
                is_wet = wet_rows[j, wet_at + 8 * tile : wet_at + 8 * tile + 8] > l
                a = 0.05 - 0.05 * us
                b = 0.05 + 0.05 * un
                c = 0.05 - 0.05 * ve
                d = 0.05 + 0.05 * vw
                kept = 0.8 * t
                if heat is not None:
                    kept = kept + heat[l, j, heat_at + 8 * tile : heat_at + 8 * tile + 8]
                results = (
                    0.79 * u + 0.1 * v - 0.01 * px + 0.05 * ((un + us) + (ue + uw)),
                    0.79 * v - 0.1 * u - 0.01 * py + 0.05 * ((vn + vs) + (ve + vw)),
                    kept + ((ts * a + tn * b) + (te * c + tw * d)),
                    0.8 * s + ((ss * a + sn * b) + (se * c + sw * d)),
                )
                for f in range(4):
                    target[f, l, j, put : put + 8] = jnp.where(is_wet, results[f], 0.0)
            slopes.append((new_x, new_y))
        return slopes

    start = [([zero] * thirds, [zero] * thirds) for _ in range(tiles)]
    lax.fori_loop(0, levels, level, start, unroll=UNROLL)


def fill_heat(load, heat):
    levels, rows = heat.shape[0], heat.shape[2]
    for tile in range(rows // 8):
        for j in range(3):
            optical = jnp.zeros((8, 128), F32)
            light = jnp.ones((8, 128), F32)
            for l in range(levels):
                optical = optical + (0.05 + 0.3 * load(l, tile, j))
                lower = jnp.exp(-optical)
                heat[l, j, 8 * tile : 8 * tile + 8] = (5.0 * DT) * (light - lower)
                light = lower


def extend(own, above, below, half):
    turned = swap(own)
    return jnp.concatenate([jnp.where(half, above, turned), jnp.where(half, turned, below)], axis=0)


def tracer_weights(u_up, u_down, v_east, v_west, growth, is_wet):
    wet = spread(is_wet)
    scale = wet * 0.05
    return (
        scale - scale * u_down,
        scale + scale * u_up,
        scale - scale * v_east,
        scale + scale * v_west,
        wet * 0.8,
        (wet * DT) * growth,
    )


def tracer_level(centre, up, down, sides, weights, reaction):
    nt = len(centre)
    lane = lanes(centre[0].shape[0])
    a, b, c, d, keep, grow = weights
    results = []

    def rate(k, i):
        return jnp.broadcast_to(reaction[k, i : i + 1], centre[0].shape)

    for i in range(nt):
        side = 0.0 if sides is None else roll_lanes(sides, -2 * i - 1)
        east = jnp.where(lane == 127, side, roll_lanes(centre[i], 127))
        west = jnp.where(lane == 0, side, roll_lanes(centre[i], 1))
        mixed = rate(0, i) * centre[0]
        for k in range(1, nt):
            mixed = mixed + rate(k, i) * centre[k]
        results.append(
            (keep * centre[i] + grow * mixed)
            + ((down[i] * a + up[i] * b) + (east * c + west * d))
        )
    return results


def pigment_of(first, second):
    return 0.25 * (first * first + second * second)


def gather_kernel(tracers, forcing, above, below, wet_rows, cells, winds, border):
    section, strip, group = place()
    nt, levels = tracers.shape[0], tracers.shape[1]
    low = spread(strip > 0)
    high = spread(strip < group - 1)

    @pl.when(section == 3)
    def _():
        border[...] = jnp.zeros_like(border)

    @pl.when(section != 3)
    def _():
        half = upper_half()

        def halo(message, plane, pair, odd, upward):
            tile = message[plane // 2, 3 * (plane % 2) + pair]
            return swap(tile) if odd != upward else tile

        def build(plane, own, l, masked):
            pair, odd = l // 2, l % 2 == 1
            up = halo(above, plane, pair, odd, False)
            down = halo(below, plane, pair, not odd, False)
            if masked:
                up, down = up * low, down * high
            return extend(own, up, down, half)

        lane = lanes(16)
        for l in range(levels):
            v = build(nt + 1, forcing[1, l], l, False)
            scale = 0.05 + jnp.where(lane == 0, -0.05, 0.05) * v
            products = []
            for a in range(nt):
                cell = build(a, tracers[a, l], l, True)
                cells[a, l, 8:24] = cell
                products.append(scale * cell)
            winds[0, l, 8:24] = build(nt, forcing[0, l], l, False)
            winds[1, l, 8:24] = v
            growth = jnp.exp(0.1 * forcing[2, l] - 0.05 * forcing[3, l])
            winds[2, l, 8:24] = build(nt + 2, growth, l, False)
            border[l] = edge_tile(products)


def first_kernel(
    flow, pigment, above, below, more_above, more_below, cells, winds, wet_rows, reaction,
    send_a, send_b, send_c, flow_next, partial, rim_edges, rim_wet,
    field_0, field_1, field_2, field_3, heat,
):
    section, strip, group = place()
    levels = pigment.shape[0]
    nt = cells.shape[0]
    low = spread(strip > 0)
    high = spread(strip < group - 1)

    @pl.when(section == 3)
    def _():
        def over(row, l):
            return above[row, l] if row < SHARED else more_above[row - SHARED, l]

        def under(row, l):
            return below[row, l] if row < SHARED else more_below[row - SHARED, l]

        def fill(l, carry):
            for f in range(4):
                for j in range(3):
                    field_0[f, l, j, 8:16] = over(3 * f + j, l) * low
                    field_0[f, l, j, 16:24] = flow[f, l, j]
                    field_0[f, l, j, 24:32] = under(3 * f + j, l) * high
            return carry

        lax.fori_loop(0, levels, fill, 0)

        def load(l, tile, j):
            if tile == 1:
                return pigment[l, j]
            return (over if tile == 0 else under)(12 + j, l)

        fill_heat(load, heat)
        substep(planes(field_0), field_1, heat, wet_rows, 3, 8, 8, 0, 0)
        substep(planes(field_1), field_2, heat, wet_rows, 3, 8, 8, 0, 0)
        substep(planes(field_2), field_3, heat, wet_rows, 3, 8, 8, 0, 0)
        substep(planes(field_3), flow_next, heat, wet_rows, 2, 12, 8, 4, 4)
        lane = lanes(8)
        outs = (send_a, send_b, send_c)
        sub = lax.broadcasted_iota(jnp.int32, (8, 128), 0)

        def mean(f, l, row, j):
            total = field_1[f, l, j, row : row + 8] + field_2[f, l, j, row : row + 8]
            total = total + field_3[f, l, j, row : row + 8]
            return 0.25 * (total + flow_next[f, l, j, row - 4 : row + 4])

        edge_v = [jnp.zeros((8, 128), F32) for _ in range(3)]
        rows_above = [jnp.zeros((8, 128), F32) for _ in range(3)]
        rows_below = [jnp.zeros((8, 128), F32) for _ in range(3)]
        for l in range(levels):
            v_mean = []
            for j in range(3):
                outs[j][l] = mean(0, l, 16, j)
                v_mean.append(mean(1, l, 16, j))
                outs[j][6 + l] = v_mean[j]
                warm = flow_next[2, l, j, 12:20]
                salt = flow_next[3, l, j, 12:20]
                outs[j][12 + l] = jnp.exp(0.1 * warm - 0.05 * salt)
                first = mean(0, l, 15, j)
                last = mean(0, l, 17, j)
                rows_above[j] = jnp.where(sub == l, roll_rows(first, l), rows_above[j])
                rows_below[j] = jnp.where(sub == l, roll_rows(last, l + 1), rows_below[j])
            for j in range(3):
                if j > 0:
                    edge_v[j] = jnp.where(
                        lane == 2 * l, roll_lanes(v_mean[j - 1], 2 * l + 1), edge_v[j]
                    )
                if j < 2:
                    edge_v[j] = jnp.where(
                        lane == 2 * l + 1, roll_lanes(v_mean[j + 1], 2 * l + 1), edge_v[j]
                    )
        for j in range(3):
            outs[j][18] = edge_v[j]
            outs[j][19] = rows_above[j]
            outs[j][20] = rows_below[j]

    @pl.when(section != 3)
    def _():
        floor = wet_rows[section, 4:20]

        def level(l, carry):
            v = winds[1, l, 8:24]
            weights = tracer_weights(
                winds[0, l, 7:23], winds[0, l, 9:25], roll_lanes(v, 127), roll_lanes(v, 1),
                winds[2, l, 8:24], floor > l,
            )
            results = tracer_level(
                [cells[a, l, 8:24] for a in range(nt)],
                [cells[a, l, 7:23] for a in range(nt)],
                [cells[a, l, 9:25] for a in range(nt)],
                None, weights, reaction,
            )
            for a in range(nt):
                partial[a, l] = results[a]
            rim_edges[l] = edge_tile([partial[a, l, 4:12] for a in range(nt)])
            wet = spread(wet_rows[section, 8:16] > l)
            first = jnp.broadcast_to(wet[:, :1], (8, 128))
            last = jnp.broadcast_to(wet[:, 127:], (8, 128))
            rim_wet[l] = jnp.where(lanes(8) % 2 == 0, last, first)
            return carry

        lax.fori_loop(0, levels, level, 0)


def sides_kernel(
    outer, inner, send_a, send_b, send_c, partial, rim_edges, rim_wet, wet_rows,
    out_a, out_b, out_c,
):
    section, _, _ = place()
    levels = partial.shape[1]
    outs = (out_a, out_b, out_c)

    @pl.when(section == 3)
    def _():
        for out, send in zip(outs, (send_a, send_b, send_c)):
            out[...] = send[...]

    @pl.when(section != 3)
    def _():
        floor = wet_rows[section, 4:20]
        lane = lanes(16)
        rim = (lane == 0) | (lane == 127)
        row = lax.broadcasted_iota(jnp.int32, (16, 128), 0)
        inside = (row > 0) & (row < 15)
        for l in range(levels):
            sides = side_columns(section, inner[l], outer[l])
            wet_rim = rim & (floor > l)
            pair = [
                partial[a, l] + jnp.where(wet_rim, roll_lanes(sides, -2 * a - 1), 0.0)
                for a in range(2)
            ]
            own = side_columns(section, inner[l, 4:12], outer[l, 4:12])
            edge = rim_edges[l] + jnp.where(rim_wet[l] > 0.0, own, 0.0)
            shade = jnp.where(inside, pigment_of(pair[0], pair[1]), 0.0)
            for out in outs:
                out[2 * l] = shade[:8]
                out[2 * l + 1] = shade[8:]
                out[12 + l] = edge
        for out in outs:
            for i in range(18, 21):
                out[i] = jnp.zeros((8, 128), F32)


def roll_rows(x, by):
    by = by % 8
    return x if by == 0 else pltpu.roll(x, by, 0)


def planes(buffer):
    return [buffer.at[f] for f in range(4)]


def early_kernel(flow_next, wet_rows, partial, outer, inner, early, tracers_next):
    section, _, _ = place()
    nt, levels = partial.shape[0], partial.shape[1]

    @pl.when(section != 3)
    def _():
        floor = wet_rows[section, 4:20]
        lane = lanes(16)
        rim = (lane == 0) | (lane == 127)

        def level(l, carry):
            sides = side_columns(section, inner[l], outer[l])
            wet_rim = rim & (floor > l)
            for a in range(nt):
                side = jnp.where(wet_rim, roll_lanes(sides, -2 * a - 1), 0.0)
                tracers_next[a, l] = partial[a, l] + side
            return carry

        lax.fori_loop(0, levels, level, 0, unroll=2)

    @pl.when(section == 3)
    def _():
        substep(planes(flow_next), early, None, wet_rows, 2, 8, 8, 0, 4)


def second_kernel(
    from_b, from_a, from_c, early, tracers_next, wet_rows, reaction,
    out_a, out_b, out_c, flow_last, tracers_last, warm, field_1, field_2, heat, winds,
):
    section, _, _ = place()
    levels = heat.shape[0]
    nt = tracers_next.shape[0]

    @pl.when(section == 3)
    def _():
        shades = (from_a, from_b, from_c)

        def load(l, tile, j):
            return shades[j][2 * l + tile]

        fill_heat(load, heat)

        def warm_up(l, carry):
            for j in range(3):
                heated = jnp.where(wet_rows[j, 4:20] > l, heat[l, j], 0.0)
                warm[l, j, 8:24] = early[2, l, j, 8:24] + heated
            return carry

        lax.fori_loop(0, levels, warm_up, 0)
        first = planes(early)
        first[2] = warm
        substep(first, field_1, heat, wet_rows, 2, 8, 8, 0, 4)
        substep(planes(field_1), field_2, heat, wet_rows, 2, 8, 8, 0, 4)
        substep(planes(field_2), flow_last, heat, wet_rows, 1, 12, 0, 4, 8)
        outs = (out_a, out_b, out_c)
        for l in range(levels):
            for j in range(3):
                for f in range(2):
                    total = early[f, l, j, 12:20] + field_1[f, l, j, 12:20]
                    total = total + field_2[f, l, j, 12:20]
                    outs[j][6 * f + l] = 0.25 * (total + flow_last[f, l, j])
                outs[j][12 + l] = flow_last[2, l, j]
                outs[j][18 + l] = flow_last[3, l, j]

    @pl.when(section != 3)
    def _():
        def driven(i):
            return jnp.where(
                section == 0, from_a[i], jnp.where(section == 1, from_b[i], from_c[i])
            )

        for i in range(18):
            winds[i] = driven(i)
        edge_v = driven(18)
        rows_above = driven(19)
        rows_below = driven(20)
        lane = lanes(8)
        sub = lax.broadcasted_iota(jnp.int32, (8, 128), 0)
        for l in range(levels):
            u, v = winds[l], winds[6 + l]
            winds[18 + l] = jnp.where(sub == 0, roll_rows(rows_above, -l), roll_rows(u, 1))
            winds[24 + l] = jnp.where(sub == 7, roll_rows(rows_below, 7 - l), roll_rows(u, 7))
            winds[30 + l] = jnp.where(
                lane == 127, roll_lanes(edge_v, 126 - 2 * l), roll_lanes(v, 127)
            )
            winds[36 + l] = jnp.where(lane == 0, roll_lanes(edge_v, -2 * l), roll_lanes(v, 1))
            winds[42 + l] = side_columns(section, from_c[12 + l], from_a[12 + l])
        floor = wet_rows[section, 8:16]

        def level(l, carry):
            weights = tracer_weights(
                winds[18 + l], winds[24 + l], winds[30 + l], winds[36 + l], winds[12 + l], floor > l
            )
            results = tracer_level(
                [tracers_next[a, l, 4:12] for a in range(nt)],
                [tracers_next[a, l, 3:11] for a in range(nt)],
                [tracers_next[a, l, 5:13] for a in range(nt)],
                winds[42 + l], weights, reaction,
            )
            for a in range(nt):
                tracers_last[a, l] = results[a]
            shade = pigment_of(results[0], results[1])
            for out in (out_a, out_b, out_c):
                out[l] = shade
                for i in range(1, 4):
                    out[6 * i + l] = jnp.zeros((8, 128), F32)
            return carry

        lax.fori_loop(0, levels, level, 0)


def store_kernel(flow_last, tracers_last, flow_out, tracers_out, blank, sems):
    section, _, _ = place()
    blank[...] = jnp.zeros_like(blank)

    def put(flow_of, tracers_from):
        copies = [pltpu.make_async_copy(tracers_from, tracers_out, sems.at[3])]
        for j in range(3):
            target = flow_out.at[:, :, :, 128 * j : 128 * j + 128]
            copies.append(pltpu.make_async_copy(flow_of(j), target, sems.at[j]))
        for copy in copies:
            copy.start()
        for copy in copies:
            copy.wait()

    @pl.when(section == 3)
    def _():
        put(lambda j: flow_last.at[:, :, j], blank)

    @pl.when(section != 3)
    def _():
        put(lambda j: blank.at[0:4], tracers_last)


def last_kernel(from_a, from_b, from_c, light_out, forcing_out):
    section, _, _ = place()
    levels = light_out.shape[0]
    is_dynamics = section == 3
    for l in range(levels):
        for j, shade in enumerate((from_a, from_b, from_c)):
            light_out[l, :, 128 * j : 128 * j + 128] = jnp.where(is_dynamics, shade[l], 0.0)
        for f in range(4):
            i = 6 * f + l
            picked = jnp.where(
                section == 0, from_a[i], jnp.where(section == 1, from_b[i], from_c[i])
            )
            forcing_out[f, l] = jnp.where(is_dynamics, 0.0, picked)


def call(kernel, shapes, operands, spaces, scratch=(), out_space=pltpu.VMEM):
    operands = [
        pltpu.with_memory_space_constraint(x, pltpu.HBM) if space == pltpu.HBM else x
        for x, space in zip(operands, spaces)
    ]
    return pl.pallas_call(
        kernel,
        out_shape=[jax.ShapeDtypeStruct(shape, dtype) for shape, dtype in shapes],
        in_specs=[pl.BlockSpec(memory_space=space) for space in spaces],
        out_specs=[pl.BlockSpec(memory_space=out_space) for _ in shapes],
        scratch_shapes=list(scratch),
        compiler_params=pltpu.CompilerParams(vmem_limit_bytes=VMEM_LIMIT),
    )(*operands)


def route(target):
    total = lax.axis_size("comp") * lax.axis_size("gy") * lax.axis_size("gx")
    group = total // SECTIONS
    pairs = []
    for moved in range(total):
        section, strip = target(moved // group, moved % group, group)
        pairs.append(((moved - 1) % total, (section * group + strip - 1) % total))
    return pairs


def partner(strip, group):
    if strip in (0, group - 1):
        return group - 1 - strip
    return strip + 1 if strip % 2 == 1 else strip - 1


def trade(value, *pairs):
    other = {}
    for a, b in pairs:
        other[a], other[b] = b, a

    def target(k, s, g):
        return (other[k], s) if k in other else (k, partner(s, g))

    return lax.ppermute(value, AXES, route(target))


def along_dynamics(value, by):
    def target(k, s, g):
        return (k, (s + by) % g) if k == 3 else (k, partner(s, g))

    return lax.ppermute(value, AXES, route(target))


def along(value, by):
    return lax.ppermute(value, AXES, route(lambda k, s, g: divmod((k * g + s + by) % (SECTIONS * g), g)))


def on_device(flow_fields, chlorophyll_lag, tracers, forcing, ocean_mask, bottom, reaction):
    levels = chlorophyll_lag.shape[0]
    nt = tracers.shape[0]
    breadth = flow_fields.shape[3]
    vmem, hbm = pltpu.VMEM, pltpu.HBM
    message = (SHARED, levels, 8, 128)
    more = (15 - SHARED, levels, 8, 128)
    to_next, to_prev, more_next, more_prev, flow, pigment, tracers, forcing = call(
        load_kernel,
        [
            (message, F32), (message, F32), (more, F32), (more, F32),
            ((4, levels, 3, 8, 128), F32), ((levels, 3, 8, 128), F32),
            (tracers.shape, F32), (forcing.shape, F32),
        ],
        (flow_fields, chlorophyll_lag, tracers, forcing),
        (hbm,) * 4,
        (pltpu.SemaphoreType.DMA((2 * levels,)),),
    )
    above = along(to_next, 1)
    below = along(to_prev, -1)
    more_above = along_dynamics(more_next, 1)
    more_below = along_dynamics(more_prev, -1)
    wet_rows, rates = call(
        mask_kernel,
        [((3, 24, 128), jnp.int32), ((nt, nt, 128), F32)],
        (ocean_mask, bottom, reaction),
        (hbm, hbm, vmem),
        (
            pltpu.VMEM((3, 8, breadth), jnp.int32),
            pltpu.VMEM((3, 8, breadth), jnp.int32),
            pltpu.SemaphoreType.DMA((6,)),
        ),
    )
    cells, winds, border = call(
        gather_kernel,
        [((nt, levels, 32, 128), F32), ((3, levels, 32, 128), F32), ((levels, 16, 128), F32)],
        (tracers, forcing, above, below, wet_rows),
        (vmem,) * 5,
    )
    inner = trade(border, (0, 1))
    outer = trade(border, (1, 2))
    exchange = ((21, 8, 128), F32)
    *sends, flow_next, partial, rim_edges, rim_wet = call(
        first_kernel,
        [
            exchange, exchange, exchange,
            ((4, levels, 3, 32, 128), F32), ((nt, levels, 16, 128), F32),
            ((levels, 8, 128), F32), ((levels, 8, 128), F32),
        ],
        (
            flow, pigment, above, below, more_above, more_below, cells, winds, wet_rows,
            rates,
        ),
        (vmem,) * 10,
        (
            *[pltpu.VMEM((4, levels, 3, 40, 128), F32) for _ in range(4)],
            pltpu.VMEM((levels, 3, 24, 128), F32),
        ),
    )
    sent = call(
        sides_kernel,
        [exchange, exchange, exchange],
        (outer, inner, *sends, partial, rim_edges, rim_wet, wet_rows),
        (vmem,) * 9,
    )
    from_b = trade(sent[1], (3, 1))
    from_a = trade(sent[0], (3, 0), (1, 2))
    from_c = trade(sent[2], (3, 2), (0, 1))
    early, tracers_next = call(
        early_kernel,
        [((4, levels, 3, 32, 128), F32), ((nt, levels, 16, 128), F32)],
        (flow_next, wet_rows, partial, outer, inner),
        (vmem,) * 5,
    )
    exchange = ((24, 8, 128), F32)
    last = call(
        second_kernel,
        [
            exchange, exchange, exchange,
            ((4, levels, 3, 8, 128), F32), ((nt, levels, 8, 128), F32),
        ],
        (from_b, from_a, from_c, early, tracers_next, wet_rows, rates),
        (vmem,) * 7,
        (
            pltpu.VMEM((levels, 3, 32, 128), F32),
            *[pltpu.VMEM((4, levels, 3, 32, 128), F32) for _ in range(2)],
            pltpu.VMEM((levels, 3, 16, 128), F32),
            pltpu.VMEM((48, 8, 128), F32),
        ),
    )
    final_b = trade(last[1], (3, 1))
    final_a = trade(last[0], (3, 0))
    final_c = trade(last[2], (3, 2))
    flow_out, tracers_out = call(
        store_kernel,
        [(flow_fields.shape, F32), (tracers.shape, F32)],
        (last[3], last[4]),
        (vmem, vmem),
        (pltpu.VMEM(tracers.shape, F32), pltpu.SemaphoreType.DMA((4,))),
        hbm,
    )
    light_out, forcing_out = call(
        last_kernel,
        [((levels, 8, breadth), F32), ((4, levels, 8, 128), F32)],
        (final_a, final_b, final_c),
        (vmem,) * 3,
    )
    return flow_out, light_out, tracers_out, forcing_out


def solution(mesh):
    rows = P(None, None, AXES, None)
    light = P(None, AXES, None)
    return jax.shard_map(
        on_device,
        mesh=mesh,
        in_specs=(rows, light, rows, rows, P(), P(), P()),
        out_specs=(rows, light, rows, rows),
        check_vma=False,
    )
```

```python
import jax
import jax.numpy as jnp
from jax import lax
from jax.experimental import pallas as pl
from jax.experimental.pallas import tpu as pltpu
from jax.sharding import PartitionSpec as P

AXES = ("comp", "gy", "gx")
SECTIONS = 4
SHARED = 10
DT = 0.1
F32 = jnp.float32
UNROLL = 6
VMEM_LIMIT = 24 * 1024 * 1024


def place():
    gy = lax.axis_size("gy")
    gx = lax.axis_size("gx")
    total = lax.axis_size("comp") * gy * gx
    group = total // SECTIONS
    position = (lax.axis_index("comp") * gy + lax.axis_index("gy")) * gx + lax.axis_index("gx")
    moved = lax.rem(position + 1, total)
    return moved // group, lax.rem(moved, group), group


def lanes(rows):
    return lax.broadcasted_iota(jnp.int32, (rows, 128), 1)


def roll_lanes(x, by):
    by = by % 128
    return x if by == 0 else pltpu.roll(x, by, 1)


def swap(x):
    return pltpu.roll(x, 4, 0)


def upper_half():
    return lax.broadcasted_iota(jnp.int32, (8, 128), 0) < 4


def spread(flag):
    return jnp.where(flag, 1.0, 0.0).astype(F32)


def edge_tile(planes):
    pair = lanes(planes[0].shape[0]) // 2
    edges = jnp.zeros_like(planes[0])
    for a, x in enumerate(planes):
        edges = jnp.where(pair == a, roll_lanes(x, 2 * a + 1), edges)
    return edges


def pack_rows(tracers, forcing, to_next, to_prev, copies):
    half = upper_half()
    nt, levels = tracers.shape[0], tracers.shape[1]

    def put(plane, pair, even, odd):
        row, col = plane // 2, 3 * (plane % 2)
        to_next[row, col + pair] = jnp.where(half, swap(even), odd)
        to_prev[row, col + pair] = jnp.where(half, even, swap(odd))

    for pair in range(levels // 2):
        even, odd = 2 * pair, 2 * pair + 1
        for copy in copies[4 * pair : 4 * pair + 4]:
            copy.wait()
        for a in range(nt):
            put(a, pair, tracers[a, even], tracers[a, odd])
        put(nt, pair, forcing[0, even], forcing[0, odd])
        put(nt + 1, pair, forcing[1, even], forcing[1, odd])
        growth = [jnp.exp(0.1 * forcing[2, l] - 0.05 * forcing[3, l]) for l in (even, odd)]
        put(nt + 2, pair, growth[0], growth[1])
        put(nt + 3, pair, jnp.zeros((8, 128), F32), jnp.zeros((8, 128), F32))


def load_kernel(
    flow, pigment, tracers, forcing,
    to_next, to_prev, more_next, more_prev, flow_in, pigment_in, tracers_in, forcing_in, sems,
):
    section, _, _ = place()
    levels = pigment.shape[0]

    @pl.when(section == 3)
    def _():
        copies = []
        for j in range(3):
            cols = slice(128 * j, 128 * j + 128)
            copies.append(
                pltpu.make_async_copy(flow.at[:, :, :, cols], flow_in.at[:, :, j], sems.at[j])
            )
            copies.append(
                pltpu.make_async_copy(pigment.at[:, :, cols], pigment_in.at[:, j], sems.at[3 + j])
            )
        for copy in copies:
            copy.start()
        for copy in copies:
            copy.wait()

        def level(l, carry):
            for f in range(5):
                for j in range(3):
                    tile = flow_in[f, l, j] if f < 4 else pigment_in[l, j]
                    row = 3 * f + j
                    if row < SHARED:
                        to_next[row, l] = tile
                        to_prev[row, l] = tile
                    else:
                        more_next[row - SHARED, l] = tile
                        more_prev[row - SHARED, l] = tile
            return carry

        lax.fori_loop(0, levels, level, 0)

    @pl.when(section != 3)
    def _():
        copies = []
        for l in range(levels):
            copies.append(
                pltpu.make_async_copy(tracers.at[:, l], tracers_in.at[:, l], sems.at[l])
            )
            copies.append(
                pltpu.make_async_copy(forcing.at[:, l], forcing_in.at[:, l], sems.at[levels + l])
            )
        for copy in copies:
            copy.start()
        pack_rows(tracers_in, forcing_in, to_next, to_prev, copies)
        more_next[...] = jnp.zeros_like(more_next)
        more_prev[...] = jnp.zeros_like(more_prev)


def mask_kernel(ocean, bottom, reaction, wet_rows, rates, ocean_rows, bottom_rows, mask_sems):
    _, strip, group = place()
    starts = [jnp.maximum(strip - 1, 0), strip, jnp.minimum(strip + 1, group - 1)]
    masks = []
    for i, start in enumerate(starts):
        rows = pl.ds(pl.multiple_of(start * 8, 8), 8)
        masks.append(pltpu.make_async_copy(ocean.at[rows], ocean_rows.at[i], mask_sems.at[i]))
        masks.append(pltpu.make_async_copy(bottom.at[rows], bottom_rows.at[i], mask_sems.at[3 + i]))
    for copy in masks:
        copy.start()
    nt = reaction.shape[0]
    for k in range(nt):
        rates[k] = jnp.broadcast_to(reaction[:, k : k + 1], (nt, 128))
    for copy in masks:
        copy.wait()
    inside = [(strip > 0).astype(jnp.int32), 1, (strip < group - 1).astype(jnp.int32)]
    for i in range(3):
        floor = jnp.where(ocean_rows[i] == 1, bottom_rows[i], 0) * inside[i]
        for j in range(3):
            wet_rows[j, 8 * i : 8 * i + 8] = floor[:, 128 * j : 128 * j + 128]


def side_columns(section, inner, outer):
    even = lanes(inner.shape[0]) % 2 == 0
    east = roll_lanes(jnp.where(section == 0, inner, outer), -1)
    west = roll_lanes(jnp.where(section == 1, inner, outer), 1)
    east = jnp.where(section < 2, east, 0.0)
    west = jnp.where(section > 0, west, 0.0)
    return jnp.where(even, east, west)


def shifted(tiles):
    lane = lanes(tiles[0].shape[0])
    left = [roll_lanes(x, 127) for x in tiles]
    right = [roll_lanes(x, 1) for x in tiles]
    count = len(tiles)
    east = [
        jnp.where(lane == 127, left[j + 1] if j + 1 < count else 0.0, left[j]) for j in range(count)
    ]
    west = [jnp.where(lane == 0, right[j - 1] if j > 0 else 0.0, right[j]) for j in range(count)]
    return east, west


def substep(source, target, heat, wet_rows, tiles, read_at, write_at, heat_at, wet_at):
    levels = target.shape[1]
    thirds = 3
    zero = jnp.zeros((8, 128), F32)

    def level(l, carry):
        slopes = []
        for tile in range(tiles):
            row = read_at + 8 * tile
            put = write_at + 8 * tile
            slope_x, slope_y = carry[tile]

            def load(f, by):
                return [source[f][l, j, row + by : row + by + 8] for j in range(thirds)]

            centre = [load(f, 0) for f in range(4)]
            up = [load(f, -1) for f in range(4)]
            down = [load(f, 1) for f in range(4)]
            sides = [shifted(centre[f]) for f in range(4)]
            new_x, new_y = [], []
            for j in range(thirds):
                u, v, t, s = (centre[f][j] for f in range(4))
                un, vn, tn, sn = (up[f][j] for f in range(4))
                us, vs, ts, ss = (down[f][j] for f in range(4))
                ue, ve, te, se = (sides[f][0][j] for f in range(4))
                uw, vw, tw, sw = (sides[f][1][j] for f in range(4))
                px = slope_x[j] + ((ss - sn) - (ts - tn))
                py = slope_y[j] + ((se - sw) - (te - tw))
                new_x.append(px)
                new_y.append(py)
                is_wet = wet_rows[j, wet_at + 8 * tile : wet_at + 8 * tile + 8] > l
                a = 0.05 - 0.05 * us
                b = 0.05 + 0.05 * un
                c = 0.05 - 0.05 * ve
                d = 0.05 + 0.05 * vw
                kept = 0.8 * t
                if heat is not None:
                    kept = kept + heat[l, j, heat_at + 8 * tile : heat_at + 8 * tile + 8]
                results = (
                    0.79 * u + 0.1 * v - 0.01 * px + 0.05 * ((un + us) + (ue + uw)),
                    0.79 * v - 0.1 * u - 0.01 * py + 0.05 * ((vn + vs) + (ve + vw)),
                    kept + ((ts * a + tn * b) + (te * c + tw * d)),
                    0.8 * s + ((ss * a + sn * b) + (se * c + sw * d)),
                )
                for f in range(4):
                    target[f, l, j, put : put + 8] = jnp.where(is_wet, results[f], 0.0)
            slopes.append((new_x, new_y))
        return slopes

    start = [([zero] * thirds, [zero] * thirds) for _ in range(tiles)]
    lax.fori_loop(0, levels, level, start, unroll=UNROLL)


def fill_heat(load, heat):
    levels, rows = heat.shape[0], heat.shape[2]
    for tile in range(rows // 8):
        for j in range(3):
            optical = jnp.zeros((8, 128), F32)
            light = jnp.ones((8, 128), F32)
            for l in range(levels):
                optical = optical + (0.05 + 0.3 * load(l, tile, j))
                lower = jnp.exp(-optical)
                heat[l, j, 8 * tile : 8 * tile + 8] = (5.0 * DT) * (light - lower)
                light = lower


def extend(own, above, below, half):
    turned = swap(own)
    return jnp.concatenate([jnp.where(half, above, turned), jnp.where(half, turned, below)], axis=0)


def tracer_weights(u_up, u_down, v_east, v_west, growth, is_wet):
    wet = spread(is_wet)
    scale = wet * 0.05
    return (
        scale - scale * u_down,
        scale + scale * u_up,
        scale - scale * v_east,
        scale + scale * v_west,
        wet * 0.8,
        (wet * DT) * growth,
    )


def tracer_level(centre, up, down, sides, weights, reaction):
    nt = len(centre)
    lane = lanes(centre[0].shape[0])
    a, b, c, d, keep, grow = weights
    results = []

    def rate(k, i):
        return jnp.broadcast_to(reaction[k, i : i + 1], centre[0].shape)

    for i in range(nt):
        side = 0.0 if sides is None else roll_lanes(sides, -2 * i - 1)
        east = jnp.where(lane == 127, side, roll_lanes(centre[i], 127))
        west = jnp.where(lane == 0, side, roll_lanes(centre[i], 1))
        mixed = rate(0, i) * centre[0]
        for k in range(1, nt):
            mixed = mixed + rate(k, i) * centre[k]
        results.append(
            (keep * centre[i] + grow * mixed)
            + ((down[i] * a + up[i] * b) + (east * c + west * d))
        )
    return results


def pigment_of(first, second):
    return 0.25 * (first * first + second * second)


def gather_kernel(tracers, forcing, above, below, wet_rows, cells, winds, border):
    section, strip, group = place()
    nt, levels = tracers.shape[0], tracers.shape[1]
    low = spread(strip > 0)
    high = spread(strip < group - 1)

    @pl.when(section == 3)
    def _():
        border[...] = jnp.zeros_like(border)

    @pl.when(section != 3)
    def _():
        half = upper_half()

        def halo(message, plane, pair, odd, upward):
            tile = message[plane // 2, 3 * (plane % 2) + pair]
            return swap(tile) if odd != upward else tile

        def build(plane, own, l, masked):
            pair, odd = l // 2, l % 2 == 1
            up = halo(above, plane, pair, odd, False)
            down = halo(below, plane, pair, not odd, False)
            if masked:
                up, down = up * low, down * high
            return extend(own, up, down, half)

        lane = lanes(16)
        for l in range(levels):
            v = build(nt + 1, forcing[1, l], l, False)
            scale = 0.05 + jnp.where(lane == 0, -0.05, 0.05) * v
            products = []
            for a in range(nt):
                cell = build(a, tracers[a, l], l, True)
                cells[a, l, 8:24] = cell
                products.append(scale * cell)
            winds[0, l, 8:24] = build(nt, forcing[0, l], l, False)
            winds[1, l, 8:24] = v
            growth = jnp.exp(0.1 * forcing[2, l] - 0.05 * forcing[3, l])
            winds[2, l, 8:24] = build(nt + 2, growth, l, False)
            border[l] = edge_tile(products)


def first_kernel(
    flow, pigment, above, below, more_above, more_below, cells, winds, wet_rows, reaction,
    send_a, send_b, send_c, flow_next, partial, rim_edges, rim_wet,
    field_0, field_1, field_2, field_3, heat,
):
    section, strip, group = place()
    levels = pigment.shape[0]
    nt = cells.shape[0]
    low = spread(strip > 0)
    high = spread(strip < group - 1)

    @pl.when(section == 3)
    def _():
        def over(row, l):
            return above[row, l] if row < SHARED else more_above[row - SHARED, l]

        def under(row, l):
            return below[row, l] if row < SHARED else more_below[row - SHARED, l]

        def fill(l, carry):
            for f in range(4):
                for j in range(3):
                    field_0[f, l, j, 8:16] = over(3 * f + j, l) * low
                    field_0[f, l, j, 16:24] = flow[f, l, j]
                    field_0[f, l, j, 24:32] = under(3 * f + j, l) * high
            return carry

        lax.fori_loop(0, levels, fill, 0)

        def load(l, tile, j):
            if tile == 1:
                return pigment[l, j]
            return (over if tile == 0 else under)(12 + j, l)

        fill_heat(load, heat)
        substep(planes(field_0), field_1, heat, wet_rows, 3, 8, 8, 0, 0)
        substep(planes(field_1), field_2, heat, wet_rows, 3, 8, 8, 0, 0)
        substep(planes(field_2), field_3, heat, wet_rows, 3, 8, 8, 0, 0)
        substep(planes(field_3), flow_next, heat, wet_rows, 2, 12, 8, 4, 4)
        lane = lanes(8)
        outs = (send_a, send_b, send_c)
        sub = lax.broadcasted_iota(jnp.int32, (8, 128), 0)

        def mean(f, l, row, j):
            total = field_1[f, l, j, row : row + 8] + field_2[f, l, j, row : row + 8]
            total = total + field_3[f, l, j, row : row + 8]
            return 0.25 * (total + flow_next[f, l, j, row - 4 : row + 4])

        edge_v = [jnp.zeros((8, 128), F32) for _ in range(3)]
        rows_above = [jnp.zeros((8, 128), F32) for _ in range(3)]
        rows_below = [jnp.zeros((8, 128), F32) for _ in range(3)]
        for l in range(levels):
            v_mean = []
            for j in range(3):
                outs[j][l] = mean(0, l, 16, j)
                v_mean.append(mean(1, l, 16, j))
                outs[j][6 + l] = v_mean[j]
                warm = flow_next[2, l, j, 12:20]
                salt = flow_next[3, l, j, 12:20]
                outs[j][12 + l] = jnp.exp(0.1 * warm - 0.05 * salt)
                first = mean(0, l, 15, j)
                last = mean(0, l, 17, j)
                rows_above[j] = jnp.where(sub == l, roll_rows(first, l), rows_above[j])
                rows_below[j] = jnp.where(sub == l, roll_rows(last, l + 1), rows_below[j])
            for j in range(3):
                if j > 0:
                    edge_v[j] = jnp.where(
                        lane == 2 * l, roll_lanes(v_mean[j - 1], 2 * l + 1), edge_v[j]
                    )
                if j < 2:
                    edge_v[j] = jnp.where(
                        lane == 2 * l + 1, roll_lanes(v_mean[j + 1], 2 * l + 1), edge_v[j]
                    )
        for j in range(3):
            outs[j][18] = edge_v[j]
            outs[j][19] = rows_above[j]
            outs[j][20] = rows_below[j]

    @pl.when(section != 3)
    def _():
        floor = wet_rows[section, 4:20]

        def level(l, carry):
            v = winds[1, l, 8:24]
            weights = tracer_weights(
                winds[0, l, 7:23], winds[0, l, 9:25], roll_lanes(v, 127), roll_lanes(v, 1),
                winds[2, l, 8:24], floor > l,
            )
            results = tracer_level(
                [cells[a, l, 8:24] for a in range(nt)],
                [cells[a, l, 7:23] for a in range(nt)],
                [cells[a, l, 9:25] for a in range(nt)],
                None, weights, reaction,
            )
            for a in range(nt):
                partial[a, l] = results[a]
            rim_edges[l] = edge_tile([partial[a, l, 4:12] for a in range(nt)])
            wet = spread(wet_rows[section, 8:16] > l)
            first = jnp.broadcast_to(wet[:, :1], (8, 128))
            last = jnp.broadcast_to(wet[:, 127:], (8, 128))
            rim_wet[l] = jnp.where(lanes(8) % 2 == 0, last, first)
            return carry

        lax.fori_loop(0, levels, level, 0)


def sides_kernel(
    outer, inner, send_a, send_b, send_c, partial, rim_edges, rim_wet, wet_rows,
    out_a, out_b, out_c,
):
    section, _, _ = place()
    levels = partial.shape[1]
    outs = (out_a, out_b, out_c)

    @pl.when(section == 3)
    def _():
        for out, send in zip(outs, (send_a, send_b, send_c)):
            out[...] = send[...]

    @pl.when(section != 3)
    def _():
        floor = wet_rows[section, 4:20]
        lane = lanes(16)
        rim = (lane == 0) | (lane == 127)
        row = lax.broadcasted_iota(jnp.int32, (16, 128), 0)
        inside = (row > 0) & (row < 15)
        for l in range(levels):
            sides = side_columns(section, inner[l], outer[l])
            wet_rim = rim & (floor > l)
            pair = [
                partial[a, l] + jnp.where(wet_rim, roll_lanes(sides, -2 * a - 1), 0.0)
                for a in range(2)
            ]
            own = side_columns(section, inner[l, 4:12], outer[l, 4:12])
            edge = rim_edges[l] + jnp.where(rim_wet[l] > 0.0, own, 0.0)
            shade = jnp.where(inside, pigment_of(pair[0], pair[1]), 0.0)
            for out in outs:
                out[2 * l] = shade[:8]
                out[2 * l + 1] = shade[8:]
                out[12 + l] = edge
        for out in outs:
            for i in range(18, 21):
                out[i] = jnp.zeros((8, 128), F32)


def roll_rows(x, by):
    by = by % 8
    return x if by == 0 else pltpu.roll(x, by, 0)


def planes(buffer):
    return [buffer.at[f] for f in range(4)]


def early_kernel(flow_next, wet_rows, partial, outer, inner, early, tracers_next):
    section, _, _ = place()
    nt, levels = partial.shape[0], partial.shape[1]

    @pl.when(section != 3)
    def _():
        floor = wet_rows[section, 4:20]
        lane = lanes(16)
        rim = (lane == 0) | (lane == 127)

        def level(l, carry):
            sides = side_columns(section, inner[l], outer[l])
            wet_rim = rim & (floor > l)
            for a in range(nt):
                side = jnp.where(wet_rim, roll_lanes(sides, -2 * a - 1), 0.0)
                tracers_next[a, l] = partial[a, l] + side
            return carry

        lax.fori_loop(0, levels, level, 0, unroll=2)

    @pl.when(section == 3)
    def _():
        substep(planes(flow_next), early, None, wet_rows, 2, 8, 8, 0, 4)


def second_kernel(
    from_a, from_b, from_c, early, tracers_next, wet_rows, reaction,
    out_a, out_b, out_c, flow_last, tracers_last, warm, field_1, field_2, heat, winds,
):
    section, _, _ = place()
    levels = heat.shape[0]
    nt = tracers_next.shape[0]

    @pl.when(section == 3)
    def _():
        shades = (from_a, from_b, from_c)

        def load(l, tile, j):
            return shades[j][2 * l + tile]

        fill_heat(load, heat)

        def warm_up(l, carry):
            for j in range(3):
                heated = jnp.where(wet_rows[j, 4:20] > l, heat[l, j], 0.0)
                warm[l, j, 8:24] = early[2, l, j, 8:24] + heated
            return carry

        lax.fori_loop(0, levels, warm_up, 0)
        first = planes(early)
        first[2] = warm
        substep(first, field_1, heat, wet_rows, 2, 8, 8, 0, 4)
        substep(planes(field_1), field_2, heat, wet_rows, 2, 8, 8, 0, 4)
        substep(planes(field_2), flow_last, heat, wet_rows, 1, 12, 0, 4, 8)
        outs = (out_a, out_b, out_c)
        for l in range(levels):
            for j in range(3):
                for f in range(2):
                    total = early[f, l, j, 12:20] + field_1[f, l, j, 12:20]
                    total = total + field_2[f, l, j, 12:20]
                    outs[j][6 * f + l] = 0.25 * (total + flow_last[f, l, j])
                outs[j][12 + l] = flow_last[2, l, j]
                outs[j][18 + l] = flow_last[3, l, j]

    @pl.when(section != 3)
    def _():
        def driven(i):
            return jnp.where(
                section == 0, from_a[i], jnp.where(section == 1, from_b[i], from_c[i])
            )

        for i in range(18):
            winds[i] = driven(i)
        edge_v = driven(18)
        rows_above = driven(19)
        rows_below = driven(20)
        lane = lanes(8)
        sub = lax.broadcasted_iota(jnp.int32, (8, 128), 0)
        for l in range(levels):
            u, v = winds[l], winds[6 + l]
            winds[18 + l] = jnp.where(sub == 0, roll_rows(rows_above, -l), roll_rows(u, 1))
            winds[24 + l] = jnp.where(sub == 7, roll_rows(rows_below, 7 - l), roll_rows(u, 7))
            winds[30 + l] = jnp.where(
                lane == 127, roll_lanes(edge_v, 126 - 2 * l), roll_lanes(v, 127)
            )
            winds[36 + l] = jnp.where(lane == 0, roll_lanes(edge_v, -2 * l), roll_lanes(v, 1))
            winds[42 + l] = side_columns(section, from_c[12 + l], from_a[12 + l])
        floor = wet_rows[section, 8:16]

        def level(l, carry):
            weights = tracer_weights(
                winds[18 + l], winds[24 + l], winds[30 + l], winds[36 + l], winds[12 + l], floor > l
            )
            results = tracer_level(
                [tracers_next[a, l, 4:12] for a in range(nt)],
                [tracers_next[a, l, 3:11] for a in range(nt)],
                [tracers_next[a, l, 5:13] for a in range(nt)],
                winds[42 + l], weights, reaction,
            )
            for a in range(nt):
                tracers_last[a, l] = results[a]
            shade = pigment_of(results[0], results[1])
            for out in (out_a, out_b, out_c):
                out[l] = shade
                for i in range(1, 4):
                    out[6 * i + l] = jnp.zeros((8, 128), F32)
            return carry

        lax.fori_loop(0, levels, level, 0)


def store_kernel(flow_last, tracers_last, flow_out, tracers_out, blank, sems):
    section, _, _ = place()
    blank[...] = jnp.zeros_like(blank)

    def put(flow_of, tracers_from):
        copies = [pltpu.make_async_copy(tracers_from, tracers_out, sems.at[3])]
        for j in range(3):
            target = flow_out.at[:, :, :, 128 * j : 128 * j + 128]
            copies.append(pltpu.make_async_copy(flow_of(j), target, sems.at[j]))
        for copy in copies:
            copy.start()
        for copy in copies:
            copy.wait()

    @pl.when(section == 3)
    def _():
        put(lambda j: flow_last.at[:, :, j], blank)

    @pl.when(section != 3)
    def _():
        put(lambda j: blank.at[0:4], tracers_last)


def last_kernel(from_a, from_c, from_b, light_out, forcing_out):
    section, _, _ = place()
    levels = light_out.shape[0]
    is_dynamics = section == 3
    for l in range(levels):
        for j, shade in enumerate((from_a, from_b, from_c)):
            light_out[l, :, 128 * j : 128 * j + 128] = jnp.where(is_dynamics, shade[l], 0.0)
        for f in range(4):
            i = 6 * f + l
            picked = jnp.where(
                section == 0, from_a[i], jnp.where(section == 1, from_b[i], from_c[i])
            )
            forcing_out[f, l] = jnp.where(is_dynamics, 0.0, picked)


def call(kernel, shapes, operands, spaces, scratch=(), out_space=pltpu.VMEM):
    operands = [
        pltpu.with_memory_space_constraint(x, pltpu.HBM) if space == pltpu.HBM else x
        for x, space in zip(operands, spaces)
    ]
    return pl.pallas_call(
        kernel,
        out_shape=[jax.ShapeDtypeStruct(shape, dtype) for shape, dtype in shapes],
        in_specs=[pl.BlockSpec(memory_space=space) for space in spaces],
        out_specs=[pl.BlockSpec(memory_space=out_space) for _ in shapes],
        scratch_shapes=list(scratch),
        compiler_params=pltpu.CompilerParams(vmem_limit_bytes=VMEM_LIMIT),
    )(*operands)


def route(target):
    total = lax.axis_size("comp") * lax.axis_size("gy") * lax.axis_size("gx")
    group = total // SECTIONS
    pairs = []
    for moved in range(total):
        section, strip = target(moved // group, moved % group, group)
        pairs.append(((moved - 1) % total, (section * group + strip - 1) % total))
    return pairs


def partner(strip, group):
    if strip in (0, group - 1):
        return group - 1 - strip
    return strip + 1 if strip % 2 == 1 else strip - 1


def trade(value, *pairs):
    other = {}
    for a, b in pairs:
        other[a], other[b] = b, a

    def target(k, s, g):
        return (other[k], s) if k in other else (k, partner(s, g))

    return lax.ppermute(value, AXES, route(target))


def along_dynamics(value, by):
    def target(k, s, g):
        return (k, (s + by) % g) if k == 3 else (k, partner(s, g))

    return lax.ppermute(value, AXES, route(target))


def along(value, by):
    return lax.ppermute(value, AXES, route(lambda k, s, g: divmod((k * g + s + by) % (SECTIONS * g), g)))


def on_device(flow_fields, chlorophyll_lag, tracers, forcing, ocean_mask, bottom, reaction):
    levels = chlorophyll_lag.shape[0]
    nt = tracers.shape[0]
    breadth = flow_fields.shape[3]
    vmem, hbm = pltpu.VMEM, pltpu.HBM
    message = (SHARED, levels, 8, 128)
    more = (15 - SHARED, levels, 8, 128)
    to_next, to_prev, more_next, more_prev, flow, pigment, tracers, forcing = call(
        load_kernel,
        [
            (message, F32), (message, F32), (more, F32), (more, F32),
            ((4, levels, 3, 8, 128), F32), ((levels, 3, 8, 128), F32),
            (tracers.shape, F32), (forcing.shape, F32),
        ],
        (flow_fields, chlorophyll_lag, tracers, forcing),
        (hbm,) * 4,
        (pltpu.SemaphoreType.DMA((2 * levels,)),),
    )
    above = along(to_next, 1)
    below = along(to_prev, -1)
    more_above = along_dynamics(more_next, 1)
    more_below = along_dynamics(more_prev, -1)
    wet_rows, rates = call(
        mask_kernel,
        [((3, 24, 128), jnp.int32), ((nt, nt, 128), F32)],
        (ocean_mask, bottom, reaction),
        (hbm, hbm, vmem),
        (
            pltpu.VMEM((3, 8, breadth), jnp.int32),
            pltpu.VMEM((3, 8, breadth), jnp.int32),
            pltpu.SemaphoreType.DMA((6,)),
        ),
    )
    cells, winds, border = call(
        gather_kernel,
        [((nt, levels, 32, 128), F32), ((3, levels, 32, 128), F32), ((levels, 16, 128), F32)],
        (tracers, forcing, above, below, wet_rows),
        (vmem,) * 5,
    )
    inner = trade(border, (0, 1))
    outer = trade(border, (1, 2))
    exchange = ((21, 8, 128), F32)
    *sends, flow_next, partial, rim_edges, rim_wet = call(
        first_kernel,
        [
            exchange, exchange, exchange,
            ((4, levels, 3, 32, 128), F32), ((nt, levels, 16, 128), F32),
            ((levels, 8, 128), F32), ((levels, 8, 128), F32),
        ],
        (
            flow, pigment, above, below, more_above, more_below, cells, winds, wet_rows,
            rates,
        ),
        (vmem,) * 10,
        (
            *[pltpu.VMEM((4, levels, 3, 40, 128), F32) for _ in range(4)],
            pltpu.VMEM((levels, 3, 24, 128), F32),
        ),
    )
    sent = call(
        sides_kernel,
        [exchange, exchange, exchange],
        (outer, inner, *sends, partial, rim_edges, rim_wet, wet_rows),
        (vmem,) * 9,
    )
    from_b = trade(sent[1], (3, 1))
    from_a = trade(sent[0], (3, 0), (1, 2))
    from_c = trade(sent[2], (3, 2), (0, 1))
    early, tracers_next = call(
        early_kernel,
        [((4, levels, 3, 32, 128), F32), ((nt, levels, 16, 128), F32)],
        (flow_next, wet_rows, partial, outer, inner),
        (vmem,) * 5,
    )
    exchange = ((24, 8, 128), F32)
    last = call(
        second_kernel,
        [
            exchange, exchange, exchange,
            ((4, levels, 3, 8, 128), F32), ((nt, levels, 8, 128), F32),
        ],
        (from_a, from_b, from_c, early, tracers_next, wet_rows, rates),
        (vmem,) * 7,
        (
            pltpu.VMEM((levels, 3, 32, 128), F32),
            *[pltpu.VMEM((4, levels, 3, 32, 128), F32) for _ in range(2)],
            pltpu.VMEM((levels, 3, 16, 128), F32),
            pltpu.VMEM((48, 8, 128), F32),
        ),
    )
    final_b = trade(last[1], (3, 1))
    final_a = trade(last[0], (3, 0))
    final_c = trade(last[2], (3, 2))
    flow_out, tracers_out = call(
        store_kernel,
        [(flow_fields.shape, F32), (tracers.shape, F32)],
        (last[3], last[4]),
        (vmem, vmem),
        (pltpu.VMEM(tracers.shape, F32), pltpu.SemaphoreType.DMA((4,))),
        hbm,
    )
    light_out, forcing_out = call(
        last_kernel,
        [((levels, 8, breadth), F32), ((4, levels, 8, 128), F32)],
        (final_a, final_c, final_b),
        (vmem,) * 3,
    )
    return flow_out, light_out, tracers_out, forcing_out


def solution(mesh):
    rows = P(None, None, AXES, None)
    light = P(None, AXES, None)
    return jax.shard_map(
        on_device,
        mesh=mesh,
        in_specs=(rows, light, rows, rows, P(), P(), P()),
        out_specs=(rows, light, rows, rows),
        check_vma=False,
    )
```
